32 devices in a mesh: ctx: 8 (over y, x, core), fsdp: 4 (over z).
Axes of the slice: x: 2, y: 2, z: 4, core: 2. Of those that a mesh axis runs over, the one named last changes fastest.
Arguments:
- tokens: bfloat16 [2, 4, 2048, 1024], P(None, 'fsdp', 'ctx'), may hold values from -6 to 6
- cotangent: bfloat16 [2, 4, 2048, 1024], P(None, 'fsdp', 'ctx'), may hold values from -6 to 6
- lengths: int32 [2, 4, 2], P(None, 'fsdp'), may hold values from 512 to 1536, as said below
- order: int32 [2, 4, 16], P(None, 'fsdp'), may hold values from 0 to 15, each once within a row
- w_qkv: bfloat16 [1024, 3072], P('fsdp'), may hold values from -0.1875 to 0.1875
- w_out: bfloat16 [1024, 1024], P('fsdp'), may hold values from -3 to 3
- w_up: bfloat16 [1024, 4096], P('fsdp'), may hold values from -0.1875 to 0.1875
- w_down: bfloat16 [4096, 1024], P('fsdp'), may hold values from -0.09375 to 0.09375
- q_bias: bfloat16 [1024], P('fsdp'), may hold values from -3 to 3
- v_bias: bfloat16 [1024], P('fsdp'), may hold values from -0.19921875 to 0.19921875
- out_bias: bfloat16 [1024], P('fsdp'), may hold values from -1.5 to 1.5
- norm1_gain: bfloat16 [1024], P('fsdp'), may hold values from 0.5 to 1.5
- norm1_bias: bfloat16 [1024], P('fsdp'), may hold values from -0.59765625 to 0.59765625
- up_bias: bfloat16 [4096], P('fsdp'), may hold values from -1.1953125 to 1.1953125
- down_bias: bfloat16 [1024], P('fsdp'), may hold values from -0.59765625 to 0.59765625
- norm2_gain: bfloat16 [1024], P('fsdp'), may hold values from 0.5 to 1.5
- norm2_bias: bfloat16 [1024], P('fsdp'), may hold values from -0.59765625 to 0.59765625
Outputs:
- mixed: bfloat16 [2, 4, 2048, 1024], P(None, 'fsdp', 'ctx')
- tokens_grad: bfloat16 [2, 4, 2048, 1024], P(None, 'fsdp', 'ctx')
- w_qkv_grad: float32 [1024, 3072], P(('ctx', 'fsdp'))
- w_out_grad: float32 [1024, 1024], P(('ctx', 'fsdp'))
- w_up_grad: float32 [1024, 4096], P(('ctx', 'fsdp'))
- w_down_grad: float32 [4096, 1024], P(('ctx', 'fsdp'))
- q_bias_grad: float32 [1024], P(('ctx', 'fsdp'))
- v_bias_grad: float32 [1024], P(('ctx', 'fsdp'))
- out_bias_grad: float32 [1024], P(('ctx', 'fsdp'))
- norm1_gain_grad: float32 [1024], P(('ctx', 'fsdp'))
- norm1_bias_grad: float32 [1024], P(('ctx', 'fsdp'))
- up_bias_grad: float32 [4096], P(('ctx', 'fsdp'))
- down_bias_grad: float32 [1024], P(('ctx', 'fsdp'))
- norm2_gain_grad: float32 [1024], P(('ctx', 'fsdp'))
- norm2_bias_grad: float32 [1024], P(('ctx', 'fsdp'))
The draws below stay inside these ranges and needn't reach their ends.
Inputs may be any that keep to these rules, and one draw needn't show every extreme that they name: The 2 lengths of each group add up to 2048. `order`: each row names every block position of its group once.
All inputs are finite; a program needn't handle non-finite values.
Results may differ from the reference program's by a relative error of at most 0.029.
Values may be sent and summed in bfloat16 or wider, within the bound.
No kernel may reach another device: no remote copies, remote signals or barrier semaphores. Data moves between devices by JAX's collectives and lax.ppermute only.
A program may use at most 256 MiB of HBM per device.

```python
import math
import jax
import jax.numpy as jnp
from jax import lax

D = 1024
H = 16
HD = 64
FF = 4096
BLK = 128
SEQS = 2
MB = 2
GTOK = 2048
NBLK = 16
LEAST = 512
N_FSDP = 4


def draw_lengths(key, part):
    leading = jax.random.randint(key, (MB, N_FSDP), LEAST, GTOK - LEAST + 1)
    leading = leading.at[0, 0].set(GTOK - LEAST)
    return jnp.stack([leading, GTOK - leading], -1).astype(jnp.int32)


def levels(stream_key, shape, shards, low, largest):
    loudness = 1.0
    for axis_at, blocks in shards:
        heights = jax.random.uniform(jax.random.fold_in(jax.random.fold_in(stream_key, 6), axis_at), (blocks,), jnp.float32, low / len(shards), largest / len(shards))
        loudness = loudness * jnp.repeat(jnp.exp(heights), shape[axis_at] // blocks).reshape((-1,) + (1,) * (len(shape) - 1 - axis_at))
    return loudness


def scatter_about(key, extent, scale, limit, shards=(), held_as=jnp.bfloat16):
    values = scale * jax.random.normal(key, extent, jnp.float32)
    if shards:
        values = values * levels(key, extent, shards, -0.22, 0.18)
    return jnp.clip(values, -limit, limit).astype(held_as)


def setup_inputs(seed: int = 0) -> dict:
    streams_of = jax.random.split(jax.random.key(seed), 18)
    tokens = scatter_about(streams_of[0], (MB, N_FSDP, GTOK, D), 1.0, 6.0, ((1, 4), (2, 8)))
    cotangent = scatter_about(streams_of[1], (MB, N_FSDP, GTOK, D), 1.0, 6.0, ((1, 4), (2, 8)))
    lengths = draw_lengths(jax.random.fold_in(streams_of[17], 71), 0)
    order = jax.vmap(lambda own: jax.random.permutation(own, NBLK))(jax.random.split(streams_of[3], MB * N_FSDP)).reshape((MB, N_FSDP, NBLK)).astype(jnp.int32)
    w_qkv = scatter_about(streams_of[4], (D, 3 * D), D ** -0.5, 0.1875, ((0, 4),))
    w_out = scatter_about(streams_of[5], (D, D), (max(1, D // 256)) ** -0.5, 3.0, ((0, 4),))
    w_up = scatter_about(streams_of[6], (D, FF), D ** -0.5, 0.1875, ((0, 4),))
    w_down = scatter_about(streams_of[7], (FF, D), FF ** -0.5, 0.09375, ((0, 4),))
    q_bias = scatter_about(streams_of[8], (D,), 0.5, 3.0, ((0, 4),))
    v_bias = scatter_about(streams_of[9], (D,), 0.03, 0.19921875, ((0, 4),))
    out_bias = scatter_about(streams_of[10], (D,), 0.25, 1.5, ((0, 4),))
    norm1_gain = jnp.clip(1.0 + 0.1 * jax.random.normal(streams_of[11], (D,), jnp.float32), 0.5, 1.5).astype(jnp.bfloat16)
    norm1_bias = scatter_about(streams_of[12], (D,), 0.1, 0.59765625, ((0, 4),))
    up_bias = scatter_about(streams_of[13], (FF,), 0.2, 1.1953125, ((0, 4),))
    down_bias = scatter_about(streams_of[14], (D,), 0.1, 0.59765625, ((0, 4),))
    norm2_gain = jnp.clip(1.0 + 0.1 * jax.random.normal(streams_of[15], (D,), jnp.float32), 0.5, 1.5).astype(jnp.bfloat16)
    norm2_bias = scatter_about(streams_of[16], (D,), 0.1, 0.59765625, ((0, 4),))
    return {"tokens": tokens, "cotangent": cotangent, "lengths": lengths, "order": order, "w_qkv": w_qkv, "w_out": w_out, "w_up": w_up, "w_down": w_down, "q_bias": q_bias, "v_bias": v_bias, "out_bias": out_bias, "norm1_gain": norm1_gain, "norm1_bias": norm1_bias, "up_bias": up_bias, "down_bias": down_bias, "norm2_gain": norm2_gain, "norm2_bias": norm2_bias}


HIGHEST = lax.Precision.HIGHEST
NEGATIVE = -1e+30
EPSILON = 1e-05

@jax.custom_vjp
def low(v):
    return lax.optimization_barrier(v.astype(jnp.bfloat16)).astype(jnp.float32)

@jax.custom_vjp
def low_back(v):
    return v

def low_keep(v):
    return (low(v), None)

def low_pass(kept, grad):
    return (grad,)

def back_keep(v):
    return (v, None)

def back_low(kept, grad):
    return (low(grad),)
low.defvjp(low_keep, low_pass)
low_back.defvjp(back_keep, back_low)

def layer_norm(values_in, gain_vec, shift_vec):
    center = values_in - lax.optimization_barrier(jnp.mean(values_in, -1, keepdims=True))
    inverse = lax.rsqrt(lax.optimization_barrier(jnp.mean(center * center, -1, keepdims=True)) + EPSILON)
    return center * inverse * gain_vec + shift_vec

def attention(queries, key_rows, value_rows, segment_ids):
    count = queries.shape[0]
    block_rows = math.gcd(count, 512)
    scaling = 1.0 / math.sqrt(HD)

    def one_block(pair):
        query_block, segment_block = pair
        raw_scores = low_back(jnp.einsum('qhd,khd->hqk', query_block, key_rows, precision=HIGHEST))
        allowed = (segment_block[:, None] == segment_ids[None, :])[None]
        scores = jnp.where(allowed, raw_scores * scaling, NEGATIVE)
        peak_val = lax.optimization_barrier(jnp.max(scores, -1, keepdims=True))
        expos = jnp.where(allowed, jnp.exp(scores - peak_val), 0.0)
        probs = low(expos / lax.optimization_barrier(jnp.sum(expos, -1, keepdims=True)))
        return jnp.einsum('hqk,khd->qhd', probs, value_rows, precision=HIGHEST)
    blocks = count // block_rows
    result = lax.map(jax.checkpoint(one_block), (queries.reshape(blocks, block_rows, H, HD), segment_ids.reshape(blocks, block_rows)))
    return result.reshape(count, D)

def layer(token_rows, weight_set, segment_all):
    w_qkv, w_out, w_up, w_down, q_bias, v_bias, out_bias, norm1_gain, norm1_bias, up_bias, down_bias, norm2_gain, norm2_bias = weight_set
    full_bias = jnp.concatenate([q_bias, jnp.zeros_like(q_bias), v_bias])

    def group(pair):
        group_rows, segment_ids = pair
        count = group_rows.shape[0]
        qkv_rows = low_back(low(jnp.dot(group_rows, w_qkv, precision=HIGHEST) + full_bias))
        attended = attention(qkv_rows[:, :D].reshape(count, H, HD), qkv_rows[:, D:2 * D].reshape(count, H, HD), qkv_rows[:, 2 * D:].reshape(count, H, HD), segment_ids)
        attn_low = low_back(low(attended))
        branch = low_back(jnp.dot(attn_low, w_out, precision=HIGHEST) + out_bias)
        first_out = layer_norm(group_rows + branch, norm1_gain, norm1_bias)
        hidden_in = low_back(jnp.dot(low(first_out), w_up, precision=HIGHEST) + up_bias)
        activated = low(jax.nn.gelu(hidden_in, approximate=False))
        down_out = low_back(jnp.dot(activated, w_down, precision=HIGHEST) + down_bias)
        return layer_norm(first_out + down_out, norm2_gain, norm2_bias)
    return lax.map(group, (token_rows, segment_all))

def reference(tokens, cotangent, lengths, order, w_qkv, w_out, w_up, w_down, q_bias, v_bias, out_bias, norm1_gain, norm1_bias, up_bias, down_bias, norm2_gain, norm2_bias):
    groups = MB * N_FSDP
    token_rows = tokens.astype(jnp.float32).reshape(groups, GTOK, D)
    cot_rows = cotangent.astype(jnp.float32).reshape(groups, GTOK, D)
    bounds = jnp.cumsum(lengths.reshape(groups, SEQS), 1)[:, :-1]
    positions = jnp.arange(GTOK, dtype=jnp.int32)
    segment_all = lax.optimization_barrier(jnp.sum((positions[None, :, None] >= bounds[:, None, :]).astype(jnp.int32), 2))
    order_all = order.reshape(groups, NBLK).astype(jnp.int32)
    weight_set = tuple((weight.astype(jnp.float32) for weight in (w_qkv, w_out, w_up, w_down, q_bias, v_bias, out_bias, norm1_gain, norm1_bias, up_bias, down_bias, norm2_gain, norm2_bias)))

    def whole_layer(rows_in, weights_in):
        given = layer(rows_in, weights_in, segment_all).reshape(groups, NBLK, BLK, D)
        dealt = jnp.take_along_axis(given, order_all[:, :, None, None], 1)
        return dealt.reshape(groups, GTOK, D)
    outputs, pullback = jax.vjp(whole_layer, token_rows, weight_set)
    token_grad, weight_grad = pullback(cot_rows)
    full_shape = tokens.shape
    return (outputs.reshape(full_shape).astype(jnp.bfloat16), token_grad.reshape(full_shape).astype(jnp.bfloat16), weight_grad[0], weight_grad[1], weight_grad[2], weight_grad[3], weight_grad[4], weight_grad[5], weight_grad[6], weight_grad[7], weight_grad[8], weight_grad[9], weight_grad[10], weight_grad[11], weight_grad[12])
```

```python
from functools import partial
import math

import jax
import jax.numpy as jnp
from jax import lax
from jax.experimental import pallas as pl
from jax.experimental.pallas import tpu as pltpu
from jax.sharding import PartitionSpec as P

D = 1024
H = 16
HD = 64
BLK = 128
MB = 2

NEGATIVE = -1e30
EPSILON = 1e-05
BF = jnp.bfloat16
F32 = jnp.float32


def contract(a, b, ca, cb):
    return lax.dot_general(a, b, (((ca,), (cb,)), ((), ())), preferred_element_type=F32)


def norm_forward(values_in, gain_vec, shift_vec):
    center = values_in - jnp.mean(values_in, -1, keepdims=True)
    inverse = lax.rsqrt(jnp.mean(center * center, -1, keepdims=True) + EPSILON)
    normed = center * inverse
    return (normed * gain_vec + shift_vec, normed, inverse)


def norm_backward(grad_out, normed, inverse, gain_vec):
    grad_norm = grad_out * gain_vec
    return inverse * (
        grad_norm
        - jnp.mean(grad_norm, -1, keepdims=True)
        - normed * jnp.mean(grad_norm * normed, -1, keepdims=True)
    )


def hop(value, mask):
    count = lax.axis_size("ctx")
    return lax.ppermute(value, "ctx", [(i, i ^ mask) for i in range(count)])


VMEM = pl.BlockSpec(memory_space=pltpu.VMEM)
SMEM = pl.BlockSpec(memory_space=pltpu.SMEM)
ANY = pl.BlockSpec(memory_space=pl.ANY)


def params(mib):
    return pltpu.CompilerParams(vmem_limit_bytes=mib << 20)


def struct(shape, dtype):
    return jax.ShapeDtypeStruct(shape, dtype)


def segment_lanes(first, rows, split, is_query):
    position = first + lax.broadcasted_iota(jnp.int32, (rows, HD), 0)
    lane = lax.broadcasted_iota(jnp.int32, (rows, HD), 1)
    second = (position >= split).astype(jnp.int32)
    if is_query:
        return jnp.where(lane == 1 - second, NEGATIVE, 0.0).astype(BF)
    return jnp.where(lane == second, 1.0, 0.0).astype(BF)


def key_range(q0, bq, split, bk, total):
    low = jnp.where(q0 >= split, split // bk, 0)
    high = jnp.where(q0 + bq <= split, (split + bk - 1) // bk, total // bk)
    return low, high


def attention_forward_kernel(scal, qkv, out, out_t, lse, qa, ka, vt, sc, *, heads, chunk, bq, bk):
    total = qkv.shape[0]
    chunks = total // chunk
    width = heads * HD
    split = scal[0]
    top = scal[1]
    for m in range(chunks):
        pos = pl.multiple_of(scal[2 + m], chunk)
        rows = slice(m * chunk, (m + 1) * chunk)
        qtail = segment_lanes(pos, chunk, split, True)
        ktail = segment_lanes(pos, chunk, split, False)
        for h in range(heads):
            q = qkv[rows, h * HD : (h + 1) * HD]
            k = qkv[rows, width + h * HD : width + (h + 1) * HD]
            q = (q.astype(F32) * 0.125).astype(BF)
            qa[h, pl.ds(pos, chunk), :] = jnp.concatenate([q, qtail], 1)
            ka[h, pl.ds(pos, chunk), :] = jnp.concatenate([k, ktail], 1)
        vt[:, pl.ds(pos, chunk)] = qkv[rows, 2 * width : 3 * width].T

    def q_step(qi, _):
        q0 = pl.multiple_of(qi * bq, bq)
        low, high = key_range(q0, bq, split, bk, total)

        def max_step(ki, carry):
            k0 = pl.multiple_of(ki * bk, bk)
            result = []
            for h in range(heads):
                st = contract(ka[h, pl.ds(k0, bk), :], qa[h, pl.ds(q0, bq), :], 1, 1)
                sc[h, pl.ds(k0, bk), :] = st
                result.append(jnp.maximum(carry[h], jnp.max(st.reshape(bk // 8, 8, bq), 0)))
            return tuple(result)

        start = tuple(jnp.full((8, bq), NEGATIVE, F32) for _ in range(heads))
        peaks = lax.fori_loop(low, high, max_step, start)
        peaks = [jnp.max(m, 0, keepdims=True) for m in peaks]

        def k_step(ki, carry):
            k0 = pl.multiple_of(ki * bk, bk)
            result = []
            for h in range(heads):
                total_p, acc = carry[2 * h : 2 * h + 2]
                p = jnp.exp(sc[h, pl.ds(k0, bk), :] - peaks[h])
                total_p = total_p + jnp.sum(p.reshape(bk // 8, 8, bq), 0)
                acc = acc + contract(
                    vt[h * HD : (h + 1) * HD, pl.ds(k0, bk)], p.astype(BF), 1, 0
                )
                result += [total_p, acc]
            return tuple(result)

        start = []
        for h in range(heads):
            start += [jnp.zeros((8, bq), F32), jnp.zeros((HD, bq), F32)]
        done = lax.fori_loop(low, high, k_step, tuple(start))
        pieces = []
        for h in range(heads):
            denom = jnp.sum(done[2 * h], 0, keepdims=True)
            pieces.append(done[2 * h + 1] / denom)
            lse[h : h + 1, pl.ds(q0, bq)] = peaks[h] + jnp.log(denom)
        turned = jnp.concatenate(pieces, 0)
        out_t[:, pl.ds(q0, bq)] = turned
        low_rows = turned.T.astype(BF)
        half = chunks // 2
        for i in range(bq // chunk):
            c = q0 // chunk + i
            out[c % half, (c // half) ^ top] = low_rows[i * chunk : (i + 1) * chunk]
        return 0

    lax.fori_loop(0, total // bq, q_step, 0)


def attention_forward(scal, qkv, chunk, bq=512, bk=512):
    total, triple = qkv.shape
    width = triple // 3
    heads = width // HD
    half = total // chunk // 2
    return pl.pallas_call(
        partial(attention_forward_kernel, heads=heads, chunk=chunk, bq=bq, bk=bk),
        out_shape=(
            struct((half, 2, chunk, width), BF),
            struct((width, total), F32),
            struct((heads, total), F32),
        ),
        in_specs=[SMEM, VMEM],
        out_specs=(VMEM, VMEM, VMEM),
        scratch_shapes=[
            pltpu.VMEM((heads, total, 128), BF),
            pltpu.VMEM((heads, total, 128), BF),
            pltpu.VMEM((width, total), BF),
            pltpu.VMEM((heads, total, bq), F32),
        ],
        compiler_params=params(56),
        cost_estimate=pl.CostEstimate(
            flops=8 * total * total * width, bytes_accessed=5 * total * width * 2, transcendentals=0
        ),
        name="attention_forward",
    )(scal, qkv)


def attention_backward_kernel(
    scal, qkv, grad, out_t, lse, dqkv, qa, ka, kt, va, ga, gt, dkv, dq, *, heads, chunk, bq, bk
):
    total = qkv.shape[0]
    chunks = total // chunk
    half = chunks // 2
    width = heads * HD
    split = scal[0]
    top = scal[1]
    blank = jnp.zeros((chunk, HD), BF)
    for m in range(chunks):
        pos = pl.multiple_of(scal[2 + m], chunk)
        rows = slice(m * chunk, (m + 1) * chunk)
        qtail = segment_lanes(pos, chunk, split, True)
        ktail = segment_lanes(pos, chunk, split, False)
        for h in range(heads):
            q = qkv[rows, h * HD : (h + 1) * HD]
            k = qkv[rows, width + h * HD : width + (h + 1) * HD]
            v = qkv[rows, 2 * width + h * HD : 2 * width + (h + 1) * HD]
            q = (q.astype(F32) * 0.125).astype(BF)
            qa[h, pl.ds(pos, chunk), :] = jnp.concatenate([q, qtail], 1)
            ka[h, pl.ds(pos, chunk), :] = jnp.concatenate([k, ktail], 1)
            va[h, pl.ds(pos, chunk), :] = jnp.concatenate([v, blank], 1)
        kt[:, pl.ds(pos, chunk)] = qkv[rows, width : 2 * width].T
    for j in range(half):
        for s in range(2):
            pos = pl.multiple_of((j + half * (s ^ top)) * chunk, chunk)
            for h in range(heads):
                g = grad[j, s, :, h * HD : (h + 1) * HD]
                ga[h, pl.ds(pos, chunk), :] = jnp.concatenate([g, blank], 1)
            gt[:, pl.ds(pos, chunk)] = grad[j, s].T
    dkv[...] = jnp.zeros_like(dkv)

    def q_step(qi, _):
        q0 = pl.multiple_of(qi * bq, bq)
        low, high = key_range(q0, bq, split, bk, total)
        product = gt[:, pl.ds(q0, bq)].astype(F32) * out_t[:, pl.ds(q0, bq)]
        delta = [jnp.sum(product[h * HD : (h + 1) * HD], 0, keepdims=True) for h in range(heads)]
        held_lse = lse[:, pl.ds(q0, bq)]
        totals = [held_lse[h : h + 1] for h in range(heads)]

        def k_step(ki, carry):
            k0 = pl.multiple_of(ki * bk, bk)
            result = []
            for h in range(heads):
                q = qa[h, pl.ds(q0, bq), :]
                g = ga[h, pl.ds(q0, bq), :]
                st = contract(ka[h, pl.ds(k0, bk), :], q, 1, 1)
                p = jnp.exp(st - totals[h])
                dp = contract(va[h, pl.ds(k0, bk), :], g, 1, 1)
                ds = (p * (dp - delta[h]) * 0.125).astype(BF)
                dkv[0, h, pl.ds(k0, bk), :] += contract(ds, q, 1, 0)
                dkv[1, h, pl.ds(k0, bk), :] += contract(p.astype(BF), g, 1, 0)
                result.append(
                    carry[h] + contract(kt[h * HD : (h + 1) * HD, pl.ds(k0, bk)], ds, 1, 0)
                )
            return tuple(result)

        start = tuple(jnp.zeros((HD, bq), F32) for _ in range(heads))
        turned = lax.fori_loop(low, high, k_step, start)
        dq[pl.ds(q0, bq), :] = jnp.concatenate(turned, 0).T.astype(BF)
        return 0

    lax.fori_loop(0, total // bq, q_step, 0)
    for m in range(chunks):
        pos = pl.multiple_of(scal[2 + m], chunk)
        rows = slice(m * chunk, (m + 1) * chunk)
        dqkv[rows, 0:width] = dq[pl.ds(pos, chunk), :]
        for h in range(0, heads, 2):
            for part, gain in ((0, 8.0), (1, 1.0)):
                pair = [dkv[part, h + e, pl.ds(pos, chunk), :][:, :HD] for e in range(2)]
                base = (1 + part) * width + h * HD
                dqkv[rows, base : base + 2 * HD] = (jnp.concatenate(pair, 1) * gain).astype(BF)


def attention_backward(scal, qkv, grad, out_t, lse, chunk, bq=512, bk=512):
    total, triple = qkv.shape
    width = triple // 3
    heads = width // HD
    wide = pltpu.VMEM((heads, total, 128), BF)
    return pl.pallas_call(
        partial(attention_backward_kernel, heads=heads, chunk=chunk, bq=bq, bk=bk),
        out_shape=struct((total, triple), BF),
        in_specs=[SMEM, VMEM, VMEM, VMEM, VMEM],
        out_specs=VMEM,
        scratch_shapes=[
            wide,
            wide,
            pltpu.VMEM((width, total), BF),
            wide,
            wide,
            pltpu.VMEM((width, total), BF),
            pltpu.VMEM((2, heads, total, 128), F32),
            pltpu.VMEM((total, width), BF),
        ],
        compiler_params=params(56),
        cost_estimate=pl.CostEstimate(
            flops=16 * total * total * width, bytes_accessed=9 * total * width * 2, transcendentals=0
        ),
        name="attention_backward",
    )(scal, qkv, grad, out_t, lse)


PIECES = (0, 2, 4, 6, 1, 3, 5, 7)
CHUNKS = (0, 4, 2, 6, 1, 5, 3, 7)


def start_all(copies):
    for copy in copies:
        copy.start()


def wait_all(copies):
    for copy in copies:
        copy.wait()


def carve_kernel(
    scal, tokens, cot, w_qkv, w_out, w_up, w_down, small,
    own, other, cot_own, cot_other, pack, up_slice, down_slice, sems,
):
    me, low, top = scal[0], scal[1], scal[2]
    pairs = []
    for k in range(3):
        columns = pl.ds(pl.multiple_of(k * D + low * 256, 256), 256)
        pairs.append((w_qkv.at[:, columns], pack.at[0:256, 256 * k : 256 * (k + 1)]))
    pairs.append((small, pack.at[256:272, :]))
    pairs += [(tokens.at[top, 0], own), (tokens.at[1 - top, 0], other)]
    for k in range(4):
        columns = pl.ds(pl.multiple_of(k * D + me * 128, 128), 128)
        pairs.append((w_up.at[:, columns], up_slice.at[:, 128 * k : 128 * (k + 1)]))
    columns = pl.ds(pl.multiple_of(me * 128, 128), 128)
    pairs.append((w_out.at[:, columns], up_slice.at[:, 512:640]))
    pairs.append((w_down.at[columns, :], down_slice))
    pairs += [(cot.at[top, 0], cot_own), (cot.at[1 - top, 0], cot_other)]
    copies = [pltpu.make_async_copy(a, b, sems.at[i]) for i, (a, b) in enumerate(pairs)]
    start_all(copies)
    wait_all(copies)


def carve(scal, tokens, cot, w_qkv, w_out, w_up, w_down, small):
    rows = tokens.shape[2]
    return pl.pallas_call(
        carve_kernel,
        out_shape=tuple(struct((rows, D), BF) for _ in range(4))
        + (struct((272, 768), BF), struct((256, 640), BF), struct((128, D), BF)),
        in_specs=[SMEM] + [ANY] * 7,
        out_specs=(ANY,) * 7,
        scratch_shapes=[pltpu.SemaphoreType.DMA((14,))],
        compiler_params=params(16),
        cost_estimate=pl.CostEstimate(flops=0, bytes_accessed=8 << 20, transcendentals=0),
        name="carve",
    )(scal, tokens, cot, w_qkv, w_out, w_up, w_down, small)


def project_kernel(scal, vecs, packed, *rest):
    pieces, (qkv, x_all, weight, sems) = rest[:8], rest[8:]
    chunk = pieces[0].shape[0]
    loads = [
        pltpu.make_async_copy(packed.at[f, 0:256], weight.at[256 * f : 256 * (f + 1)], sems.at[f])
        for f in range(4)
    ]
    moves = [
        pltpu.make_async_copy(piece, x_all.at[m * chunk : (m + 1) * chunk], sems.at[4 + m])
        for m, piece in enumerate(pieces)
    ]
    start_all(loads)
    start_all(moves)
    here = pl.ds(pl.multiple_of(scal[1] * 256, 256), 256)
    bias = jnp.concatenate([vecs[0:1, here], jnp.zeros((1, 256), F32), vecs[1:2, here]], 1)
    wait_all(loads)
    for m in range(8):
        moves[m].wait()
        rows = slice(m * chunk, (m + 1) * chunk)
        qkv[rows, :] = (contract(x_all[rows, :], weight[...], 1, 0) + bias).astype(BF)


def project(scal, vecs, packed, pieces):
    chunk = pieces[0].shape[0]
    return pl.pallas_call(
        project_kernel,
        out_shape=(struct((8 * chunk, 768), BF), struct((8 * chunk, D), BF)),
        in_specs=[SMEM, VMEM, ANY] + [ANY] * 8,
        out_specs=(VMEM, VMEM),
        scratch_shapes=[pltpu.VMEM((D, 768), BF), pltpu.SemaphoreType.DMA((12,))],
        compiler_params=params(40),
        cost_estimate=pl.CostEstimate(
            flops=2 * 8 * chunk * D * 768, bytes_accessed=13 << 20, transcendentals=0
        ),
        name="project",
    )(scal, vecs, packed, *pieces)


def up_pairs(scal, pieces, local, first, width, held):
    pairs = []
    for m in range(8):
        for k in range(3):
            base = pl.multiple_of(scal[4 + k] * 256, 256)
            columns = slice(first, first + width)
            if m == 3:
                lower = pl.ds(base, 128)
                upper = pl.ds(pl.multiple_of(base + 128, 128), 128)
                pairs.append((pieces[3].at[k, :, columns], held.at[m, lower]))
                pairs.append((pieces[4].at[k, :, columns], held.at[m, upper]))
            elif m == 7:
                lower = pl.ds(base, 128)
                upper = pl.ds(pl.multiple_of(base + 128, 128), 128)
                pairs.append((pieces[8].at[k, :, columns], held.at[m, lower]))
                pairs.append((pieces[9].at[k, :, columns], held.at[m, upper]))
            else:
                piece = pieces[m if m < 3 else m + 1]
                pairs.append((piece.at[k, :, columns], held.at[m, pl.ds(base, 256)]))
    own = pl.ds(pl.multiple_of(scal[3] * 256, 256), 256)
    w_up, w_out = local
    for m in range(8):
        block = scal[0] ^ PIECES[m]
        if first < 512:
            for k in range(4):
                columns = pl.ds(pl.multiple_of(k * D + block * 128, 128), 128)
                pairs.append((w_up.at[:, columns], held.at[m, own, 128 * k : 128 * (k + 1)]))
        if first + width > 512:
            columns = pl.ds(pl.multiple_of(block * 128, 128), 128)
            pairs.append((w_out.at[:, columns], held.at[m, own, 512 - first : 640 - first]))
    return pairs


def per_piece(pairs, owners, sems, base=0):
    groups = [[] for _ in range(8)]
    for i, ((source, target), m) in enumerate(zip(pairs, owners)):
        groups[m].append(pltpu.make_async_copy(source, target, sems.at[base + i]))
    return groups


def up_owners(first, width):
    owners = []
    for m in range(8):
        owners += [m] * (6 if m in (3, 7) else 3)
    for m in range(8):
        owners += [m] * ((4 if first < 512 else 0) + (1 if first + width > 512 else 0))
    return owners


def down_pairs(pieces, held):
    pairs, owners = [], []
    places = {3: (3, 4), 7: (8, 9)}
    for m in range(8):
        if m in places:
            for f in range(4):
                for e in range(2):
                    rows = slice(128 * f + 64 * e, 128 * f + 64 * (e + 1))
                    pairs.append((pieces[places[m][e]].at[f], held.at[m, rows]))
                    owners.append(m)
        else:
            piece = pieces[m if m < 3 else m + 1]
            for f in range(4):
                pairs.append((piece.at[f], held.at[m, 128 * f : 128 * (f + 1)]))
                owners.append(m)
    return pairs, owners


def attention_out_kernel(scal, attn, x, vecs, w_up, w_out, *rest):
    pieces, (y1, y1_low, n1, r1, held, mixed, sems) = rest[:10], rest[10:]
    pairs = up_pairs(scal, pieces, (w_up, w_out), 512, 128, held)
    groups = per_piece(pairs, up_owners(512, 128), sems)
    for group in groups:
        start_all(group)
    for m, group in enumerate(groups):
        wait_all(group)
        part = contract(attn[0], held[m, 0:256, :], 1, 0)
        for t in range(1, 4):
            part = part + contract(attn[t], held[m, 256 * t : 256 * (t + 1), :], 1, 0)
        mixed[scal[0] ^ PIECES[m]] = part
    branch = jnp.concatenate([mixed[b] for b in range(8)], 1)
    h1 = x[...].astype(F32) + branch + vecs[2:3]
    out, normed, inverse = norm_forward(h1, vecs[3:4], vecs[4:5])
    y1[...] = out
    y1_low[...] = out.astype(BF)
    n1[...] = normed
    r1[...] = jnp.broadcast_to(inverse, r1.shape)


def attention_out(scal, attn, x_all, vecs, w_up, w_out, pieces):
    rows = attn.shape[1]
    return pl.pallas_call(
        attention_out_kernel,
        grid=(1,),
        out_shape=(
            struct((rows, D), F32),
            struct((rows, D), BF),
            struct((rows, D), F32),
            struct((rows, 128), F32),
        ),
        in_specs=[SMEM, VMEM, pl.BlockSpec((rows, D), lambda i: (0, 0)), VMEM] + [ANY] * 12,
        out_specs=(VMEM,) * 4,
        scratch_shapes=[
            pltpu.VMEM((8, D, 128), BF),
            pltpu.VMEM((8, rows, 128), F32),
            pltpu.SemaphoreType.DMA((len(up_owners(512, 128)),)),
        ],
        compiler_params=params(40),
        cost_estimate=pl.CostEstimate(
            flops=2 * rows * D * D, bytes_accessed=8 << 20, transcendentals=0
        ),
        name="attention_out",
    )(scal, attn, x_all, vecs, w_up, w_out, *pieces)


def up_kernel(scal, y1_low, up_bias, w_up, w_out, *rest):
    pieces, (act, slope, held, sems) = rest[:10], rest[10:]
    pairs = up_pairs(scal, pieces, (w_up, w_out), 0, 512, held)
    groups = per_piece(pairs, up_owners(0, 512), sems)
    for group in groups:
        start_all(group)
    for m, group in enumerate(groups):
        wait_all(group)
        b = scal[0] ^ PIECES[m]
        bias = up_bias[pl.ds(b, 1), :]
        for r in (slice(0, 256), slice(256, 512)):
            u = contract(y1_low[r, :], held[m], 1, 0) + bias
            cdf = 0.5 * (1.0 + lax.erf(u * (1.0 / math.sqrt(2.0))))
            density = jnp.exp(-0.5 * u * u) * (1.0 / math.sqrt(2.0 * math.pi))
            slope[b, r, :] = (cdf + u * density).astype(BF)
            act[b, r, :] = (u * cdf).astype(BF)


def feed_up(scal, y1_low, up_bias, w_up, w_out, pieces):
    rows = y1_low.shape[0]
    return pl.pallas_call(
        up_kernel,
        out_shape=(struct((8, rows, 512), BF), struct((8, rows, 512), BF)),
        in_specs=[SMEM, VMEM, VMEM] + [ANY] * 12,
        out_specs=(VMEM, VMEM),
        scratch_shapes=[
            pltpu.VMEM((8, D, 512), BF),
            pltpu.SemaphoreType.DMA((len(up_owners(0, 512)),)),
        ],
        compiler_params=params(48),
        cost_estimate=pl.CostEstimate(
            flops=8 * rows * D * D, bytes_accessed=17 << 20, transcendentals=0
        ),
        name="feed_up",
    )(scal, y1_low, up_bias, w_up, w_out, *pieces)


def down_kernel(scal, act, y1, cot, vecs, *rest):
    pieces, (out2, dh2, dz2, sums, held, acc, sems) = rest[:10], rest[10:]
    pairs, owners = down_pairs(pieces, held)
    groups = per_piece(pairs, owners, sems)
    for group in groups:
        start_all(group)
    acc[...] = y1[...] + vecs[5:6]
    for m, group in enumerate(groups):
        wait_all(group)
        b = scal[0] ^ PIECES[m]
        for r in (slice(0, 256), slice(256, 512)):
            acc[r, :] += contract(act[b, r, :], held[m], 1, 0)
    out, normed, inverse = norm_forward(acc[...], vecs[6:7], vecs[7:8])
    out2[...] = out.astype(BF)
    c = cot[...].astype(F32)
    grad = norm_backward(c, normed, inverse, vecs[6:7])
    dh2[...] = grad
    low = grad.astype(BF)
    dz2[...] = low
    sums[0:1, :] = jnp.sum(c * normed, 0, keepdims=True)
    sums[1:2, :] = jnp.sum(c, 0, keepdims=True)
    sums[2:3, :] = jnp.sum(low.astype(F32), 0, keepdims=True)


DOWN_COPIES = 6 * 4 + 2 * 8


def feed_down(scal, act, y1, cot, vecs, pieces):
    rows = y1.shape[0]
    return pl.pallas_call(
        down_kernel,
        out_shape=(
            struct((rows, D), BF),
            struct((rows, D), F32),
            struct((rows, D), BF),
            struct((8, D), F32),
        ),
        in_specs=[SMEM] + [VMEM] * 4 + [ANY] * 10,
        out_specs=(VMEM,) * 4,
        scratch_shapes=[
            pltpu.VMEM((8, 512, D), BF),
            pltpu.VMEM((rows, D), F32),
            pltpu.SemaphoreType.DMA((DOWN_COPIES,)),
        ],
        compiler_params=params(48),
        cost_estimate=pl.CostEstimate(
            flops=8 * rows * D * D, bytes_accessed=20 << 20, transcendentals=0
        ),
        name="feed_down",
    )(scal, act, y1, cot, vecs, *pieces)


def feed_back_kernel(scal, dz2, dh2, slope, n1, r1, vecs, w_up, w_out, *rest):
    ups, downs = rest[:10], rest[10:20]
    du, dh1, dao, dattn, sums, up_sums, up_held, down_held, acc, sems = rest[20:]
    pairs, owners = down_pairs(downs, down_held)
    down_groups = per_piece(pairs, owners, sems)
    up_groups = per_piece(
        up_pairs(scal, ups, (w_up, w_out), 0, 640, up_held), up_owners(0, 640), sems, DOWN_COPIES
    )
    for down_group, up_group in zip(down_groups, up_groups):
        start_all(down_group)
        start_all(up_group)
    acc[...] = dh2[...]
    for m in range(8):
        wait_all(down_groups[m])
        wait_all(up_groups[m])
        b = scal[0] ^ PIECES[m]
        total = jnp.zeros((1, 512), F32)
        for r in (slice(0, 256), slice(256, 512)):
            low = (contract(dz2[r, :], down_held[m], 1, 1) * slope[b, r, :].astype(F32)).astype(BF)
            du[b, r, :] = low
            total = total + jnp.sum(low.astype(F32), 0, keepdims=True)
            acc[r, :] += contract(low, up_held[m, :, 0:512], 1, 1)
        up_sums[pl.ds(b, 1), :] = total
    dy1 = acc[...]
    normed = n1[...]
    grad = norm_backward(dy1, normed, r1[:, 0:1], vecs[3:4])
    dh1[...] = grad
    low = grad.astype(BF)
    dao[...] = low
    sums[0:1, :] = jnp.sum(dy1 * normed, 0, keepdims=True)
    sums[1:2, :] = jnp.sum(dy1, 0, keepdims=True)
    sums[2:3, :] = jnp.sum(low.astype(F32), 0, keepdims=True)
    acc[...] = jnp.zeros_like(acc)
    for m in range(8):
        columns = pl.ds(pl.multiple_of((scal[0] ^ PIECES[m]) * 128, 128), 128)
        acc[...] += contract(dao[:, columns], up_held[m, :, 512:640], 1, 1)
    for t in range(4):
        dattn[t] = acc[:, 256 * t : 256 * (t + 1)].astype(BF)


def feed_back(scal, dz2, dh2, slope, n1, r1, vecs, w_up, w_out, ups, downs):
    rows = dz2.shape[0]
    return pl.pallas_call(
        feed_back_kernel,
        out_shape=(
            struct((8, rows, 512), BF),
            struct((rows, D), F32),
            struct((rows, D), BF),
            struct((4, rows, 256), BF),
            struct((8, D), F32),
            struct((8, 512), F32),
        ),
        in_specs=[SMEM] + [VMEM] * 6 + [ANY] * 22,
        out_specs=(VMEM,) * 6,
        scratch_shapes=[
            pltpu.VMEM((8, D, 640), BF),
            pltpu.VMEM((8, 512, D), BF),
            pltpu.VMEM((rows, D), F32),
            pltpu.SemaphoreType.DMA((DOWN_COPIES + len(up_owners(0, 640)),)),
        ],
        compiler_params=params(58),
        cost_estimate=pl.CostEstimate(
            flops=18 * rows * D * D, bytes_accessed=40 << 20, transcendentals=0
        ),
        name="feed_back",
    )(scal, dz2, dh2, slope, n1, r1, vecs, w_up, w_out, *ups, *downs)


def other_core(index_map):
    return lambda n, s: index_map(n, s[0] ^ 1, s)


def own_core(index_map):
    return lambda n, s: index_map(n, s[0], s)


def split_write(n, block, a_keep, a_send, b_keep, b_send):
    half = a_keep.shape[1]
    top_rows, low_rows = block[:half], block[half:]
    for step in range(4):

        @pl.when(n == step)
        def _():
            (a_send if step in (1, 3) else a_keep)[0] = top_rows
            (b_send if step in (2, 3) else b_keep)[0] = low_rows


def split_specs(rows, columns):
    half = (1, rows // 2, columns)
    return (
        pl.BlockSpec(half, lambda n, s: (n // 2, 0, 0)),
        pl.BlockSpec(half, lambda n, s: (n // 2, 0, 0)),
        pl.BlockSpec(half, lambda n, s: (jnp.minimum(n, 1), 0, 0)),
        pl.BlockSpec(half, lambda n, s: (jnp.maximum(n - 2, 0), 0, 0)),
    )


def split_shapes(rows, columns):
    return (struct((2, rows // 2, columns), BF),) * 4


def down_block(act, dz2):
    return jnp.concatenate([contract(act[f], dz2[...], 0, 0) for f in range(4)], 0)


def down_grad_other_kernel(scal, act, dz2, out):
    out[0] = down_block(act, dz2).astype(BF)


def down_grad_own_kernel(scal, act, dz2, came, *outs):
    block = (down_block(act, dz2) + came[0].astype(F32)).astype(BF)
    split_write(pl.program_id(0), block, *outs)


def down_grad(scal, act, dz2, came=None):
    rows = dz2.shape[0]
    act_map = lambda n, core, s: (core, 0, s[1 + n])
    cost = pl.CostEstimate(flops=4 * rows * D * D, bytes_accessed=9 << 20, transcendentals=0)
    dz2_spec = pl.BlockSpec((rows, D), lambda n, s: (0, 0))
    act_block = (4, rows, 128)
    if came is None:
        return pl.pallas_call(
            down_grad_other_kernel,
            out_shape=struct((4, 512, D), BF),
            grid_spec=pltpu.PrefetchScalarGridSpec(
                num_scalar_prefetch=1,
                grid=(4,),
                in_specs=[pl.BlockSpec(act_block, other_core(act_map)), dz2_spec],
                out_specs=pl.BlockSpec((1, 512, D), lambda n, s: (n, 0, 0)),
            ),
            compiler_params=params(40),
            cost_estimate=cost,
            name="down_grad_other",
        )(scal, act, dz2)
    return pl.pallas_call(
        down_grad_own_kernel,
        out_shape=split_shapes(512, D),
        grid_spec=pltpu.PrefetchScalarGridSpec(
            num_scalar_prefetch=1,
            grid=(4,),
            in_specs=[
                pl.BlockSpec(act_block, own_core(act_map)),
                dz2_spec,
                pl.BlockSpec((1, 512, D), lambda n, s: (n, 0, 0)),
            ],
            out_specs=split_specs(512, D),
        ),
        compiler_params=params(40),
        cost_estimate=cost,
        name="down_grad_own",
    )(scal, act, dz2, came)


UP_WIDTH = 4096 + 1024 + 128


def up_block(y1_low, du, attn, dao, small):
    left = y1_low[...]
    parts = [contract(left, du[b], 0, 0) for b in range(8)]
    parts.append(contract(attn[0], dao[...], 0, 0))
    parts.append(small[0])
    return jnp.concatenate(parts, 1)


def up_grad_other_kernel(scal, y1_low, du, attn, dao, small, out):
    out[0] = up_block(y1_low, du, attn, dao, small).astype(BF)


def up_grad_own_kernel(scal, y1_low, du, attn, dao, small, came, *outs):
    block = (up_block(y1_low, du, attn, dao, small) + came[0].astype(F32)).astype(BF)
    split_write(pl.program_id(0), block, *outs)


def up_grad(scal, y1_low, du, attn, dao, small, came=None):
    rows = dao.shape[0]
    side = other_core if came is None else own_core
    in_specs = [
        pl.BlockSpec((rows, 128), side(lambda n, core, s: (0, 2 * s[1 + n] + core))),
        pl.BlockSpec((8, rows, 512), lambda n, s: (0, 0, 0)),
        pl.BlockSpec((1, rows, 128), side(lambda n, core, s: (s[1 + n], 0, core))),
        pl.BlockSpec((rows, D), lambda n, s: (0, 0)),
        pl.BlockSpec((1, 128, 128), side(lambda n, core, s: (2 * s[1 + n] + core, 0, 0))),
    ]
    cost = pl.CostEstimate(flops=5 * rows * D * D, bytes_accessed=12 << 20, transcendentals=0)
    if came is None:
        return pl.pallas_call(
            up_grad_other_kernel,
            out_shape=struct((4, 128, UP_WIDTH), BF),
            grid_spec=pltpu.PrefetchScalarGridSpec(
                num_scalar_prefetch=1,
                grid=(4,),
                in_specs=in_specs,
                out_specs=pl.BlockSpec((1, 128, UP_WIDTH), lambda n, s: (n, 0, 0)),
            ),
            compiler_params=params(48),
            cost_estimate=cost,
            name="up_grad_other",
        )(scal, y1_low, du, attn, dao, small)
    return pl.pallas_call(
        up_grad_own_kernel,
        out_shape=split_shapes(128, UP_WIDTH),
        grid_spec=pltpu.PrefetchScalarGridSpec(
            num_scalar_prefetch=1,
            grid=(4,),
            in_specs=in_specs
            + [pl.BlockSpec((1, 128, UP_WIDTH), lambda n, s: (n, 0, 0))],
            out_specs=split_specs(128, UP_WIDTH),
        ),
        compiler_params=params(48),
        cost_estimate=cost,
        name="up_grad_own",
    )(scal, y1_low, du, attn, dao, small, came)


def add_low(a, b):
    return (a.astype(F32) + b.astype(F32)).astype(BF)


def reduce_chips(a_keep, a_send, b_keep, b_send):
    a_came = hop(a_send, 2)
    b_came = hop(b_send, 4)
    a_next = hop(add_low(a_keep[1], a_came[1]), 4)
    b_next = hop(add_low(b_keep[1], b_came[1]), 2)
    a_all = a_keep[0].astype(F32) + a_came[0].astype(F32) + a_next.astype(F32)
    b_all = b_keep[0].astype(F32) + b_came[0].astype(F32) + b_next.astype(F32)
    both = jnp.concatenate([a_all, b_all], 0).astype(BF)
    return lax.psum_scatter(both, "fsdp", scatter_dimension=0, tiled=True).astype(F32)


def after(value, *others):
    return lax.optimization_barrier((value,) + others)[0]


def near_chips(own):
    return hop(own, 2), hop(own, 4)


def gather_chips(own, from_x, from_y):
    half = own.shape[1] // 2
    mine = [own, from_x, from_y, hop(from_y[:, :half], 2), hop(from_x[:, half:], 4)]
    return mine + [hop(piece, 1) for piece in mine]


def tiled_device(
    tokens, cotangent, lengths, order, w_qkv, w_out, w_up, w_down, q_bias, v_bias, out_bias,
    norm1_gain, norm1_bias, up_bias, down_bias, norm2_gain, norm2_bias,
):
    me = lax.axis_index("ctx")
    shard = lax.axis_index("fsdp")
    core, low, top = me % 2, me % 4, me // 4
    chunk = tokens.shape[2]
    half_groups = [[0, 1, 2, 3], [4, 5, 6, 7]]
    scal = jnp.stack(
        [me, low, top, shard] + [(shard + 4 - k) % 4 for k in (1, 2, 3)]
    ).astype(jnp.int32)
    chips = jnp.stack([core] + [(me // 2) ^ n for n in range(4)]).astype(jnp.int32)
    first_length = jnp.where(top == 0, lengths[0, 0, 0], lengths[1, 0, 0])
    places = jnp.stack([first_length, top] + [(me ^ k) * chunk for k in CHUNKS]).astype(jnp.int32)
    small = jnp.concatenate(
        [
            q_bias, v_bias, out_bias, norm1_gain, norm1_bias, down_bias, norm2_gain, norm2_bias,
            up_bias, jnp.zeros((12 * 768,), BF),
        ]
    ).reshape(16, 768)
    own_rows, other_rows, cot_own, cot_other, pack, up_slice, down_slice = carve(
        scal, tokens, cotangent, w_qkv, w_out, w_up, w_down, small
    )

    packed = lax.all_gather(pack, "fsdp", axis=0)
    held = [own_rows, hop(other_rows, 4), hop(own_rows, 2), hop(other_rows, 6)]
    held = held + [hop(piece, 1) for piece in held]
    foreign = jnp.stack(
        [
            lax.ppermute(up_slice, "fsdp", [(i, (i + k) % 4) for i in range(4)])
            for k in (1, 2, 3)
        ]
    )
    vectors = packed[:, 256:260].reshape(4, 3072).astype(F32)
    vecs = vectors[:, :2048].reshape(4, 8, 256).transpose(1, 0, 2).reshape(8, D)
    up_b = vectors[:, 2048:].reshape(4, 8, 128).transpose(1, 0, 2).reshape(8, 512)
    qkv, x_all = project(scal, vecs, packed, held)

    down_own = lax.all_gather(after(down_slice, packed), "fsdp", axis=0)
    up_x, up_y = near_chips(foreign)
    attn_send, attn_t, lse = attention_forward(places, after(qkv, foreign), chunk)
    attn = lax.all_to_all(
        attn_send.reshape(4, 2 * chunk, 256), "ctx", 0, 0, tiled=True,
        axis_index_groups=half_groups,
    )
    up_x, up_y = lax.optimization_barrier((up_x, up_y, attn_send))[:2]
    ups = gather_chips(foreign, up_x, up_y)
    down_own = after(down_own, attn_send)
    down_x, down_y = near_chips(down_own)

    order_row = jnp.where(top == 0, order[0, 0], order[1, 0])
    cot_held = jnp.concatenate([cot_own, hop(cot_other, 4)], 0)
    cot_all = lax.all_gather(
        after(cot_held, down_own), "ctx", axis=0, tiled=True, axis_index_groups=half_groups
    )
    cot_blocks = cot_all.reshape(16, BLK, D)
    blocks = jnp.arange(16, dtype=jnp.int32)

    def held_place(block):
        device = block // 2
        return (device % 4) * 4 + ((device // 4) ^ top) * 2 + block % 2

    cot_rows = []
    for k in (0, 4):
        for e in range(2):
            given = 2 * (me ^ k) + e
            dealt = jnp.sum(jnp.where(order_row == given, blocks, 0))
            cot_rows.append(
                lax.dynamic_index_in_dim(cot_blocks, held_place(dealt), 0, False)
            )
    cot_rows = jnp.concatenate(cot_rows, 0)

    y1, y1_low, n1, r1 = attention_out(scal, attn, x_all, vecs, w_up, w_out, ups)
    act, slope = feed_up(scal, y1_low, up_b, w_up, w_out, ups)
    downs = gather_chips(down_own, down_x, down_y)
    out2, dh2, dz2, sums2 = feed_down(scal, act, y1, cot_rows, vecs, downs)

    out_all = lax.all_gather(out2, "ctx", axis=0, tiled=True, axis_index_groups=half_groups)
    out_blocks = out_all.reshape(16, BLK, D)

    def dealt_rows(device):
        rows = []
        for e in range(2):
            given = jnp.sum(jnp.where(blocks == 2 * device + e, order_row, 0))
            rows.append(lax.dynamic_index_in_dim(out_blocks, held_place(given), 0, False))
        return jnp.concatenate(rows, 0)

    down_other = down_grad(chips, act, dz2)
    du, dh1, dao, dattn, sums1, up_sums = feed_back(
        scal, after(dz2, down_other), dh2, slope, n1, r1, vecs, w_up, w_out, ups, downs
    )
    dattn_send = dattn
    dattn = lax.all_to_all(
        dattn, "ctx", 0, 0, tiled=True, axis_index_groups=half_groups
    ).reshape(4, 2, chunk, 256)
    down_parts = down_grad(chips, after(act, dattn_send), dz2, hop(down_other, 1))

    def per_owner(vector):
        return vector.reshape(8, 4, 32)

    up_owner = up_sums.reshape(8, 4, 128).transpose(1, 0, 2).reshape(8, 4, 128)
    vec_block = jnp.concatenate(
        [per_owner(sums1[2]), per_owner(sums1[0]), per_owner(sums1[1]), per_owner(sums2[2]),
         per_owner(sums2[0]), per_owner(sums2[1]), up_owner, jnp.zeros((8, 4, 64), F32)], 2
    ).reshape(8, 4, 3, 128)
    vec_block = jnp.concatenate([vec_block, jnp.zeros((8, 4, 29, 128), F32)], 2).reshape(
        8, 128, 128
    )
    up_other = up_grad(chips, y1_low, after(du, down_parts[0]), attn, dao, vec_block)
    up_parts = up_grad(chips, y1_low, du, attn, dao, vec_block, hop(up_other, 1))

    dattn, out_blocks = lax.optimization_barrier((dattn, out_blocks, *up_parts))[:2]
    dqkv = attention_backward(places, qkv, dattn, attn_t, lse, chunk)
    down_rows = reduce_chips(*down_parts)
    up_rows = reduce_chips(*up_parts)

    mixed_own = dealt_rows(me)
    mixed_came = hop(dealt_rows(me ^ 4), 4)
    mixed = jnp.where(
        top == 0, jnp.stack([mixed_own, mixed_came]), jnp.stack([mixed_came, mixed_own])
    )[:, None]

    grad_qkv = contract(x_all, dqkv, 0, 0)
    column_sums = jnp.sum(dqkv.astype(F32), 0)
    spread = (jnp.arange(4) == low).astype(F32)[:, None]
    q_sum = (spread * column_sums[None, :256]).reshape(D, 1)
    v_sum = (spread * column_sums[None, 512:]).reshape(D, 1)
    grad_qkv = jnp.concatenate([grad_qkv, q_sum, v_sum, jnp.zeros((D, 126), F32)], 1).astype(BF)
    grad_qkv = grad_qkv.reshape(2, 4, 4, 32, 896).transpose(0, 2, 1, 3, 4)
    keep = lax.dynamic_index_in_dim(grad_qkv, top, 0, False)
    send = lax.dynamic_index_in_dim(grad_qkv, 1 - top, 0, False)
    pair = add_low(keep, hop(send, 4)).reshape(16 * 32, 896)
    mine = lax.psum_scatter(pair, "fsdp", scatter_dimension=0, tiled=True)
    mine = lax.all_to_all(
        mine.reshape(4, 32, 896), "ctx", 0, 0, tiled=True, axis_index_groups=half_groups
    ).astype(F32)
    w_qkv_grad = mine[:, :, :768].reshape(4, 32, 3, 256).transpose(1, 2, 0, 3).reshape(32, 3072)
    q_bias_grad = jnp.sum(mine[:, :, 768], 0)
    v_bias_grad = jnp.sum(mine[:, :, 769], 0)

    qkv_weight = packed[:, :256].reshape(D, 768)
    dx = contract(dqkv, qkv_weight, 1, 1).astype(BF).reshape(8, chunk, D)
    dx = add_low(dx[:4], hop(dx[4:], 1))
    dx = dx[:2].astype(F32) + hop(dx[2:], 2).astype(F32)
    dx = (dx.reshape(2 * chunk, D) + dh1).astype(BF)
    grad_own = dx[:chunk]
    grad_came = hop(dx[chunk:], 4)
    tokens_grad = jnp.where(
        top == 0, jnp.stack([grad_own, grad_came]), jnp.stack([grad_came, grad_own])
    )[:, None]

    w_up_grad = (
        up_rows[:, :4096].reshape(32, 8, 4, 128).transpose(0, 2, 1, 3).reshape(32, 4096)
    )
    w_out_grad = up_rows[:, 4096:5120]
    sums = up_rows[:3, 5120:].reshape(384)
    return (
        mixed, tokens_grad, w_qkv_grad, w_out_grad, w_up_grad, down_rows, q_bias_grad, v_bias_grad,
        sums[0:32], sums[32:64], sums[64:96], sums[192:320], sums[96:128], sums[128:160],
        sums[160:192],
    )


def pick_blocks(wanted, rows):
    shaped = rows.reshape(-1, BLK, rows.shape[-1])
    picked = [
        lax.dynamic_index_in_dim(shaped, wanted[e], 0, False) for e in range(wanted.shape[0])
    ]
    return jnp.concatenate(picked, 0)


def plain_device(
    tokens, cotangent, lengths, order, w_qkv, w_out, w_up, w_down, q_bias, v_bias, out_bias,
    norm1_gain, norm1_bias, up_bias, down_bias, norm2_gain, norm2_bias,
):
    shards = (
        w_qkv, w_out, w_up, w_down, q_bias, v_bias, out_bias, norm1_gain, norm1_bias, up_bias,
        down_bias, norm2_gain, norm2_bias,
    )
    me = lax.axis_index("ctx")
    count = lax.axis_size("ctx")
    rows = tokens.shape[2]
    per_device = rows // BLK
    whole_rows = rows * count
    scaling = 1.0 / math.sqrt(HD)
    (
        qkv_full, out_full, up_full, down_full, qbias_full, vbias_full, obias_full, gain_one,
        shift_one, ubias_full, dbias_full, gain_two, shift_two,
    ) = tuple(lax.all_gather(shard, "fsdp", axis=0, tiled=True) for shard in shards)
    full_bias = jnp.concatenate([qbias_full, jnp.zeros_like(qbias_full), vbias_full]).astype(F32)
    gain_one, shift_one, gain_two, shift_two = (
        vector.astype(F32) for vector in (gain_one, shift_one, gain_two, shift_two)
    )
    positions = jnp.arange(whole_rows, dtype=jnp.int32)
    mixed_list, grad_list, totals = [], [], None
    for micro in range(tokens.shape[0]):
        order_row = order[micro, 0]
        bound = lengths[micro, 0, 0]
        segment_all = (positions >= bound).astype(jnp.int32)
        segment_query = (me * rows + jnp.arange(rows, dtype=jnp.int32) >= bound).astype(jnp.int32)
        dealt = me * per_device + jnp.arange(per_device, dtype=jnp.int32)
        blocks = jnp.arange(order_row.shape[0], dtype=jnp.int32)
        inverse = jnp.sum(jnp.where(order_row[None, :] == dealt[:, None], blocks[None, :], 0), 1)
        forward = jnp.sum(jnp.where(blocks[None, :] == dealt[:, None], order_row[None, :], 0), 1)
        token_rows = tokens[micro, 0]
        cot_rows = pick_blocks(
            inverse, lax.all_gather(cotangent[micro, 0], "ctx", axis=0, tiled=True)
        ).astype(F32)
        qkv_rows = (jnp.dot(token_rows, qkv_full, preferred_element_type=F32) + full_bias).astype(BF)
        queries = qkv_rows[:, :D].reshape(rows, H, HD)
        keys_values = lax.all_gather(qkv_rows[:, D:], "ctx", axis=0, tiled=True)
        keys = keys_values[:, :D].reshape(whole_rows, H, HD)
        values = keys_values[:, D:].reshape(whole_rows, H, HD)
        allowed = (segment_query[:, None] == segment_all[None, :])[None]
        scores = jnp.einsum("rhd,khd->hrk", queries, keys, preferred_element_type=F32) * scaling
        scores = jnp.where(allowed, scores, NEGATIVE)
        expos = jnp.where(allowed, jnp.exp(scores - jnp.max(scores, -1, keepdims=True)), 0.0)
        probs = expos / jnp.sum(expos, -1, keepdims=True)
        probs_low = probs.astype(BF)
        attn_float = jnp.einsum("hrk,khd->rhd", probs_low, values, preferred_element_type=F32)
        attn_low = attn_float.reshape(rows, D).astype(BF)
        first_in = (
            token_rows.astype(F32)
            + jnp.dot(attn_low, out_full, preferred_element_type=F32)
            + obias_full.astype(F32)
        )
        first_out, normed_one, inverse_one = norm_forward(first_in, gain_one, shift_one)
        first_low = first_out.astype(BF)
        hidden_in = jnp.dot(first_low, up_full, preferred_element_type=F32) + ubias_full.astype(F32)
        activated, gelu_back = jax.vjp(partial(jax.nn.gelu, approximate=False), hidden_in)
        act_low = activated.astype(BF)
        second_in = (
            first_out
            + jnp.dot(act_low, down_full, preferred_element_type=F32)
            + dbias_full.astype(F32)
        )
        second_out, normed_two, inverse_two = norm_forward(second_in, gain_two, shift_two)
        out_all = lax.all_gather(second_out.astype(BF), "ctx", axis=0, tiled=True)
        mixed_list.append(pick_blocks(forward, out_all))

        grad_second = norm_backward(cot_rows, normed_two, inverse_two, gain_two)
        grad_down_low = grad_second.astype(BF)
        (grad_hidden,) = gelu_back(contract(grad_down_low, down_full, 1, 1))
        grad_hidden_low = grad_hidden.astype(BF)
        grad_first = grad_second + contract(grad_hidden_low, up_full, 1, 1)
        grad_first_in = norm_backward(grad_first, normed_one, inverse_one, gain_one)
        grad_branch = grad_first_in.astype(BF)
        grad_attn = contract(grad_branch, out_full, 1, 1).astype(BF).reshape(rows, H, HD)
        grad_probs = jnp.einsum("rhd,khd->hrk", grad_attn, values, preferred_element_type=F32)
        delta = jnp.sum(probs * grad_probs, -1, keepdims=True)
        grad_scores = (probs * (grad_probs - delta) * scaling).astype(BF)
        grad_query = jnp.einsum("hrk,khd->rhd", grad_scores, keys, preferred_element_type=F32)
        grad_keys = jnp.einsum("hrk,rhd->khd", grad_scores, queries, preferred_element_type=F32)
        grad_values = jnp.einsum("hrk,rhd->khd", probs_low, grad_attn, preferred_element_type=F32)
        both = jnp.concatenate(
            [grad_keys.reshape(whole_rows, D), grad_values.reshape(whole_rows, D)], 1
        )
        both = lax.psum_scatter(both, "ctx", scatter_dimension=0, tiled=True)
        grad_qkv = jnp.concatenate([grad_query.reshape(rows, D), both], 1).astype(BF)
        column_sums = jnp.sum(grad_qkv.astype(F32), 0)
        grad_list.append((grad_first_in + contract(grad_qkv, qkv_full, 1, 1)).astype(BF))
        parts = (
            contract(token_rows, grad_qkv, 0, 0),
            contract(attn_low, grad_branch, 0, 0),
            contract(first_low, grad_hidden_low, 0, 0),
            contract(act_low, grad_down_low, 0, 0),
            column_sums[:D],
            column_sums[2 * D :],
            jnp.sum(grad_branch.astype(F32), 0),
            jnp.sum(grad_first * normed_one, 0),
            jnp.sum(grad_first, 0),
            jnp.sum(grad_hidden_low.astype(F32), 0),
            jnp.sum(grad_down_low.astype(F32), 0),
            jnp.sum(cot_rows * normed_two, 0),
            jnp.sum(cot_rows, 0),
        )
        totals = parts if totals is None else tuple(a + b for a, b in zip(totals, parts))
    shares = tuple(
        lax.psum_scatter(part, ("ctx", "fsdp"), scatter_dimension=0, tiled=True) for part in totals
    )
    return (jnp.stack(mixed_list)[:, None], jnp.stack(grad_list)[:, None]) + shares


def solution(mesh):
    fits = mesh.shape["ctx"] == 8 and mesh.shape["fsdp"] == 4
    weights = (P("fsdp", None),) * 4 + (P("fsdp"),) * 9
    owners = (P(("ctx", "fsdp"), None),) * 4 + (P(("ctx", "fsdp")),) * 9
    rows = P(None, "fsdp", "ctx", None)
    return jax.shard_map(
        tiled_device if fits else plain_device,
        mesh=mesh,
        in_specs=(rows, rows, P(None, "fsdp", None), P(None, "fsdp", None)) + weights,
        out_specs=(rows, rows) + owners,
        check_vma=False,
    )
```

```python
from functools import partial
import math

import jax
import jax.numpy as jnp
from jax import lax
from jax.experimental import pallas as pl
from jax.experimental.pallas import tpu as pltpu
from jax.sharding import PartitionSpec as P

D = 1024
H = 16
HD = 64
BLK = 128
MB = 2

NEGATIVE = -1e30
EPSILON = 1e-05
BF = jnp.bfloat16
F32 = jnp.float32


def contract(a, b, ca, cb):
    return lax.dot_general(a, b, (((ca,), (cb,)), ((), ())), preferred_element_type=F32)


def norm_forward(values_in, gain_vec, shift_vec):
    center = values_in - jnp.mean(values_in, -1, keepdims=True)
    inverse = lax.rsqrt(jnp.mean(center * center, -1, keepdims=True) + EPSILON)
    normed = center * inverse
    return (normed * gain_vec + shift_vec, normed, inverse)


def norm_backward(grad_out, normed, inverse, gain_vec):
    grad_norm = grad_out * gain_vec
    return inverse * (
        grad_norm
        - jnp.mean(grad_norm, -1, keepdims=True)
        - normed * jnp.mean(grad_norm * normed, -1, keepdims=True)
    )


def hop(value, mask):
    count = lax.axis_size("ctx")
    return lax.ppermute(value, "ctx", [(i, i ^ mask) for i in range(count)])


VMEM = pl.BlockSpec(memory_space=pltpu.VMEM)
SMEM = pl.BlockSpec(memory_space=pltpu.SMEM)
HBM = pl.BlockSpec(memory_space=pltpu.HBM)


def takes(microseconds):
    return pl.CostEstimate(
        flops=int(microseconds * 1.15e9), bytes_accessed=1 << 20, transcendentals=0
    )


def params(mib):
    return pltpu.CompilerParams(vmem_limit_bytes=mib << 20)


def struct(shape, dtype):
    return jax.ShapeDtypeStruct(shape, dtype)


ME, LOW, TOP, SHARD, CORE, CHIP, SPLIT, ORDER, INVERSE = 0, 1, 2, 3, 7, 8, 9, 10, 26
CHUNKS = (0, 4, 2, 6, 1, 5, 3, 7)
ROWS = 512


def scalars(order, lengths):
    me = lax.axis_index("ctx")
    shard = lax.axis_index("fsdp")
    core, low, top = me % 2, me % 4, me // 4
    order_row = jnp.where(top == 0, order[0, 0], order[1, 0])
    first = jnp.where(top == 0, lengths[0, 0, 0], lengths[1, 0, 0])
    blocks = jnp.arange(16, dtype=jnp.int32)
    inverse = jnp.sum(jnp.where(order_row[None, :] == blocks[:, None], blocks[None, :], 0), 1)
    others = [(shard + 4 - k) % 4 for k in (1, 2, 3)]
    return jnp.concatenate(
        [jnp.stack([me, low, top, shard, *others, core, me // 2, first]), order_row, inverse]
    ).astype(jnp.int32)


def start_all(copies):
    for copy in copies:
        copy.start()


def wait_all(copies):
    for copy in copies:
        copy.wait()


def copies_of(pairs, sems, base=0):
    return [
        pltpu.make_async_copy(a, b, sems.at[base + i]) for i, (a, b) in enumerate(pairs)
    ]


def aligned(start, size):
    return pl.ds(pl.multiple_of(start, size), size)


def segment_lanes(first, rows, split, is_query):
    position = first + lax.broadcasted_iota(jnp.int32, (rows, HD), 0)
    lane = lax.broadcasted_iota(jnp.int32, (rows, HD), 1)
    second = (position >= split).astype(jnp.int32)
    if is_query:
        return jnp.where(lane == 1 - second, NEGATIVE, 0.0).astype(BF)
    return jnp.where(lane == second, 1.0, 0.0).astype(BF)


def key_range(q0, bq, split, bk, total):
    begin = jnp.where(q0 >= split, split // bk, 0)
    end = jnp.where(q0 + bq <= split, (split + bk - 1) // bk, total // bk)
    return begin, end


def widen(scal, qkv, qa, ka, begin, heads, chunk):
    total = qkv.shape[0]
    width = qkv.shape[1] // 3
    split = scal[SPLIT]
    for m in range(total // chunk):
        pos = pl.multiple_of((scal[ME] ^ CHUNKS[m]) * chunk, chunk)
        rows = slice(m * chunk, (m + 1) * chunk)
        qtail = segment_lanes(pos, chunk, split, True)
        ktail = segment_lanes(pos, chunk, split, False)
        for h in range(heads):
            at = begin + h * HD
            q = qkv[rows, at : at + HD]
            k = qkv[rows, width + at : width + at + HD]
            q = (q.astype(F32) * 0.125).astype(BF)
            qa[h, pl.ds(pos, chunk), :] = jnp.concatenate([q, qtail], 1)
            ka[h, pl.ds(pos, chunk), :] = jnp.concatenate([k, ktail], 1)


def attention_forward_kernel(
    scal, qkv, out0, out1, out2, out3, out_t, lse, qa, ka, vt, sc, out, *, heads, chunk, bq, bk
):
    total = qkv.shape[0]
    width = qkv.shape[1] // 3
    split = scal[SPLIT]
    widen(scal, qkv, qa, ka, 0, heads, chunk)
    for m in range(total // chunk):
        pos = pl.multiple_of((scal[ME] ^ CHUNKS[m]) * chunk, chunk)
        rows = slice(m * chunk, (m + 1) * chunk)
        vt[:, pl.ds(pos, chunk)] = qkv[rows, 2 * width :].T

    def q_step(qi, _):
        q0 = pl.multiple_of(qi * bq, bq)
        begin_k, end_k = key_range(q0, bq, split, bk, total)

        def max_step(ki, carry):
            k0 = pl.multiple_of(ki * bk, bk)
            result = []
            for h in range(heads):
                st = contract(ka[h, pl.ds(k0, bk), :], qa[h, pl.ds(q0, bq), :], 1, 1)
                sc[h, pl.ds(k0, bk), :] = st
                result.append(jnp.maximum(carry[h], jnp.max(st.reshape(bk // 8, 8, bq), 0)))
            return tuple(result)

        start = tuple(jnp.full((8, bq), NEGATIVE, F32) for _ in range(heads))
        peaks = lax.fori_loop(begin_k, end_k, max_step, start)
        peaks = [jnp.max(m, 0, keepdims=True) for m in peaks]

        def k_step(ki, carry):
            k0 = pl.multiple_of(ki * bk, bk)
            result = []
            for h in range(heads):
                total_p, acc = carry[2 * h : 2 * h + 2]
                p = jnp.exp(sc[h, pl.ds(k0, bk), :] - peaks[h])
                total_p = total_p + jnp.sum(p.reshape(bk // 8, 8, bq), 0)
                acc = acc + contract(
                    vt[h * HD : (h + 1) * HD, pl.ds(k0, bk)], p.astype(BF), 1, 0
                )
                result += [total_p, acc]
            return tuple(result)

        start = []
        for h in range(heads):
            start += [jnp.zeros((8, bq), F32), jnp.zeros((HD, bq), F32)]
        done = lax.fori_loop(begin_k, end_k, k_step, tuple(start))
        pieces = []
        for h in range(heads):
            denom = jnp.sum(done[2 * h], 0, keepdims=True)
            pieces.append(done[2 * h + 1] / denom)
            lse[h : h + 1, pl.ds(q0, bq)] = peaks[h] + jnp.log(denom)
        turned = jnp.concatenate(pieces, 0)
        out_t[:, pl.ds(q0, bq)] = turned
        low_rows = turned.T.astype(BF)
        for i in range(bq // BLK):
            place = scal[INVERSE + q0 // BLK + i]
            device = place // 2
            row = ((device // 4) ^ scal[TOP]) * 256 + (place % 2) * BLK
            out[(device % 4) ^ scal[LOW], aligned(row, BLK), :] = low_rows[
                i * BLK : (i + 1) * BLK
            ]
        return 0

    lax.fori_loop(0, total // bq, q_step, 0)
    for k, sent in enumerate((out0, out1, out2, out3)):
        sent[...] = out[k]


def attention_forward(scal, qkv, chunk, bq=512, bk=512):
    total = qkv.shape[0]
    width = qkv.shape[1] // 3
    heads = width // HD
    return pl.pallas_call(
        partial(attention_forward_kernel, heads=heads, chunk=chunk, bq=bq, bk=bk),
        out_shape=(struct((ROWS, width), BF),) * 4
        + (struct((width, total), F32), struct((heads, total), F32)),
        in_specs=[SMEM, VMEM],
        out_specs=(VMEM,) * 6,
        scratch_shapes=[
            pltpu.VMEM((heads, total, 128), BF),
            pltpu.VMEM((heads, total, 128), BF),
            pltpu.VMEM((width, total), BF),
            pltpu.VMEM((heads, total, bq), F32),
            pltpu.VMEM((4, ROWS, width), BF),
        ],
        compiler_params=params(60),
        cost_estimate=takes(23),
        name="attention_forward",
    )(scal, qkv)


def attention_backward_kernel(
    scal, qkv, grad0, grad1, grad2, grad3, out_t, lse, dqkv, qa, ka, kt, va, ga, gt, dkv, dq,
    *, first, heads, chunk, bq, bk
):
    total = qkv.shape[0]
    width = qkv.shape[1] // 3
    begin = first * HD
    end = begin + heads * HD
    split = scal[SPLIT]
    blank = jnp.zeros((chunk, HD), BF)
    short = jnp.zeros((BLK, HD), BF)
    widen(scal, qkv, qa, ka, begin, heads, chunk)
    for m in range(total // chunk):
        pos = pl.multiple_of((scal[ME] ^ CHUNKS[m]) * chunk, chunk)
        rows = slice(m * chunk, (m + 1) * chunk)
        for h in range(heads):
            at = 2 * width + begin + h * HD
            va[h, pl.ds(pos, chunk), :] = jnp.concatenate([qkv[rows, at : at + HD], blank], 1)
        kt[:, pl.ds(pos, chunk)] = qkv[rows, width + begin : width + end].T
    for k, grad in enumerate((grad0, grad1, grad2, grad3)):
        for e in range(4):
            device = (scal[LOW] ^ k) + 4 * ((e // 2) ^ scal[TOP])
            pos = pl.multiple_of(scal[ORDER + 2 * device + e % 2] * BLK, BLK)
            rows = slice(e * BLK, (e + 1) * BLK)
            for h in range(heads):
                g = grad[rows, begin + h * HD : begin + (h + 1) * HD]
                ga[h, pl.ds(pos, BLK), :] = jnp.concatenate([g, short], 1)
            gt[:, pl.ds(pos, BLK)] = grad[rows, begin:end].T
    dkv[...] = jnp.zeros_like(dkv)

    def q_step(qi, _):
        q0 = pl.multiple_of(qi * bq, bq)
        begin_k, end_k = key_range(q0, bq, split, bk, total)
        product = gt[:, pl.ds(q0, bq)].astype(F32) * out_t[begin:end, pl.ds(q0, bq)]
        delta = [jnp.sum(product[h * HD : (h + 1) * HD], 0, keepdims=True) for h in range(heads)]
        held_lse = lse[:, pl.ds(q0, bq)]
        totals = [held_lse[first + h : first + h + 1] for h in range(heads)]

        def k_step(ki, carry):
            k0 = pl.multiple_of(ki * bk, bk)
            result = []
            for h in range(heads):
                q = qa[h, pl.ds(q0, bq), :]
                g = ga[h, pl.ds(q0, bq), :]
                st = contract(ka[h, pl.ds(k0, bk), :], q, 1, 1)
                p = jnp.exp(st - totals[h])
                dp = contract(va[h, pl.ds(k0, bk), :], g, 1, 1)
                ds = (p * (dp - delta[h]) * 0.125).astype(BF)
                dkv[0, h, pl.ds(k0, bk), :] += contract(ds, q, 1, 0)
                dkv[1, h, pl.ds(k0, bk), :] += contract(p.astype(BF), g, 1, 0)
                result.append(
                    carry[h] + contract(kt[h * HD : (h + 1) * HD, pl.ds(k0, bk)], ds, 1, 0)
                )
            return tuple(result)

        start = tuple(jnp.zeros((HD, bq), F32) for _ in range(heads))
        turned = lax.fori_loop(begin_k, end_k, k_step, start)
        dq[pl.ds(q0, bq), :] = jnp.concatenate(turned, 0).T.astype(BF)
        return 0

    lax.fori_loop(0, total // bq, q_step, 0)
    for m in range(total // chunk):
        pos = pl.multiple_of((scal[ME] ^ CHUNKS[m]) * chunk, chunk)
        rows = slice(m * chunk, (m + 1) * chunk)
        dqkv[rows, 0 : heads * HD] = dq[pl.ds(pos, chunk), :]
        for h in range(0, heads, 2):
            for part, gain in ((0, 8.0), (1, 1.0)):
                pair = [dkv[part, h + e, pl.ds(pos, chunk), :][:, :HD] for e in range(2)]
                base = ((1 + part) * heads + h) * HD
                dqkv[rows, base : base + 2 * HD] = (jnp.concatenate(pair, 1) * gain).astype(BF)


def attention_backward(scal, qkv, grads, out_t, lse, chunk, first, heads, bq=512, bk=512):
    total = qkv.shape[0]
    width = heads * HD
    wide = pltpu.VMEM((heads, total, 128), BF)
    return pl.pallas_call(
        partial(
            attention_backward_kernel, first=first, heads=heads, chunk=chunk, bq=bq, bk=bk
        ),
        out_shape=struct((total, 3 * width), BF),
        in_specs=[SMEM] + [VMEM] * 7,
        out_specs=VMEM,
        scratch_shapes=[
            wide,
            wide,
            pltpu.VMEM((width, total), BF),
            wide,
            wide,
            pltpu.VMEM((width, total), BF),
            pltpu.VMEM((2, heads, total, 128), F32),
            pltpu.VMEM((total, width), BF),
        ],
        compiler_params=params(60),
        cost_estimate=takes(19),
        name="attention_backward",
    )(scal, qkv, *grads, out_t, lse)


def carve_kernel(
    tokens, cot, w_qkv, w_out, w_up, w_down, small,
    own, other, cot_own, cot_other, pack, pack_sent, up_slice, down_slice, sems,
):
    me = lax.axis_index("ctx")
    core, low, top, chip = me % 2, me % 4, me // 4, me // 2
    block = core * 4 + chip
    pairs = [(tokens.at[top, 0], own), (tokens.at[1 - top, 0], other)]
    half = aligned(top * 128, 128)
    for k in range(3):
        columns = aligned(k * D + low * 256, 256)
        target = slice(256 * k, 256 * (k + 1))
        pairs.append((w_qkv.at[:, columns], pack.at[:, target]))
        pairs.append((w_qkv.at[half, columns], pack_sent.at[0:128, target]))
    for k in range(4):
        columns = aligned(k * D + block * 128, 128)
        pairs.append((w_up.at[:, columns], up_slice.at[:, 128 * k : 128 * (k + 1)]))
    pairs.append((w_out.at[:, aligned(block * 128, 128)], up_slice.at[:, 512:640]))
    pairs.append((w_down.at[aligned(core * 512 + top * 128, 128), :], down_slice.at[0]))
    side = core * 512 + 256 + (chip % 2) * 128
    pairs.append((w_down.at[aligned(side, 128), :], down_slice.at[1]))
    pairs += [(cot.at[top, 0], cot_own), (cot.at[1 - top, 0], cot_other)]
    copies = copies_of(pairs, sems)
    start_all(copies)
    pack_sent[128:144, 0:256] = small[...]
    wait_all(copies)


def carve(tokens, cot, w_qkv, w_out, w_up, w_down, small):
    rows = tokens.shape[2]
    return pl.pallas_call(
        carve_kernel,
        out_shape=tuple(struct((rows, D), BF) for _ in range(4))
        + (
            struct((256, 768), BF),
            struct((144, 768), BF),
            struct((256, 640), BF),
            struct((2, 128, D), BF),
        ),
        in_specs=[HBM] * 6 + [VMEM],
        out_specs=(VMEM,) * 8,
        scratch_shapes=[pltpu.SemaphoreType.DMA((17,))],
        compiler_params=params(60),
        cost_estimate=takes(4),
        name="carve",
    )(tokens, cot, w_qkv, w_out, w_up, w_down, small)


def project_kernel(
    scal, pack, small, near, away, own, y, x, core_own, core_rest,
    qkv, x_all, weight, vecs, up_bias, qkv_held, x_held, rows_held, sems, out_sems,
):
    chunk = own.shape[0]
    own_f = scal[SHARD]
    pairs = [(pack, weight.at[aligned(own_f * 256, 256)]), (small, rows_held.at[own_f])]
    for k in range(3):
        f = scal[SHARD + 1 + k]
        mine = aligned(f * 256 + scal[TOP] * 128, 128)
        rest = aligned(f * 256 + (1 - scal[TOP]) * 128, 128)
        pairs.append((near.at[k, 0:128], weight.at[mine]))
        pairs.append((away.at[k, 0:128], weight.at[rest]))
        pairs.append((near.at[k, 128:144, 0:256], rows_held.at[f]))
    loads = len(pairs)
    sources = [own, y, x.at[0], x.at[1], core_own] + [core_rest.at[k] for k in range(3)]
    pairs += [
        (piece, x_held.at[m * chunk : (m + 1) * chunk]) for m, piece in enumerate(sources)
    ]
    copies = copies_of(pairs, sems)
    start_all(copies)
    wait_all(copies[:loads])
    for f in range(4):
        held = rows_held[f].astype(F32)
        vecs[:, 256 * f : 256 * (f + 1)] = held[0:8]
        for j in range(4):
            for e in range(2):
                up_bias[2 * j + e : 2 * j + e + 1, 128 * f : 128 * (f + 1)] = held[
                    8 + j : 9 + j, 128 * e : 128 * (e + 1)
                ]
    here = aligned(scal[LOW] * 256, 256)
    bias = jnp.concatenate([vecs[0:1, here], jnp.zeros((1, 256), F32), vecs[1:2, here]], 1)
    outs = []
    for m in range(8):
        copies[loads + m].wait()
        rows = slice(m * chunk, (m + 1) * chunk)
        qkv_held[rows, :] = (contract(x_held[rows, :], weight[...], 1, 0) + bias).astype(BF)
        sent = copies_of(
            [(x_held.at[rows], x_all.at[rows]), (qkv_held.at[rows], qkv.at[rows])], out_sems, 2 * m
        )
        start_all(sent)
        outs += sent
    wait_all(outs)


def project(scal, pack, small, near, away, pieces):
    chunk = pieces[0].shape[0]
    return pl.pallas_call(
        project_kernel,
        out_shape=(
            struct((8 * chunk, 768), BF),
            struct((8 * chunk, D), BF),
            struct((D, 768), BF),
            struct((8, D), F32),
            struct((8, 512), F32),
        ),
        in_specs=[SMEM] + [HBM] * 9,
        out_specs=(HBM, HBM, VMEM, VMEM, VMEM),
        scratch_shapes=[
            pltpu.VMEM((8 * chunk, 768), BF),
            pltpu.VMEM((8 * chunk, D), BF),
            pltpu.VMEM((4, 16, 256), BF),
            pltpu.SemaphoreType.DMA((19,)),
            pltpu.SemaphoreType.DMA((16,)),
        ],
        compiler_params=params(60),
        cost_estimate=takes(8),
        name="project",
    )(scal, pack, small, near, away, *pieces)


def out_pairs(scal, near, away, w_out, held):
    pairs = []
    for side, pieces in enumerate((near, away)):
        for m in range(4):
            block = 4 * (scal[CORE] ^ side) + (scal[CHIP] ^ m)
            for k in range(3):
                rows = aligned(scal[SHARD + 1 + k] * 256, 256)
                pairs.append((pieces.at[m, k], held.at[block, rows]))
            columns = aligned(block * 128, 128)
            rows = aligned(scal[SHARD] * 256, 256)
            pairs.append((w_out.at[:, columns], held.at[block, rows]))
    return pairs


def attention_out_kernel(
    scal, h0, h1, h2, h3, vecs, x_all, w_out, near, away, y1, y1_low, n1, r1, held, x, sems
):
    pairs = out_pairs(scal, near, away, w_out, held)
    for e in range(4):
        device = scal[ME] ^ (4 * (e // 2))
        given = scal[ORDER + 2 * device + e % 2]
        turn = scal[ME] ^ (given // 2)
        chunk = (turn % 2) * 4 + ((turn // 2) % 2) * 2 + turn // 4
        rows = aligned(chunk * 256 + (given % 2) * BLK, BLK)
        pairs.append((x_all.at[rows, :], x.at[e * BLK : (e + 1) * BLK]))
    copies = copies_of(pairs, sems)
    start_all(copies)
    wait_all(copies)
    columns = []
    for b in range(8):
        part = 0.0
        for k, heads in enumerate((h0, h1, h2, h3)):
            rows = aligned((scal[LOW] ^ k) * 256, 256)
            part = part + contract(heads[...], held[b, rows, :], 1, 0)
        columns.append(part)
    into = x[...].astype(F32) + jnp.concatenate(columns, 1) + vecs[2:3]
    out, normed, inverse = norm_forward(into, vecs[3:4], vecs[4:5])
    y1[...] = out
    y1_low[...] = out.astype(BF)
    n1[...] = normed
    r1[...] = jnp.broadcast_to(inverse, r1.shape)


def attention_out(scal, heads, vecs, x_all, w_out, near, away):
    return pl.pallas_call(
        attention_out_kernel,
        out_shape=(
            struct((ROWS, D), F32),
            struct((ROWS, D), BF),
            struct((ROWS, D), F32),
            struct((ROWS, 128), F32),
        ),
        in_specs=[SMEM] + [VMEM] * 5 + [HBM] * 4,
        out_specs=(VMEM,) * 4,
        scratch_shapes=[
            pltpu.VMEM((8, D, 128), BF),
            pltpu.VMEM((ROWS, D), BF),
            pltpu.SemaphoreType.DMA((36,)),
        ],
        compiler_params=params(60),
        cost_estimate=takes(9),
        name="attention_out",
    )(scal, *heads, vecs, x_all, w_out, near, away)


def up_pairs(scal, pieces, w_up, held):
    own, from_x, from_y, far_a, far_b = pieces
    groups = [[] for _ in range(4)]
    for k in range(3):
        base = scal[SHARD + 1 + k] * 256
        for m, piece in enumerate((own, from_x, from_y)):
            target = held.at[scal[CHIP] ^ m, aligned(base, 256)]
            groups[m].append((piece.at[k, :, 0:512], target))
        for half, piece in enumerate((far_a, far_b)):
            target = held.at[scal[CHIP] ^ 3, aligned(base + 128 * half, 128)]
            groups[3].append((piece.at[k, :, 0:512], target))
    rows = aligned(scal[SHARD] * 256, 256)
    for m in range(4):
        chip = scal[CHIP] ^ m
        for k in range(4):
            columns = aligned(k * D + (scal[CORE] * 4 + chip) * 128, 128)
            target = held.at[chip, rows, 128 * k : 128 * (k + 1)]
            groups[m].append((w_up.at[:, columns], target))
    return groups


UP_COPIES = 3 * 7 + 10


def grouped_copies(groups, sems, base=0):
    result = []
    for group in groups:
        result.append(copies_of(group, sems, base))
        base += len(group)
    return result


def down_pairs(scal, own, from_y, from_x, held):
    side = scal[CHIP] % 2
    pairs = []
    for f in range(4):
        rows = slice(128 * f, 128 * (f + 1))
        pairs.append((own.at[f, 0], held.at[scal[TOP], rows]))
        pairs.append((own.at[f, 1], held.at[2 + side, rows]))
        pairs.append((from_y.at[f], held.at[1 - scal[TOP], rows]))
        pairs.append((from_x.at[f], held.at[3 - side, rows]))
    return pairs


DOWN_COPIES = 16


def up_kernel(scal, y1_low, up_bias, w_up, *rest):
    pieces, (act, slope, held, act_held, slope_held, sems, out_sems) = rest[:5], rest[5:]
    groups = grouped_copies(up_pairs(scal, pieces, w_up, held), sems)
    for group in groups:
        start_all(group)
    outs = []
    for m, group in enumerate(groups):
        wait_all(group)
        q = scal[CHIP] ^ m
        bias = up_bias[pl.ds(scal[CORE] * 4 + q, 1), :]
        for r in (slice(0, 256), slice(256, 512)):
            u = contract(y1_low[r, :], held[q], 1, 0) + bias
            cdf = 0.5 * (1.0 + lax.erf(u * (1.0 / math.sqrt(2.0))))
            density = jnp.exp(-0.5 * u * u) * (1.0 / math.sqrt(2.0 * math.pi))
            slope_held[q, r, :] = (cdf + u * density).astype(BF)
            act_held[q, r, :] = (u * cdf).astype(BF)
        copies = copies_of(
            [(act_held.at[q], act.at[q]), (slope_held.at[q], slope.at[q])], out_sems, 2 * m
        )
        start_all(copies)
        outs += copies
    wait_all(outs)


def feed_up(scal, y1_low, up_bias, w_up, pieces):
    block = pltpu.VMEM((4, ROWS, 512), BF)
    return pl.pallas_call(
        up_kernel,
        out_shape=(struct((4, ROWS, 512), BF), struct((4, ROWS, 512), BF)),
        in_specs=[SMEM, VMEM, VMEM] + [HBM] * 6,
        out_specs=(HBM, HBM),
        scratch_shapes=[
            pltpu.VMEM((4, D, 512), BF),
            block,
            block,
            pltpu.SemaphoreType.DMA((UP_COPIES,)),
            pltpu.SemaphoreType.DMA((8,)),
        ],
        compiler_params=params(60),
        cost_estimate=takes(7),
        name="feed_up",
    )(scal, y1_low, up_bias, w_up, *pieces)


def down_kernel(scal, act, own, from_y, from_x, part, held, act_held, total, sems):
    pairs = down_pairs(scal, own, from_y, from_x, held)
    copies = copies_of(pairs, sems)
    acts = copies_of([(act.at[q], act_held.at[q]) for q in range(4)], sems, DOWN_COPIES)
    start_all(copies)
    start_all(acts)
    wait_all(copies)
    for q in range(4):
        acts[q].wait()
        moved = contract(act_held[q], held[q], 1, 0)
        if q == 0:
            total[...] = moved
        elif q < 3:
            total[...] += moved
        else:
            part[...] = (total[...] + moved).astype(part.dtype)


def feed_down(scal, act, pieces, dtype):
    return pl.pallas_call(
        down_kernel,
        out_shape=struct((ROWS, D), dtype),
        in_specs=[SMEM] + [HBM] * 4,
        out_specs=VMEM,
        scratch_shapes=[
            pltpu.VMEM((4, 512, D), BF),
            pltpu.VMEM((4, ROWS, 512), BF),
            pltpu.VMEM((ROWS, D), F32),
            pltpu.SemaphoreType.DMA((DOWN_COPIES + 4,)),
        ],
        compiler_params=params(60),
        cost_estimate=takes(5),
        name="feed_down",
    )(scal, act, *pieces)


def second_norm_kernel(y1, part, came, cot_own, cot_came, vecs, out_own, out_away, dh2, dz2, sums):
    n = pl.program_id(0)
    h2 = y1[...] + part[...] + came[...].astype(F32) + vecs[5:6]
    out, normed, inverse = norm_forward(h2, vecs[6:7], vecs[7:8])
    out = out.astype(BF)
    c = jnp.where(n < 2, cot_own[...], cot_came[...]).astype(F32)
    grad = norm_backward(c, normed, inverse, vecs[6:7])
    dh2[...] = grad
    low = grad.astype(BF)
    dz2[...] = low

    @pl.when(n == 0)
    def _():
        sums[...] = jnp.zeros_like(sums)

    for i, value in enumerate((c * normed, c, low.astype(F32))):
        sums[i : i + 1, :] += jnp.sum(value, 0, keepdims=True)

    @pl.when(n < 2)
    def _():
        out_own[...] = out

    @pl.when(n >= 2)
    def _():
        out_away[...] = out


def second_norm(y1, part, came, cot_own, cot_came, vecs):
    half = struct((ROWS // 2, D), BF)
    rows = pl.BlockSpec((128, D), lambda n: (n, 0))
    first = pl.BlockSpec((128, D), lambda n: (jnp.minimum(n, 1), 0))
    last = pl.BlockSpec((128, D), lambda n: (jnp.maximum(n - 2, 0), 0))
    whole = pl.BlockSpec((8, D), lambda n: (0, 0))
    return pl.pallas_call(
        second_norm_kernel,
        grid=(4,),
        out_shape=(half, half, struct((ROWS, D), F32), struct((ROWS, D), BF), struct((8, D), F32)),
        in_specs=[rows, rows, rows, first, last, whole],
        out_specs=(first, last, rows, rows, whole),
        compiler_params=params(60),
        cost_estimate=takes(4),
        name="second_norm",
    )(y1, part, came, cot_own, cot_came, vecs)


def back_kernel(scal, dz2_a, dz2_b, slope_a, slope_b, w_up, *rest):
    ups, downs, outs, scratch = rest[:5], rest[5:8], rest[8:13], rest[13:]
    du_a, du_b, part_a, part_b, up_sums = outs
    up_held, down_held, slopes, dus, acc_a, acc_b, sems, out_sems = scratch
    down_copies = copies_of(down_pairs(scal, *downs, down_held), sems)
    groups = grouped_copies(up_pairs(scal, ups, w_up, up_held), sems, DOWN_COPIES)
    loads = []
    for m in range(4):
        q = scal[CHIP] ^ m
        pairs = [(slope_b.at[q], slopes.at[1, q]), (slope_a.at[q], slopes.at[0, q])]
        loads.append(copies_of(pairs, sems, DOWN_COPIES + UP_COPIES + 2 * m))
    start_all(down_copies)
    for group, load in zip(groups, loads):
        start_all(load)
        start_all(group)
    wait_all(down_copies)
    sent = []
    for m in range(4):
        wait_all(loads[m])
        wait_all(groups[m])
        q = scal[CHIP] ^ m
        total = jnp.zeros((1, 512), F32)
        for side, (dz2, du, acc) in enumerate(((dz2_a, du_a, acc_a), (dz2_b, du_b, acc_b))):
            for r in (slice(0, 256), slice(256, 512)):
                low = contract(dz2[r, :], down_held[q], 1, 1) * slopes[side, q, r, :].astype(F32)
                low = low.astype(BF)
                dus[side, q, r, :] = low
                total = total + jnp.sum(low.astype(F32), 0, keepdims=True)
                moved = contract(low, up_held[q], 1, 1)
                if m == 0:
                    acc[r, :] = moved
                else:
                    acc[r, :] += moved
            copies = copies_of([(dus.at[side, q], du.at[q])], out_sems, 2 * m + side)
            start_all(copies)
            sent += copies
        up_sums[pl.ds(q, 1), :] = total
    part_a[...] = acc_a[...]
    part_b[...] = acc_b[...].astype(BF)
    wait_all(sent)


def feed_back(scal, dz2s, slopes, w_up, ups, downs):
    du = struct((4, ROWS, 512), BF)
    return pl.pallas_call(
        back_kernel,
        out_shape=(
            du, du, struct((ROWS, D), F32), struct((ROWS, D), BF), struct((8, 512), F32)
        ),
        in_specs=[SMEM, VMEM, VMEM] + [HBM] * 11,
        out_specs=(HBM, HBM, VMEM, VMEM, VMEM),
        scratch_shapes=[
            pltpu.VMEM((4, D, 512), BF),
            pltpu.VMEM((4, 512, D), BF),
            pltpu.VMEM((2, 4, ROWS, 512), BF),
            pltpu.VMEM((2, 4, ROWS, 512), BF),
            pltpu.VMEM((ROWS, D), F32),
            pltpu.VMEM((ROWS, D), F32),
            pltpu.SemaphoreType.DMA((DOWN_COPIES + UP_COPIES + 8,)),
            pltpu.SemaphoreType.DMA((8,)),
        ],
        compiler_params=params(60),
        cost_estimate=takes(22),
        name="feed_back",
    )(scal, *dz2s, *slopes, w_up, *ups, *downs)


def first_norm_kernel(
    scal, dh2, part, came, n1, r1, vecs, w_out, near, away, dao, g0, g1, g2, g3, sums, held, sems
):
    copies = copies_of(out_pairs(scal, near, away, w_out, held), sems)
    start_all(copies)
    dy1 = dh2[...] + part[...] + came[...].astype(F32)
    normed = n1[...]
    low = norm_backward(dy1, normed, r1[:, 0:1], vecs[3:4]).astype(BF)
    dao[...] = low
    sums[0:1, :] = jnp.sum(dy1 * normed, 0, keepdims=True)
    sums[1:2, :] = jnp.sum(dy1, 0, keepdims=True)
    sums[2:3, :] = jnp.sum(low.astype(F32), 0, keepdims=True)
    wait_all(copies)
    for k, out in enumerate((g0, g1, g2, g3)):
        rows = aligned((scal[LOW] ^ k) * 256, 256)
        total = 0.0
        for b in range(0, 8, 2):
            weight = jnp.concatenate([held[b, rows, :], held[b + 1, rows, :]], 1)
            total = total + contract(dao[:, b * 128 : (b + 2) * 128], weight, 1, 1)
        out[...] = total.astype(BF)


def first_norm(scal, dh2, part, came, n1, r1, vecs, w_out, near, away):
    return pl.pallas_call(
        first_norm_kernel,
        out_shape=(struct((ROWS, D), BF),) + (struct((ROWS, 256), BF),) * 4 + (struct((8, D), F32),),
        in_specs=[SMEM] + [VMEM] * 6 + [HBM] * 3,
        out_specs=(VMEM,) * 6,
        scratch_shapes=[pltpu.VMEM((8, D, 128), BF), pltpu.SemaphoreType.DMA((32,))],
        compiler_params=params(60),
        cost_estimate=takes(7),
        name="first_norm",
    )(scal, dh2, part, came, n1, r1, vecs, w_out, near, away)


def split_write(n, block, a_keep, a_send, b_keep, b_send):
    half = a_keep.shape[1]
    top_rows, low_rows = block[:half], block[half:]
    for step in range(4):

        @pl.when(n == step)
        def _():
            (a_send if step in (1, 3) else a_keep)[0] = top_rows
            (b_send if step in (2, 3) else b_keep)[0] = low_rows


def split_specs(rows, columns):
    half = (1, rows // 2, columns)
    return (
        pl.BlockSpec(half, lambda n, s: (n // 2, 0, 0)),
        pl.BlockSpec(half, lambda n, s: (n // 2, 0, 0)),
        pl.BlockSpec(half, lambda n, s: (jnp.minimum(n, 1), 0, 0)),
        pl.BlockSpec(half, lambda n, s: (jnp.maximum(n - 2, 0), 0, 0)),
    )


def split_shapes(rows, columns):
    return (struct((2, rows // 2, columns), BF),) * 4


def down_grad_kernel(scal, act_a, act_b, dz2_a, dz2_b, *outs):
    left = [jnp.concatenate([act[f] for f in range(4)], 1) for act in (act_a, act_b)]
    rows = contract(left[0], dz2_a[...], 0, 0) + contract(left[1], dz2_b[...], 0, 0)
    split_write(pl.program_id(0), rows.astype(BF), *outs)


def down_grad(scal, acts, dz2s):
    act_spec = pl.BlockSpec((4, ROWS, 128), lambda n, s: (0, 0, s[CHIP] ^ n))
    dz2_spec = pl.BlockSpec((ROWS, D), lambda n, s: (0, 0))
    return pl.pallas_call(
        down_grad_kernel,
        out_shape=split_shapes(512, D),
        grid_spec=pltpu.PrefetchScalarGridSpec(
            num_scalar_prefetch=1,
            grid=(4,),
            in_specs=[act_spec, act_spec, dz2_spec, dz2_spec],
            out_specs=split_specs(512, D),
        ),
        compiler_params=params(60),
        cost_estimate=takes(11),
        name="down_grad",
    )(scal, *acts, *dz2s)


OUT_WIDTH = 1024 + 128
UP_WIDTH = 4096 + 1024 + 128


def up_parts(y1_a, y1_b, du_a, du_b):
    return [
        contract(y1_a[...], du_a[q], 0, 0) + contract(y1_b[...], du_b[q], 0, 0) for q in range(4)
    ]


def up_grad_other_kernel(scal, y1_a, y1_b, du_a, du_b, out, left):
    @pl.when(pl.program_id(0) == 0)
    def _():
        for side, y1 in enumerate((y1_a, y1_b)):
            for n in range(4):
                row = 2 * (scal[CHIP] ^ n) + 1 - scal[CORE]
                left[side, :, 128 * n : 128 * (n + 1)] = y1[:, aligned(row * 128, 128)]

    rows = contract(left[0], du_a[0], 0, 0) + contract(left[1], du_b[0], 0, 0)
    for n in range(4):
        out[n] = rows[128 * n : 128 * (n + 1)].astype(BF)


def out_grad_other_kernel(scal, heads, dao, small, out):
    parts = [contract(heads[0], dao[...], 0, 0), small[0]]
    out[0] = jnp.concatenate(parts, 1).astype(BF)


def up_grad_own_kernel(scal, y1_a, y1_b, du_a, du_b, heads, dao, small, came, came_out, *rest):
    outs, block = rest[:4], rest[4]
    core = scal[CORE]
    own = jnp.concatenate(up_parts(y1_a, y1_b, du_a, du_b), 1).astype(BF)
    block[:, aligned(core * 2048, 2048)] = own
    block[:, aligned((1 - core) * 2048, 2048)] = came[0]
    out_rows = contract(heads[0], dao[...], 0, 0) + came_out[0, :, :1024].astype(F32)
    block[:, 4096:5120] = out_rows.astype(BF)
    block[:, 5120:] = (small[0] + came_out[0, :, 1024:].astype(F32)).astype(BF)
    split_write(pl.program_id(0), block, *outs)


def of_row(index, flip):
    return lambda n, s: index(s[CHIP] ^ n, s[CORE] ^ flip, s)


def up_specs(flip):
    y1_spec = pl.BlockSpec((ROWS, 128), of_row(lambda q, c, s: (0, 2 * q + c), flip))
    du_spec = pl.BlockSpec((4, ROWS, 512), lambda n, s: (0, 0, 0))
    return [y1_spec, y1_spec, du_spec, du_spec]


def out_specs(flip):
    return [
        pl.BlockSpec((1, ROWS, 128), of_row(lambda q, c, s: (q ^ s[LOW], 0, c), flip)),
        pl.BlockSpec((ROWS, D), lambda n, s: (0, 0)),
        pl.BlockSpec((1, 128, 128), of_row(lambda q, c, s: (2 * q + c, 0, 0), flip)),
    ]


UP_SENT = pl.BlockSpec((1, 128, 2048), lambda n, s: (n, 0, 0))
OUT_SENT = pl.BlockSpec((1, 128, OUT_WIDTH), lambda n, s: (n, 0, 0))


def up_grad_other(scal, y1s, dus):
    y1_spec = pl.BlockSpec((ROWS, D), lambda q, s: (0, 0))
    du_spec = pl.BlockSpec((1, ROWS, 512), lambda q, s: (q, 0, 0))
    return pl.pallas_call(
        up_grad_other_kernel,
        out_shape=struct((4, 128, 2048), BF),
        grid_spec=pltpu.PrefetchScalarGridSpec(
            num_scalar_prefetch=1,
            grid=(4,),
            in_specs=[y1_spec, y1_spec, du_spec, du_spec],
            out_specs=pl.BlockSpec((4, 128, 512), lambda q, s: (0, 0, q)),
            scratch_shapes=[pltpu.VMEM((2, ROWS, 512), BF)],
        ),
        compiler_params=params(60),
        cost_estimate=takes(6),
        name="up_grad_other",
    )(scal, *y1s, *dus)


def out_grad_other(scal, heads, dao, small):
    return pl.pallas_call(
        out_grad_other_kernel,
        out_shape=struct((4, 128, OUT_WIDTH), BF),
        grid_spec=pltpu.PrefetchScalarGridSpec(
            num_scalar_prefetch=1, grid=(4,), in_specs=out_specs(1), out_specs=OUT_SENT
        ),
        compiler_params=params(60),
        cost_estimate=takes(3),
        name="out_grad_other",
    )(scal, heads, dao, small)


def up_grad_own(scal, y1s, dus, heads, dao, small, came, came_out):
    return pl.pallas_call(
        up_grad_own_kernel,
        out_shape=split_shapes(128, UP_WIDTH),
        grid_spec=pltpu.PrefetchScalarGridSpec(
            num_scalar_prefetch=1,
            grid=(4,),
            in_specs=up_specs(0) + out_specs(0) + [UP_SENT, OUT_SENT],
            out_specs=split_specs(128, UP_WIDTH),
            scratch_shapes=[pltpu.VMEM((128, UP_WIDTH), BF)],
        ),
        compiler_params=params(60),
        cost_estimate=takes(10),
        name="up_grad_own",
    )(scal, *y1s, *dus, heads, dao, small, came, came_out)


def qkv_grad_kernel(scal, x, dqkv, out, acc, sums, *, half):
    n = pl.program_id(0)
    ones = jnp.ones((dqkv.shape[0], 128), BF)
    rows = contract(x[...], dqkv[...], 0, 0)
    q_sum = contract(dqkv[:, 0:128], ones, 0, 0)
    v_sum = contract(dqkv[:, 256:384], ones, 0, 0)

    @pl.when(n == 0)
    def _():
        acc[...] = rows
        sums[0] = q_sum
        sums[1] = v_sum

    @pl.when(n > 0)
    def _():
        acc[...] += rows
        sums[0] += q_sum
        sums[1] += v_sum

    @pl.when(n == 3)
    def _():
        lane = lax.broadcasted_iota(jnp.int32, (128, 128), 1)
        extra = jnp.where(lane == 0, sums[0], jnp.where(lane == 1, sums[1], 0.0))
        for r in range(8):
            here = jnp.where(2 * scal[LOW] + half == r, 1.0, 0.0)
            block = jnp.concatenate(
                [acc[128 * r : 128 * (r + 1), :], extra * here], 1
            ).astype(BF)
            for f in range(4):
                out[r // 4, f, r % 4] = block[32 * f : 32 * (f + 1), :]


def qkv_grad(scal, x_all, dqkv, half, cost):
    total = x_all.shape[0]
    part = total // 4
    return pl.pallas_call(
        partial(qkv_grad_kernel, half=half),
        out_shape=struct((2, 4, 4, 32, 512), BF),
        grid_spec=pltpu.PrefetchScalarGridSpec(
            num_scalar_prefetch=1,
            grid=(4,),
            in_specs=[
                pl.BlockSpec((part, D), lambda n, s: (n, 0)),
                pl.BlockSpec((part, 384), lambda n, s: (n, 0)),
            ],
            out_specs=pl.BlockSpec((2, 4, 4, 32, 512), lambda n, s: (0, 0, 0, 0, 0)),
            scratch_shapes=[pltpu.VMEM((D, 384), F32), pltpu.VMEM((2, 128, 128), F32)],
        ),
        compiler_params=params(60),
        cost_estimate=takes(cost),
        name="qkv_grad",
    )(scal, x_all, dqkv)


def input_grad_kernel(scal, dqkv_a, dqkv_b, weight, dao, away, near):
    n = pl.program_id(0)
    held = (n + 4) % 8
    joined = jnp.concatenate(
        [dqkv[:, 128 * k : 128 * (k + 1)] for k in range(3) for dqkv in (dqkv_a, dqkv_b)], 1
    )
    total = contract(joined, weight[...], 1, 1)
    turn = (held // 4) + 2 * ((held // 2) % 2) + 4 * (held % 2)
    parts = []
    for e in range(2):
        place = scal[INVERSE + 2 * (scal[ME] ^ turn) + e]
        other = (place // 2) ^ scal[ME]
        mine = jnp.where((other == 0) | (other == 4), 1.0, 0.0)
        source = aligned(((other // 4) % 2) * 256 + (place % 2) * BLK, BLK)
        rows = total[BLK * e : BLK * (e + 1)]
        parts.append((rows + dao[source, :].astype(F32) * mine).astype(BF))
    result = jnp.concatenate(parts, 0)

    @pl.when(n < 4)
    def _():
        away[0] = result

    @pl.when(n >= 4)
    def _():
        near[0] = result


def input_grad(scal, dqkv_a, dqkv_b, weight, dao):
    rows = pl.BlockSpec((256, 384), lambda n, s: ((n + 4) % 8, 0))
    return pl.pallas_call(
        input_grad_kernel,
        out_shape=(struct((4, 256, D), BF),) * 2,
        grid_spec=pltpu.PrefetchScalarGridSpec(
            num_scalar_prefetch=1,
            grid=(8,),
            in_specs=[
                rows,
                rows,
                pl.BlockSpec((D, 768), lambda n, s: (0, 0)),
                pl.BlockSpec((ROWS, D), lambda n, s: (0, 0)),
            ],
            out_specs=(
                pl.BlockSpec((1, 256, D), lambda n, s: (jnp.minimum(n, 3), 0, 0)),
                pl.BlockSpec((1, 256, D), lambda n, s: (jnp.maximum(n - 4, 0), 0, 0)),
            ),
        ),
        compiler_params=params(60),
        cost_estimate=takes(7),
        name="input_grad",
    )(scal, dqkv_a, dqkv_b, weight, dao)


def after(value, *others):
    return lax.optimization_barrier((value,) + others)[0]


def tied(*values):
    return lax.optimization_barrier(values)


def add_low(a, b):
    return (a.astype(F32) + b.astype(F32)).astype(BF)


def add_far(a_keep, b_keep, a_came, b_came):
    return hop(add_low(a_keep[1], a_came[1]), 4), hop(add_low(b_keep[1], b_came[1]), 2)


def own_rows_of(a_keep, b_keep, a_came, b_came, a_next, b_next):
    a_all = a_keep[0].astype(F32) + a_came[0].astype(F32) + a_next.astype(F32)
    b_all = b_keep[0].astype(F32) + b_came[0].astype(F32) + b_next.astype(F32)
    both = jnp.concatenate([a_all, b_all], 0).astype(BF)
    return lax.psum_scatter(both, "fsdp", scatter_dimension=0, tiled=True)


def tiled_device(
    tokens, cotangent, lengths, order, w_qkv, w_out, w_up, w_down, q_bias, v_bias, out_bias,
    norm1_gain, norm1_bias, up_bias, down_bias, norm2_gain, norm2_bias,
):
    me = lax.axis_index("ctx")
    core, low, top = me % 2, me % 4, me // 4
    chunk = tokens.shape[2]
    half_groups = [[0, 1, 2, 3], [4, 5, 6, 7]]
    scal = scalars(order, lengths)
    small = jnp.zeros((16, 256), BF)
    row = lax.broadcasted_iota(jnp.int32, (16, 256), 0)
    rows_of_small = [
        q_bias, v_bias, out_bias, norm1_gain, norm1_bias, down_bias, norm2_gain, norm2_bias,
    ] + [up_bias[256 * k : 256 * (k + 1)] for k in range(4)]
    for k, vector in enumerate(rows_of_small):
        small = jnp.where(row == k, vector[None, :], small)
    own_rows, other_rows, cot_own, cot_other, pack, pack_sent, up_slice, down_slice = carve(
        tokens, cotangent, w_qkv, w_out, w_up, w_down, small
    )

    def around(value):
        return [
            lax.ppermute(value, "fsdp", [(i, (i + k) % 4) for i in range(4)]) for k in (1, 2, 3)
        ]

    *pack_near, from_y = tied(*around(pack_sent), hop(other_rows, 4))
    pack_near = jnp.stack(pack_near)
    from_x, pack_away = tied(hop(jnp.stack([own_rows, from_y]), 2), hop(pack_near, 4))
    up_own = lax.all_gather(after(up_slice, from_y), "fsdp", axis=0)
    core_own = hop(own_rows, 1)
    core_rest = hop(jnp.concatenate([from_y[None], from_x], 0), 1)
    down_own = lax.all_gather(after(down_slice, from_x), "fsdp", axis=0)
    qkv, x_all, qkv_weight, vecs, up_b = project(
        scal, pack, small, pack_near, pack_away,
        (own_rows, from_y, from_x, core_own, core_rest),
    )
    up_own, qkv = tied(up_own, qkv)
    foreign = jnp.stack(
        [lax.dynamic_index_in_dim(up_own, scal[SHARD + k], 0, False) for k in (1, 2, 3)]
    )
    up_x, up_y = hop(foreign, 2), hop(foreign, 4)
    *sent, turned, lse = attention_forward(scal, after(qkv, foreign), chunk)
    up_x, up_y, *sent = tied(up_x, up_y, *sent)
    far_a, far_b, *far_heads = tied(
        hop(up_y[:, :128], 2), hop(up_x[:, 128:], 4), hop(sent[2], 2), hop(sent[3], 3)
    )
    heads = [sent[0], hop(sent[1], 1), *far_heads]
    ups = (foreign, up_x, up_y, far_a, far_b)
    near = jnp.stack(
        [piece[:, :, 512:] for piece in (foreign, up_x, up_y)]
        + [jnp.concatenate([far_a[:, :, 512:], far_b[:, :, 512:]], 1)]
    )
    away = hop(near, 1)
    down_own = after(down_own, far_a, far_b)
    down_y, down_x = hop(down_own[:, 0], 4), hop(down_own[:, 1], 2)

    y1, y1_low, n1, r1 = attention_out(scal, heads, vecs, x_all, w_out, near, away)

    y1_away = hop(y1_low, 1)
    act, slope = feed_up(scal, y1_low, up_b, w_up, ups)
    act, slope, y1_away = tied(act, slope, y1_away)
    act_away, slope_away = feed_up(scal, y1_away, up_b, w_up, ups)
    act_away, slope_away, down_x, down_y = tied(act_away, slope_away, down_x, down_y)
    downs = (down_own, down_y, down_x)
    part_away = hop(feed_down(scal, act_away, downs, BF), 1)
    cot_came = hop(after(cot_other, act_away), 4)
    part = feed_down(scal, act, downs, F32)
    part, part_away, cot_came = tied(part, part_away, cot_came)
    out_own, out_away, dh2, dz2, sums2 = second_norm(y1, part, part_away, cot_own, cot_came, vecs)
    dz2_away = hop(dz2, 1)
    mixed_came = hop(out_away, 4)
    mixed = jnp.where(
        top == 0, jnp.stack([out_own, mixed_came]), jnp.stack([mixed_came, out_own])
    )[:, None]

    dak, das, dbk, dbs = down_grad(scal, (act, act_away), (dz2, dz2_away))
    da_came, db_came = hop(das, 2), hop(dbs, 4)
    du, du_away, part, part_away, up_sums = feed_back(
        scal, (dz2, after(dz2_away, dak)), (slope, slope_away), w_up, ups, downs
    )
    part, du, du_away, up_sums, part_away, da_came, db_came = tied(
        part, du, du_away, up_sums, part_away, da_came, db_came
    )
    part_away = hop(part_away, 1)
    y1s, dus = (y1_low, y1_away), (du, du_away)
    up_other = up_grad_other(scal, y1s, dus)
    up_other, part_away = tied(up_other, part_away)
    dao, *dattn, sums1 = first_norm(
        scal, dh2, part, part_away, n1, r1, vecs, w_out, near, away
    )
    dattn = [dattn[0]] + [hop(dattn[k], k) for k in (1, 2, 3)]
    up_came = hop(up_other, 1)

    def per_owner(vector):
        return vector.reshape(8, 4, 32)

    unit_sums = up_sums[:4].reshape(4, 4, 128).transpose(1, 0, 2)
    mine = (jnp.arange(2) == core)[None, :, None, None]
    up_owner = jnp.where(mine, unit_sums[:, None], 0.0).reshape(8, 4, 128)
    vec_block = jnp.concatenate(
        [per_owner(sums1[2]), per_owner(sums1[0]), per_owner(sums1[1]), per_owner(sums2[2]),
         per_owner(sums2[0]), per_owner(sums2[1]), up_owner, jnp.zeros((8, 4, 64), F32)], 2
    ).reshape(8, 4, 3, 128)
    vec_block = jnp.concatenate([vec_block, jnp.zeros((8, 4, 29, 128), F32)], 2).reshape(
        8, 128, 128
    )
    all_heads = jnp.stack(heads)
    out_other = out_grad_other(scal, all_heads, dao, vec_block)
    uak, uas, ubk, ubs = up_grad_own(
        scal, y1s, dus, all_heads, dao, vec_block, up_came, hop(out_other, 1)
    )
    uak, uas, ubk, ubs, *dattn = tied(uak, uas, ubk, ubs, *dattn)
    ua_came, ub_came = hop(uas, 2), hop(ubs, 4)
    da_next, db_next = add_far(dak, dbk, da_came, db_came)
    dqkv_a = attention_backward(
        scal, after(qkv, uak), dattn, turned, lse, chunk, 0, 2
    )
    da_next, db_next, dqkv_a = tied(da_next, db_next, dqkv_a)
    down_rows = own_rows_of(dak, dbk, da_came, db_came, da_next, db_next)
    grad_a = qkv_grad(scal, x_all, dqkv_a, 0, 0.05)
    ua_came, ub_came, grad_a = tied(ua_came, ub_came, grad_a)
    ua_next, ub_next = add_far(uak, ubk, ua_came, ub_came)

    def to_owners(grad):
        groups = [[4 * ctx + f for ctx in (k, k + 4) for f in range(4)] for k in range(4)]
        return lax.all_to_all(
            grad.reshape(8, 4, 32, 512), ("ctx", "fsdp"), 0, 0, tiled=True,
            axis_index_groups=groups,
        )

    grad_a = to_owners(grad_a)
    dqkv_b = attention_backward(
        scal, after(qkv, dqkv_a, ua_came), dattn, turned, lse, chunk, 2, 2
    )
    ua_next, ub_next, grad_a, dqkv_b = tied(ua_next, ub_next, grad_a, dqkv_b)
    up_rows = own_rows_of(uak, ubk, ua_came, ub_came, ua_next, ub_next).astype(F32)

    dx_away, dx = input_grad(scal, dqkv_a, dqkv_b, qkv_weight, dao)
    grad_b = qkv_grad(scal, x_all, after(dqkv_b, dx_away), 1, 6)
    grad_b, dx_came = tied(grad_b, hop(dx_away, 1))
    dx = add_low(dx, dx_came)
    far_rows, own_rows = hop(dx[3], 2), hop(dx[2], 2)
    grad_b = to_owners(grad_b)
    grad_far = add_low(dx[1], far_rows)
    grad_came = hop(grad_far, 4)
    grad_b = after(grad_b, grad_far)
    grad_own = add_low(dx[0], after(own_rows, grad_far))
    tokens_grad = jnp.where(
        top == 0, jnp.stack([grad_own, grad_came]), jnp.stack([grad_came, grad_own])
    )[:, None]
    mine = [jnp.sum(parts.astype(F32), 0).astype(BF) for parts in (grad_a, grad_b)]
    mine = lax.all_to_all(
        jnp.concatenate(mine, 2), "ctx", 0, 0, tiled=True, axis_index_groups=half_groups
    ).astype(F32)
    mine = mine.reshape(4, 32, 2, 4, 128)
    w_qkv_grad = mine[:, :, :, :3].transpose(1, 3, 0, 2, 4).reshape(32, 3072)
    q_bias_grad = jnp.sum(mine[:, :, :, 3, 0], (0, 2))
    v_bias_grad = jnp.sum(mine[:, :, :, 3, 1], (0, 2))

    w_up_grad = (
        up_rows[:, :4096].reshape(32, 8, 4, 128).transpose(0, 2, 1, 3).reshape(32, 4096)
    )
    w_out_grad = up_rows[:, 4096:5120]
    sums = up_rows[:3, 5120:].reshape(384)
    return (
        mixed, tokens_grad, w_qkv_grad, w_out_grad, w_up_grad, down_rows.astype(F32), q_bias_grad, v_bias_grad,
        sums[0:32], sums[32:64], sums[64:96], sums[192:320], sums[96:128], sums[128:160],
        sums[160:192],
    )


def pick_blocks(wanted, rows):
    shaped = rows.reshape(-1, BLK, rows.shape[-1])
    picked = [
        lax.dynamic_index_in_dim(shaped, wanted[e], 0, False) for e in range(wanted.shape[0])
    ]
    return jnp.concatenate(picked, 0)


def plain_device(
    tokens, cotangent, lengths, order, w_qkv, w_out, w_up, w_down, q_bias, v_bias, out_bias,
    norm1_gain, norm1_bias, up_bias, down_bias, norm2_gain, norm2_bias,
):
    shards = (
        w_qkv, w_out, w_up, w_down, q_bias, v_bias, out_bias, norm1_gain, norm1_bias, up_bias,
        down_bias, norm2_gain, norm2_bias,
    )
    me = lax.axis_index("ctx")
    count = lax.axis_size("ctx")
    rows = tokens.shape[2]
    per_device = rows // BLK
    whole_rows = rows * count
    scaling = 1.0 / math.sqrt(HD)
    (
        qkv_full, out_full, up_full, down_full, qbias_full, vbias_full, obias_full, gain_one,
        shift_one, ubias_full, dbias_full, gain_two, shift_two,
    ) = tuple(lax.all_gather(shard, "fsdp", axis=0, tiled=True) for shard in shards)
    full_bias = jnp.concatenate([qbias_full, jnp.zeros_like(qbias_full), vbias_full]).astype(F32)
    gain_one, shift_one, gain_two, shift_two = (
        vector.astype(F32) for vector in (gain_one, shift_one, gain_two, shift_two)
    )
    positions = jnp.arange(whole_rows, dtype=jnp.int32)
    mixed_list, grad_list, totals = [], [], None
    for micro in range(tokens.shape[0]):
        order_row = order[micro, 0]
        bound = lengths[micro, 0, 0]
        segment_all = (positions >= bound).astype(jnp.int32)
        segment_query = (me * rows + jnp.arange(rows, dtype=jnp.int32) >= bound).astype(jnp.int32)
        dealt = me * per_device + jnp.arange(per_device, dtype=jnp.int32)
        blocks = jnp.arange(order_row.shape[0], dtype=jnp.int32)
        inverse = jnp.sum(jnp.where(order_row[None, :] == dealt[:, None], blocks[None, :], 0), 1)
        forward = jnp.sum(jnp.where(blocks[None, :] == dealt[:, None], order_row[None, :], 0), 1)
        token_rows = tokens[micro, 0]
        cot_rows = pick_blocks(
            inverse, lax.all_gather(cotangent[micro, 0], "ctx", axis=0, tiled=True)
        ).astype(F32)
        qkv_rows = (jnp.dot(token_rows, qkv_full, preferred_element_type=F32) + full_bias).astype(BF)
        queries = qkv_rows[:, :D].reshape(rows, H, HD)
        keys_values = lax.all_gather(qkv_rows[:, D:], "ctx", axis=0, tiled=True)
        keys = keys_values[:, :D].reshape(whole_rows, H, HD)
        values = keys_values[:, D:].reshape(whole_rows, H, HD)
        allowed = (segment_query[:, None] == segment_all[None, :])[None]
        scores = jnp.einsum("rhd,khd->hrk", queries, keys, preferred_element_type=F32) * scaling
        scores = jnp.where(allowed, scores, NEGATIVE)
        expos = jnp.where(allowed, jnp.exp(scores - jnp.max(scores, -1, keepdims=True)), 0.0)
        probs = expos / jnp.sum(expos, -1, keepdims=True)
        probs_low = probs.astype(BF)
        attn_float = jnp.einsum("hrk,khd->rhd", probs_low, values, preferred_element_type=F32)
        attn_low = attn_float.reshape(rows, D).astype(BF)
        first_in = (
            token_rows.astype(F32)
            + jnp.dot(attn_low, out_full, preferred_element_type=F32)
            + obias_full.astype(F32)
        )
        first_out, normed_one, inverse_one = norm_forward(first_in, gain_one, shift_one)
        first_low = first_out.astype(BF)
        hidden_in = jnp.dot(first_low, up_full, preferred_element_type=F32) + ubias_full.astype(F32)
        activated, gelu_back = jax.vjp(partial(jax.nn.gelu, approximate=False), hidden_in)
        act_low = activated.astype(BF)
        second_in = (
            first_out
            + jnp.dot(act_low, down_full, preferred_element_type=F32)
            + dbias_full.astype(F32)
        )
        second_out, normed_two, inverse_two = norm_forward(second_in, gain_two, shift_two)
        out_all = lax.all_gather(second_out.astype(BF), "ctx", axis=0, tiled=True)
        mixed_list.append(pick_blocks(forward, out_all))

        grad_second = norm_backward(cot_rows, normed_two, inverse_two, gain_two)
        grad_down_low = grad_second.astype(BF)
        (grad_hidden,) = gelu_back(contract(grad_down_low, down_full, 1, 1))
        grad_hidden_low = grad_hidden.astype(BF)
        grad_first = grad_second + contract(grad_hidden_low, up_full, 1, 1)
        grad_first_in = norm_backward(grad_first, normed_one, inverse_one, gain_one)
        grad_branch = grad_first_in.astype(BF)
        grad_attn = contract(grad_branch, out_full, 1, 1).astype(BF).reshape(rows, H, HD)
        grad_probs = jnp.einsum("rhd,khd->hrk", grad_attn, values, preferred_element_type=F32)
        delta = jnp.sum(probs * grad_probs, -1, keepdims=True)
        grad_scores = (probs * (grad_probs - delta) * scaling).astype(BF)
        grad_query = jnp.einsum("hrk,khd->rhd", grad_scores, keys, preferred_element_type=F32)
        grad_keys = jnp.einsum("hrk,rhd->khd", grad_scores, queries, preferred_element_type=F32)
        grad_values = jnp.einsum("hrk,rhd->khd", probs_low, grad_attn, preferred_element_type=F32)
        both = jnp.concatenate(
            [grad_keys.reshape(whole_rows, D), grad_values.reshape(whole_rows, D)], 1
        )
        both = lax.psum_scatter(both, "ctx", scatter_dimension=0, tiled=True)
        grad_qkv = jnp.concatenate([grad_query.reshape(rows, D), both], 1).astype(BF)
        column_sums = jnp.sum(grad_qkv.astype(F32), 0)
        grad_list.append((grad_first_in + contract(grad_qkv, qkv_full, 1, 1)).astype(BF))
        parts = (
            contract(token_rows, grad_qkv, 0, 0),
            contract(attn_low, grad_branch, 0, 0),
            contract(first_low, grad_hidden_low, 0, 0),
            contract(act_low, grad_down_low, 0, 0),
            column_sums[:D],
            column_sums[2 * D :],
            jnp.sum(grad_branch.astype(F32), 0),
            jnp.sum(grad_first * normed_one, 0),
            jnp.sum(grad_first, 0),
            jnp.sum(grad_hidden_low.astype(F32), 0),
            jnp.sum(grad_down_low.astype(F32), 0),
            jnp.sum(cot_rows * normed_two, 0),
            jnp.sum(cot_rows, 0),
        )
        totals = parts if totals is None else tuple(a + b for a, b in zip(totals, parts))
    shares = tuple(
        lax.psum_scatter(part, ("ctx", "fsdp"), scatter_dimension=0, tiled=True) for part in totals
    )
    return (jnp.stack(mixed_list)[:, None], jnp.stack(grad_list)[:, None]) + shares


def solution(mesh):
    fits = mesh.shape["ctx"] == 8 and mesh.shape["fsdp"] == 4
    weights = (P("fsdp", None),) * 4 + (P("fsdp"),) * 9
    owners = (P(("ctx", "fsdp"), None),) * 4 + (P(("ctx", "fsdp")),) * 9
    rows = P(None, "fsdp", "ctx", None)
    return jax.shard_map(
        tiled_device if fits else plain_device,
        mesh=mesh,
        in_specs=(rows, rows, P(None, "fsdp", None), P(None, "fsdp", None)) + weights,
        out_specs=(rows, rows) + owners,
        check_vma=False,
    )
```

```python
from functools import partial
import math

import jax
import jax.numpy as jnp
from jax import lax
from jax.experimental import pallas as pl
from jax.experimental.pallas import tpu as pltpu
from jax.sharding import PartitionSpec as P

D = 1024
H = 16
HD = 64
BLK = 128
MB = 2

NEGATIVE = -1e30
EPSILON = 1e-05
BF = jnp.bfloat16
F32 = jnp.float32


def contract(a, b, ca, cb):
    return lax.dot_general(a, b, (((ca,), (cb,)), ((), ())), preferred_element_type=F32)


def norm_forward(values_in, gain_vec, shift_vec):
    center = values_in - jnp.mean(values_in, -1, keepdims=True)
    inverse = lax.rsqrt(jnp.mean(center * center, -1, keepdims=True) + EPSILON)
    normed = center * inverse
    return (normed * gain_vec + shift_vec, normed, inverse)


def norm_backward(grad_out, normed, inverse, gain_vec):
    grad_norm = grad_out * gain_vec
    return inverse * (
        grad_norm
        - jnp.mean(grad_norm, -1, keepdims=True)
        - normed * jnp.mean(grad_norm * normed, -1, keepdims=True)
    )


def hop(value, mask):
    count = lax.axis_size("ctx")
    return lax.ppermute(value, "ctx", [(i, i ^ mask) for i in range(count)])


VMEM = pl.BlockSpec(memory_space=pltpu.VMEM)
SMEM = pl.BlockSpec(memory_space=pltpu.SMEM)
HBM = pl.BlockSpec(memory_space=pltpu.HBM)


def takes(microseconds):
    return pl.CostEstimate(
        flops=int(microseconds * 1.15e9), bytes_accessed=1 << 20, transcendentals=0
    )


def params(mib):
    return pltpu.CompilerParams(vmem_limit_bytes=mib << 20)


def struct(shape, dtype):
    return jax.ShapeDtypeStruct(shape, dtype)


ME, LOW, TOP, SHARD, CORE, CHIP, SPLIT, ORDER, INVERSE = 0, 1, 2, 3, 7, 8, 9, 10, 26
CHUNKS = (0, 4, 2, 6, 1, 5, 3, 7)
ROWS = 512


def scalars(order, lengths):
    me = lax.axis_index("ctx")
    shard = lax.axis_index("fsdp")
    core, low, top = me % 2, me % 4, me // 4
    order_row = jnp.where(top == 0, order[0, 0], order[1, 0])
    first = jnp.where(top == 0, lengths[0, 0, 0], lengths[1, 0, 0])
    blocks = jnp.arange(16, dtype=jnp.int32)
    inverse = jnp.sum(jnp.where(order_row[None, :] == blocks[:, None], blocks[None, :], 0), 1)
    others = [(shard + 4 - k) % 4 for k in (1, 2, 3)]
    return jnp.concatenate(
        [jnp.stack([me, low, top, shard, *others, core, me // 2, first]), order_row, inverse]
    ).astype(jnp.int32)


def start_all(copies):
    for copy in copies:
        copy.start()


def wait_all(copies):
    for copy in copies:
        copy.wait()


def copies_of(pairs, sems, base=0):
    return [
        pltpu.make_async_copy(a, b, sems.at[base + i]) for i, (a, b) in enumerate(pairs)
    ]


def aligned(start, size):
    return pl.ds(pl.multiple_of(start, size), size)


def segment_lanes(first, rows, split, is_query):
    position = first + lax.broadcasted_iota(jnp.int32, (rows, HD), 0)
    lane = lax.broadcasted_iota(jnp.int32, (rows, HD), 1)
    second = (position >= split).astype(jnp.int32)
    if is_query:
        return jnp.where(lane == 1 - second, NEGATIVE, 0.0).astype(BF)
    return jnp.where(lane == second, 1.0, 0.0).astype(BF)


def key_range(q0, bq, split, bk, total):
    begin = jnp.where(q0 >= split, split // bk, 0)
    end = jnp.where(q0 + bq <= split, (split + bk - 1) // bk, total // bk)
    return begin, end


def widen(scal, qkv, qa, ka, begin, heads, chunk):
    total = qkv.shape[0]
    width = qkv.shape[1] // 3
    split = scal[SPLIT]
    for m in range(total // chunk):
        pos = pl.multiple_of((scal[ME] ^ CHUNKS[m]) * chunk, chunk)
        rows = slice(m * chunk, (m + 1) * chunk)
        qtail = segment_lanes(pos, chunk, split, True)
        ktail = segment_lanes(pos, chunk, split, False)
        for h in range(heads):
            at = begin + h * HD
            q = qkv[rows, at : at + HD]
            k = qkv[rows, width + at : width + at + HD]
            q = (q.astype(F32) * 0.125).astype(BF)
            qa[h, pl.ds(pos, chunk), :] = jnp.concatenate([q, qtail], 1)
            ka[h, pl.ds(pos, chunk), :] = jnp.concatenate([k, ktail], 1)


def attention_forward_kernel(
    scal, qkv, out0, out1, out2, out3, out_t, lse, qa, ka, vt, sc, out, *, heads, chunk, bq, bk
):
    total = qkv.shape[0]
    width = qkv.shape[1] // 3
    split = scal[SPLIT]
    widen(scal, qkv, qa, ka, 0, heads, chunk)
    for m in range(total // chunk):
        pos = pl.multiple_of((scal[ME] ^ CHUNKS[m]) * chunk, chunk)
        rows = slice(m * chunk, (m + 1) * chunk)
        vt[:, pl.ds(pos, chunk)] = qkv[rows, 2 * width :].T

    def q_step(qi, _):
        q0 = pl.multiple_of(qi * bq, bq)
        begin_k, end_k = key_range(q0, bq, split, bk, total)

        def max_step(ki, carry):
            k0 = pl.multiple_of(ki * bk, bk)
            result = []
            for h in range(heads):
                st = contract(ka[h, pl.ds(k0, bk), :], qa[h, pl.ds(q0, bq), :], 1, 1)
                sc[h, pl.ds(k0, bk), :] = st
                result.append(jnp.maximum(carry[h], jnp.max(st.reshape(bk // 8, 8, bq), 0)))
            return tuple(result)

        start = tuple(jnp.full((8, bq), NEGATIVE, F32) for _ in range(heads))
        peaks = lax.fori_loop(begin_k, end_k, max_step, start)
        peaks = [jnp.max(m, 0, keepdims=True) for m in peaks]

        def k_step(ki, carry):
            k0 = pl.multiple_of(ki * bk, bk)
            result = []
            for h in range(heads):
                total_p, acc = carry[2 * h : 2 * h + 2]
                p = jnp.exp(sc[h, pl.ds(k0, bk), :] - peaks[h])
                total_p = total_p + jnp.sum(p.reshape(bk // 8, 8, bq), 0)
                acc = acc + contract(
                    vt[h * HD : (h + 1) * HD, pl.ds(k0, bk)], p.astype(BF), 1, 0
                )
                result += [total_p, acc]
            return tuple(result)

        start = []
        for h in range(heads):
            start += [jnp.zeros((8, bq), F32), jnp.zeros((HD, bq), F32)]
        done = lax.fori_loop(begin_k, end_k, k_step, tuple(start))
        pieces = []
        for h in range(heads):
            denom = jnp.sum(done[2 * h], 0, keepdims=True)
            pieces.append(done[2 * h + 1] / denom)
            lse[h : h + 1, pl.ds(q0, bq)] = peaks[h] + jnp.log(denom)
        turned = jnp.concatenate(pieces, 0)
        out_t[:, pl.ds(q0, bq)] = turned
        low_rows = turned.T.astype(BF)
        for i in range(bq // BLK):
            place = scal[INVERSE + q0 // BLK + i]
            device = place // 2
            row = ((device // 4) ^ scal[TOP]) * 256 + (place % 2) * BLK
            out[(device % 4) ^ scal[LOW], aligned(row, BLK), :] = low_rows[
                i * BLK : (i + 1) * BLK
            ]
        return 0

    lax.fori_loop(0, total // bq, q_step, 0)
    for k, sent in enumerate((out0, out1, out2, out3)):
        sent[...] = out[k]


def attention_forward(scal, qkv, chunk, bq=512, bk=512):
    total = qkv.shape[0]
    width = qkv.shape[1] // 3
    heads = width // HD
    return pl.pallas_call(
        partial(attention_forward_kernel, heads=heads, chunk=chunk, bq=bq, bk=bk),
        out_shape=(struct((ROWS, width), BF),) * 4
        + (struct((width, total), F32), struct((heads, total), F32)),
        in_specs=[SMEM, VMEM],
        out_specs=(VMEM,) * 6,
        scratch_shapes=[
            pltpu.VMEM((heads, total, 128), BF),
            pltpu.VMEM((heads, total, 128), BF),
            pltpu.VMEM((width, total), BF),
            pltpu.VMEM((heads, total, bq), F32),
            pltpu.VMEM((4, ROWS, width), BF),
        ],
        compiler_params=params(60),
        cost_estimate=takes(23),
        name="attention_forward",
    )(scal, qkv)


def attention_backward_kernel(
    scal, qkv, grad0, grad1, grad2, grad3, out_t, lse, dqkv, qa, ka, kt, va, ga, gt, dkv, dq,
    *, first, heads, chunk, bq, bk
):
    total = qkv.shape[0]
    width = qkv.shape[1] // 3
    begin = first * HD
    end = begin + heads * HD
    split = scal[SPLIT]
    blank = jnp.zeros((chunk, HD), BF)
    short = jnp.zeros((BLK, HD), BF)
    widen(scal, qkv, qa, ka, begin, heads, chunk)
    for m in range(total // chunk):
        pos = pl.multiple_of((scal[ME] ^ CHUNKS[m]) * chunk, chunk)
        rows = slice(m * chunk, (m + 1) * chunk)
        for h in range(heads):
            at = 2 * width + begin + h * HD
            va[h, pl.ds(pos, chunk), :] = jnp.concatenate([qkv[rows, at : at + HD], blank], 1)
        kt[:, pl.ds(pos, chunk)] = qkv[rows, width + begin : width + end].T
    for k, grad in enumerate((grad0, grad1, grad2, grad3)):
        for e in range(4):
            device = (scal[LOW] ^ k) + 4 * ((e // 2) ^ scal[TOP])
            pos = pl.multiple_of(scal[ORDER + 2 * device + e % 2] * BLK, BLK)
            rows = slice(e * BLK, (e + 1) * BLK)
            for h in range(heads):
                g = grad[rows, begin + h * HD : begin + (h + 1) * HD]
                ga[h, pl.ds(pos, BLK), :] = jnp.concatenate([g, short], 1)
            gt[:, pl.ds(pos, BLK)] = grad[rows, begin:end].T
    dkv[...] = jnp.zeros_like(dkv)

    def q_step(qi, _):
        q0 = pl.multiple_of(qi * bq, bq)
        begin_k, end_k = key_range(q0, bq, split, bk, total)
        product = gt[:, pl.ds(q0, bq)].astype(F32) * out_t[begin:end, pl.ds(q0, bq)]
        delta = [jnp.sum(product[h * HD : (h + 1) * HD], 0, keepdims=True) for h in range(heads)]
        held_lse = lse[:, pl.ds(q0, bq)]
        totals = [held_lse[first + h : first + h + 1] for h in range(heads)]

        def k_step(ki, carry):
            k0 = pl.multiple_of(ki * bk, bk)
            result = []
            for h in range(heads):
                q = qa[h, pl.ds(q0, bq), :]
                g = ga[h, pl.ds(q0, bq), :]
                st = contract(ka[h, pl.ds(k0, bk), :], q, 1, 1)
                p = jnp.exp(st - totals[h])
                dp = contract(va[h, pl.ds(k0, bk), :], g, 1, 1)
                ds = (p * (dp - delta[h]) * 0.125).astype(BF)
                dkv[0, h, pl.ds(k0, bk), :] += contract(ds, q, 1, 0)
                dkv[1, h, pl.ds(k0, bk), :] += contract(p.astype(BF), g, 1, 0)
                result.append(
                    carry[h] + contract(kt[h * HD : (h + 1) * HD, pl.ds(k0, bk)], ds, 1, 0)
                )
            return tuple(result)

        start = tuple(jnp.zeros((HD, bq), F32) for _ in range(heads))
        turned = lax.fori_loop(begin_k, end_k, k_step, start)
        dq[pl.ds(q0, bq), :] = jnp.concatenate(turned, 0).T.astype(BF)
        return 0

    lax.fori_loop(0, total // bq, q_step, 0)
    for m in range(total // chunk):
        pos = pl.multiple_of((scal[ME] ^ CHUNKS[m]) * chunk, chunk)
        rows = slice(m * chunk, (m + 1) * chunk)
        dqkv[rows, 0 : heads * HD] = dq[pl.ds(pos, chunk), :]
        for h in range(0, heads, 2):
            for part, gain in ((0, 8.0), (1, 1.0)):
                pair = [dkv[part, h + e, pl.ds(pos, chunk), :][:, :HD] for e in range(2)]
                base = ((1 + part) * heads + h) * HD
                dqkv[rows, base : base + 2 * HD] = (jnp.concatenate(pair, 1) * gain).astype(BF)


def attention_backward(scal, qkv, grads, out_t, lse, chunk, first, heads, bq=512, bk=512):
    total = qkv.shape[0]
    width = heads * HD
    wide = pltpu.VMEM((heads, total, 128), BF)
    return pl.pallas_call(
        partial(
            attention_backward_kernel, first=first, heads=heads, chunk=chunk, bq=bq, bk=bk
        ),
        out_shape=struct((total, 3 * width), BF),
        in_specs=[SMEM] + [VMEM] * 7,
        out_specs=VMEM,
        scratch_shapes=[
            wide,
            wide,
            pltpu.VMEM((width, total), BF),
            wide,
            wide,
            pltpu.VMEM((width, total), BF),
            pltpu.VMEM((2, heads, total, 128), F32),
            pltpu.VMEM((total, width), BF),
        ],
        compiler_params=params(60),
        cost_estimate=takes(40),
        name="attention_backward",
    )(scal, qkv, *grads, out_t, lse)


def carve_kernel(
    tokens, cot, w_qkv, w_out, w_up, w_down, small,
    own, other, cot_own, cot_other, pack, pack_sent, up_slice, down_slice, sems,
):
    me = lax.axis_index("ctx")
    core, low, top, chip = me % 2, me % 4, me // 4, me // 2
    block = core * 4 + chip
    pairs = [(tokens.at[top, 0], own), (tokens.at[1 - top, 0], other)]
    half = aligned(top * 128, 128)
    for k in range(3):
        columns = aligned(k * D + low * 256, 256)
        target = slice(256 * k, 256 * (k + 1))
        pairs.append((w_qkv.at[:, columns], pack.at[:, target]))
        pairs.append((w_qkv.at[half, columns], pack_sent.at[0:128, target]))
    for k in range(4):
        columns = aligned(k * D + block * 128, 128)
        pairs.append((w_up.at[:, columns], up_slice.at[:, 128 * k : 128 * (k + 1)]))
    pairs.append((w_out.at[:, aligned(block * 128, 128)], up_slice.at[:, 512:640]))
    pairs.append((w_down.at[aligned(core * 512 + top * 128, 128), :], down_slice.at[0]))
    side = core * 512 + 256 + (chip % 2) * 128
    pairs.append((w_down.at[aligned(side, 128), :], down_slice.at[1]))
    pairs += [(cot.at[top, 0], cot_own), (cot.at[1 - top, 0], cot_other)]
    copies = copies_of(pairs, sems)
    start_all(copies)
    pack_sent[128:144, 0:256] = small[...]
    wait_all(copies)


def carve(tokens, cot, w_qkv, w_out, w_up, w_down, small):
    rows = tokens.shape[2]
    return pl.pallas_call(
        carve_kernel,
        out_shape=tuple(struct((rows, D), BF) for _ in range(4))
        + (
            struct((256, 768), BF),
            struct((144, 768), BF),
            struct((256, 640), BF),
            struct((2, 128, D), BF),
        ),
        in_specs=[HBM] * 6 + [VMEM],
        out_specs=(VMEM,) * 8,
        scratch_shapes=[pltpu.SemaphoreType.DMA((17,))],
        compiler_params=params(60),
        cost_estimate=takes(4),
        name="carve",
    )(tokens, cot, w_qkv, w_out, w_up, w_down, small)


def project_kernel(
    scal, pack, small, near, away, own, y, x, core_own, core_rest,
    qkv, x_all, weight, vecs, up_bias, qkv_held, x_held, rows_held, sems, out_sems,
):
    chunk = own.shape[0]
    own_f = scal[SHARD]
    pairs = [(pack, weight.at[aligned(own_f * 256, 256)]), (small, rows_held.at[own_f])]
    for k in range(3):
        f = scal[SHARD + 1 + k]
        mine = aligned(f * 256 + scal[TOP] * 128, 128)
        rest = aligned(f * 256 + (1 - scal[TOP]) * 128, 128)
        pairs.append((near.at[k, 0:128], weight.at[mine]))
        pairs.append((away.at[k, 0:128], weight.at[rest]))
        pairs.append((near.at[k, 128:144, 0:256], rows_held.at[f]))
    loads = len(pairs)
    sources = [own, y, x.at[0], x.at[1], core_own] + [core_rest.at[k] for k in range(3)]
    pairs += [
        (piece, x_held.at[m * chunk : (m + 1) * chunk]) for m, piece in enumerate(sources)
    ]
    copies = copies_of(pairs, sems)
    start_all(copies)
    wait_all(copies[:loads])
    for f in range(4):
        held = rows_held[f].astype(F32)
        vecs[:, 256 * f : 256 * (f + 1)] = held[0:8]
        for j in range(4):
            for e in range(2):
                up_bias[2 * j + e : 2 * j + e + 1, 128 * f : 128 * (f + 1)] = held[
                    8 + j : 9 + j, 128 * e : 128 * (e + 1)
                ]
    here = aligned(scal[LOW] * 256, 256)
    bias = jnp.concatenate([vecs[0:1, here], jnp.zeros((1, 256), F32), vecs[1:2, here]], 1)
    outs = []
    for m in range(8):
        copies[loads + m].wait()
        rows = slice(m * chunk, (m + 1) * chunk)
        qkv_held[rows, :] = (contract(x_held[rows, :], weight[...], 1, 0) + bias).astype(BF)
        sent = copies_of(
            [(x_held.at[rows], x_all.at[rows]), (qkv_held.at[rows], qkv.at[rows])], out_sems, 2 * m
        )
        start_all(sent)
        outs += sent
    wait_all(outs)


def project(scal, pack, small, near, away, pieces):
    chunk = pieces[0].shape[0]
    return pl.pallas_call(
        project_kernel,
        out_shape=(
            struct((8 * chunk, 768), BF),
            struct((8 * chunk, D), BF),
            struct((D, 768), BF),
            struct((8, D), F32),
            struct((8, 512), F32),
        ),
        in_specs=[SMEM] + [HBM] * 9,
        out_specs=(HBM, HBM, VMEM, VMEM, VMEM),
        scratch_shapes=[
            pltpu.VMEM((8 * chunk, 768), BF),
            pltpu.VMEM((8 * chunk, D), BF),
            pltpu.VMEM((4, 16, 256), BF),
            pltpu.SemaphoreType.DMA((19,)),
            pltpu.SemaphoreType.DMA((16,)),
        ],
        compiler_params=params(60),
        cost_estimate=takes(8),
        name="project",
    )(scal, pack, small, near, away, *pieces)


def out_pairs(scal, near, away, w_out, held):
    pairs = []
    for side, pieces in enumerate((near, away)):
        for m in range(4):
            block = 4 * (scal[CORE] ^ side) + (scal[CHIP] ^ m)
            for k in range(3):
                rows = aligned(scal[SHARD + 1 + k] * 256, 256)
                pairs.append((pieces.at[m, k], held.at[block, rows]))
            columns = aligned(block * 128, 128)
            rows = aligned(scal[SHARD] * 256, 256)
            pairs.append((w_out.at[:, columns], held.at[block, rows]))
    return pairs


def attention_out_kernel(
    scal, h0, h1, h2, h3, vecs, x_all, w_out, near, away, y1, y1_low, n1, r1, held, x, sems
):
    pairs = out_pairs(scal, near, away, w_out, held)
    for e in range(4):
        device = scal[ME] ^ (4 * (e // 2))
        given = scal[ORDER + 2 * device + e % 2]
        turn = scal[ME] ^ (given // 2)
        chunk = (turn % 2) * 4 + ((turn // 2) % 2) * 2 + turn // 4
        rows = aligned(chunk * 256 + (given % 2) * BLK, BLK)
        pairs.append((x_all.at[rows, :], x.at[e * BLK : (e + 1) * BLK]))
    copies = copies_of(pairs, sems)
    start_all(copies)
    wait_all(copies)
    columns = []
    for b in range(8):
        part = 0.0
        for k, heads in enumerate((h0, h1, h2, h3)):
            rows = aligned((scal[LOW] ^ k) * 256, 256)
            part = part + contract(heads[...], held[b, rows, :], 1, 0)
        columns.append(part)
    into = x[...].astype(F32) + jnp.concatenate(columns, 1) + vecs[2:3]
    out, normed, inverse = norm_forward(into, vecs[3:4], vecs[4:5])
    y1[...] = out
    y1_low[...] = out.astype(BF)
    n1[...] = normed
    r1[...] = jnp.broadcast_to(inverse, r1.shape)


def attention_out(scal, heads, vecs, x_all, w_out, near, away):
    return pl.pallas_call(
        attention_out_kernel,
        out_shape=(
            struct((ROWS, D), F32),
            struct((ROWS, D), BF),
            struct((ROWS, D), F32),
            struct((ROWS, 128), F32),
        ),
        in_specs=[SMEM] + [VMEM] * 5 + [HBM] * 4,
        out_specs=(VMEM,) * 4,
        scratch_shapes=[
            pltpu.VMEM((8, D, 128), BF),
            pltpu.VMEM((ROWS, D), BF),
            pltpu.SemaphoreType.DMA((36,)),
        ],
        compiler_params=params(60),
        cost_estimate=takes(9),
        name="attention_out",
    )(scal, *heads, vecs, x_all, w_out, near, away)


def up_pairs(scal, pieces, w_up, held):
    own, from_x, from_y, far_a, far_b = pieces
    groups = [[] for _ in range(4)]
    for k in range(3):
        base = scal[SHARD + 1 + k] * 256
        for m, piece in enumerate((own, from_x, from_y)):
            target = held.at[scal[CHIP] ^ m, aligned(base, 256)]
            groups[m].append((piece.at[k, :, 0:512], target))
        for half, piece in enumerate((far_a, far_b)):
            target = held.at[scal[CHIP] ^ 3, aligned(base + 128 * half, 128)]
            groups[3].append((piece.at[k, :, 0:512], target))
    rows = aligned(scal[SHARD] * 256, 256)
    for m in range(4):
        chip = scal[CHIP] ^ m
        for k in range(4):
            columns = aligned(k * D + (scal[CORE] * 4 + chip) * 128, 128)
            target = held.at[chip, rows, 128 * k : 128 * (k + 1)]
            groups[m].append((w_up.at[:, columns], target))
    return groups


UP_COPIES = 3 * 7 + 10


def grouped_copies(groups, sems, base=0):
    result = []
    for group in groups:
        result.append(copies_of(group, sems, base))
        base += len(group)
    return result


def down_pairs(scal, own, from_y, from_x, held):
    side = scal[CHIP] % 2
    pairs = []
    for f in range(4):
        rows = slice(128 * f, 128 * (f + 1))
        pairs.append((own.at[f, 0], held.at[scal[TOP], rows]))
        pairs.append((own.at[f, 1], held.at[2 + side, rows]))
        pairs.append((from_y.at[f], held.at[1 - scal[TOP], rows]))
        pairs.append((from_x.at[f], held.at[3 - side, rows]))
    return pairs


DOWN_COPIES = 16


def up_kernel(scal, y1_low, up_bias, w_up, *rest):
    pieces, (act, slope, held, act_held, slope_held, sems, out_sems) = rest[:5], rest[5:]
    groups = grouped_copies(up_pairs(scal, pieces, w_up, held), sems)
    for group in groups:
        start_all(group)
    outs = []
    for m, group in enumerate(groups):
        wait_all(group)
        q = scal[CHIP] ^ m
        bias = up_bias[pl.ds(scal[CORE] * 4 + q, 1), :]
        for r in (slice(0, 256), slice(256, 512)):
            u = contract(y1_low[r, :], held[q], 1, 0) + bias
            cdf = 0.5 * (1.0 + lax.erf(u * (1.0 / math.sqrt(2.0))))
            density = jnp.exp(-0.5 * u * u) * (1.0 / math.sqrt(2.0 * math.pi))
            slope_held[q, r, :] = (cdf + u * density).astype(BF)
            act_held[q, r, :] = (u * cdf).astype(BF)
        copies = copies_of(
            [(act_held.at[q], act.at[q]), (slope_held.at[q], slope.at[q])], out_sems, 2 * m
        )
        start_all(copies)
        outs += copies
    wait_all(outs)


def feed_up(scal, y1_low, up_bias, w_up, pieces):
    block = pltpu.VMEM((4, ROWS, 512), BF)
    return pl.pallas_call(
        up_kernel,
        out_shape=(struct((4, ROWS, 512), BF), struct((4, ROWS, 512), BF)),
        in_specs=[SMEM, VMEM, VMEM] + [HBM] * 6,
        out_specs=(HBM, HBM),
        scratch_shapes=[
            pltpu.VMEM((4, D, 512), BF),
            block,
            block,
            pltpu.SemaphoreType.DMA((UP_COPIES,)),
            pltpu.SemaphoreType.DMA((8,)),
        ],
        compiler_params=params(60),
        cost_estimate=takes(7),
        name="feed_up",
    )(scal, y1_low, up_bias, w_up, *pieces)


def down_kernel(scal, act, own, from_y, from_x, part, held, act_held, total, sems):
    pairs = down_pairs(scal, own, from_y, from_x, held)
    copies = copies_of(pairs, sems)
    acts = copies_of([(act.at[q], act_held.at[q]) for q in range(4)], sems, DOWN_COPIES)
    start_all(copies)
    start_all(acts)
    wait_all(copies)
    for q in range(4):
        acts[q].wait()
        moved = contract(act_held[q], held[q], 1, 0)
        if q == 0:
            total[...] = moved
        elif q < 3:
            total[...] += moved
        else:
            part[...] = (total[...] + moved).astype(part.dtype)


def feed_down(scal, act, pieces, dtype):
    return pl.pallas_call(
        down_kernel,
        out_shape=struct((ROWS, D), dtype),
        in_specs=[SMEM] + [HBM] * 4,
        out_specs=VMEM,
        scratch_shapes=[
            pltpu.VMEM((4, 512, D), BF),
            pltpu.VMEM((4, ROWS, 512), BF),
            pltpu.VMEM((ROWS, D), F32),
            pltpu.SemaphoreType.DMA((DOWN_COPIES + 4,)),
        ],
        compiler_params=params(60),
        cost_estimate=takes(5),
        name="feed_down",
    )(scal, act, *pieces)


def second_norm_kernel(y1, part, came, cot_own, cot_came, vecs, out_own, out_away, dh2, dz2, sums):
    n = pl.program_id(0)
    h2 = y1[...] + part[...] + came[...].astype(F32) + vecs[5:6]
    out, normed, inverse = norm_forward(h2, vecs[6:7], vecs[7:8])
    out = out.astype(BF)
    c = jnp.where(n < 2, cot_own[...], cot_came[...]).astype(F32)
    grad = norm_backward(c, normed, inverse, vecs[6:7])
    dh2[...] = grad
    low = grad.astype(BF)
    dz2[...] = low

    @pl.when(n == 0)
    def _():
        sums[...] = jnp.zeros_like(sums)

    for i, value in enumerate((c * normed, c, low.astype(F32))):
        sums[i : i + 1, :] += jnp.sum(value, 0, keepdims=True)

    @pl.when(n < 2)
    def _():
        out_own[...] = out

    @pl.when(n >= 2)
    def _():
        out_away[...] = out


def second_norm(y1, part, came, cot_own, cot_came, vecs):
    half = struct((ROWS // 2, D), BF)
    rows = pl.BlockSpec((128, D), lambda n: (n, 0))
    first = pl.BlockSpec((128, D), lambda n: (jnp.minimum(n, 1), 0))
    last = pl.BlockSpec((128, D), lambda n: (jnp.maximum(n - 2, 0), 0))
    whole = pl.BlockSpec((8, D), lambda n: (0, 0))
    return pl.pallas_call(
        second_norm_kernel,
        grid=(4,),
        out_shape=(half, half, struct((ROWS, D), F32), struct((ROWS, D), BF), struct((8, D), F32)),
        in_specs=[rows, rows, rows, first, last, whole],
        out_specs=(first, last, rows, rows, whole),
        compiler_params=params(60),
        cost_estimate=takes(4),
        name="second_norm",
    )(y1, part, came, cot_own, cot_came, vecs)


def back_kernel(scal, dz2_a, dz2_b, slope_a, slope_b, w_up, *rest):
    ups, downs, outs, scratch = rest[:5], rest[5:8], rest[8:13], rest[13:]
    du_a, du_b, part_a, part_b, up_sums = outs
    up_held, down_held, slopes, dus, acc_a, acc_b, sems, out_sems = scratch
    down_copies = copies_of(down_pairs(scal, *downs, down_held), sems)
    groups = grouped_copies(up_pairs(scal, ups, w_up, up_held), sems, DOWN_COPIES)
    loads = []
    for m in range(4):
        q = scal[CHIP] ^ m
        pairs = [(slope_b.at[q], slopes.at[1, q]), (slope_a.at[q], slopes.at[0, q])]
        loads.append(copies_of(pairs, sems, DOWN_COPIES + UP_COPIES + 2 * m))
    start_all(down_copies)
    for group, load in zip(groups, loads):
        start_all(load)
        start_all(group)
    wait_all(down_copies)
    sent = []
    for m in range(4):
        wait_all(loads[m])
        wait_all(groups[m])
        q = scal[CHIP] ^ m
        total = jnp.zeros((1, 512), F32)
        for side, (dz2, du, acc) in enumerate(((dz2_a, du_a, acc_a), (dz2_b, du_b, acc_b))):
            for r in (slice(0, 256), slice(256, 512)):
                low = contract(dz2[r, :], down_held[q], 1, 1) * slopes[side, q, r, :].astype(F32)
                low = low.astype(BF)
                dus[side, q, r, :] = low
                total = total + jnp.sum(low.astype(F32), 0, keepdims=True)
                moved = contract(low, up_held[q], 1, 1)
                if m == 0:
                    acc[r, :] = moved
                else:
                    acc[r, :] += moved
            copies = copies_of([(dus.at[side, q], du.at[q])], out_sems, 2 * m + side)
            start_all(copies)
            sent += copies
        up_sums[pl.ds(q, 1), :] = total
    part_a[...] = acc_a[...]
    part_b[...] = acc_b[...].astype(BF)
    wait_all(sent)


def feed_back(scal, dz2s, slopes, w_up, ups, downs):
    du = struct((4, ROWS, 512), BF)
    return pl.pallas_call(
        back_kernel,
        out_shape=(
            du, du, struct((ROWS, D), F32), struct((ROWS, D), BF), struct((8, 512), F32)
        ),
        in_specs=[SMEM, VMEM, VMEM] + [HBM] * 11,
        out_specs=(HBM, HBM, VMEM, VMEM, VMEM),
        scratch_shapes=[
            pltpu.VMEM((4, D, 512), BF),
            pltpu.VMEM((4, 512, D), BF),
            pltpu.VMEM((2, 4, ROWS, 512), BF),
            pltpu.VMEM((2, 4, ROWS, 512), BF),
            pltpu.VMEM((ROWS, D), F32),
            pltpu.VMEM((ROWS, D), F32),
            pltpu.SemaphoreType.DMA((DOWN_COPIES + UP_COPIES + 8,)),
            pltpu.SemaphoreType.DMA((8,)),
        ],
        compiler_params=params(60),
        cost_estimate=takes(22),
        name="feed_back",
    )(scal, *dz2s, *slopes, w_up, *ups, *downs)


def first_norm_kernel(
    scal, dh2, part, came, n1, r1, vecs, w_out, near, away, dao, g0, g1, g2, g3, sums, held, sems
):
    copies = copies_of(out_pairs(scal, near, away, w_out, held), sems)
    start_all(copies)
    dy1 = dh2[...] + part[...] + came[...].astype(F32)
    normed = n1[...]
    low = norm_backward(dy1, normed, r1[:, 0:1], vecs[3:4]).astype(BF)
    dao[...] = low
    sums[0:1, :] = jnp.sum(dy1 * normed, 0, keepdims=True)
    sums[1:2, :] = jnp.sum(dy1, 0, keepdims=True)
    sums[2:3, :] = jnp.sum(low.astype(F32), 0, keepdims=True)
    wait_all(copies)
    for k, out in enumerate((g0, g1, g2, g3)):
        rows = aligned((scal[LOW] ^ k) * 256, 256)
        total = 0.0
        for b in range(0, 8, 2):
            weight = jnp.concatenate([held[b, rows, :], held[b + 1, rows, :]], 1)
            total = total + contract(dao[:, b * 128 : (b + 2) * 128], weight, 1, 1)
        out[...] = total.astype(BF)


def first_norm(scal, dh2, part, came, n1, r1, vecs, w_out, near, away):
    return pl.pallas_call(
        first_norm_kernel,
        out_shape=(struct((ROWS, D), BF),) + (struct((ROWS, 256), BF),) * 4 + (struct((8, D), F32),),
        in_specs=[SMEM] + [VMEM] * 6 + [HBM] * 3,
        out_specs=(VMEM,) * 6,
        scratch_shapes=[pltpu.VMEM((8, D, 128), BF), pltpu.SemaphoreType.DMA((32,))],
        compiler_params=params(60),
        cost_estimate=takes(7),
        name="first_norm",
    )(scal, dh2, part, came, n1, r1, vecs, w_out, near, away)


def split_write(n, block, a_keep, a_send, b_keep, b_send):
    half = a_keep.shape[1]
    top_rows, low_rows = block[:half], block[half:]
    for step in range(4):

        @pl.when(n == step)
        def _():
            (a_send if step in (1, 3) else a_keep)[0] = top_rows
            (b_send if step in (2, 3) else b_keep)[0] = low_rows


def split_specs(rows, columns):
    half = (1, rows // 2, columns)
    return (
        pl.BlockSpec(half, lambda n, s: (n // 2, 0, 0)),
        pl.BlockSpec(half, lambda n, s: (n // 2, 0, 0)),
        pl.BlockSpec(half, lambda n, s: (jnp.minimum(n, 1), 0, 0)),
        pl.BlockSpec(half, lambda n, s: (jnp.maximum(n - 2, 0), 0, 0)),
    )


def split_shapes(rows, columns):
    return (struct((2, rows // 2, columns), BF),) * 4


def down_grad_kernel(scal, act_a, act_b, dz2_a, dz2_b, *outs):
    left = [jnp.concatenate([act[f] for f in range(4)], 1) for act in (act_a, act_b)]
    rows = contract(left[0], dz2_a[...], 0, 0) + contract(left[1], dz2_b[...], 0, 0)
    split_write(pl.program_id(0), rows.astype(BF), *outs)


def down_grad(scal, acts, dz2s):
    act_spec = pl.BlockSpec((4, ROWS, 128), lambda n, s: (0, 0, s[CHIP] ^ n))
    dz2_spec = pl.BlockSpec((ROWS, D), lambda n, s: (0, 0))
    return pl.pallas_call(
        down_grad_kernel,
        out_shape=split_shapes(512, D),
        grid_spec=pltpu.PrefetchScalarGridSpec(
            num_scalar_prefetch=1,
            grid=(4,),
            in_specs=[act_spec, act_spec, dz2_spec, dz2_spec],
            out_specs=split_specs(512, D),
        ),
        compiler_params=params(60),
        cost_estimate=takes(11),
        name="down_grad",
    )(scal, *acts, *dz2s)


OUT_WIDTH = 1024 + 128
UP_WIDTH = 4096 + 1024 + 128


def up_parts(y1_a, y1_b, du_a, du_b):
    return [
        contract(y1_a[...], du_a[q], 0, 0) + contract(y1_b[...], du_b[q], 0, 0) for q in range(4)
    ]


def up_grad_other_kernel(scal, y1_a, y1_b, du_a, du_b, out, left):
    @pl.when(pl.program_id(0) == 0)
    def _():
        for side, y1 in enumerate((y1_a, y1_b)):
            for n in range(4):
                row = 2 * (scal[CHIP] ^ n) + 1 - scal[CORE]
                left[side, :, 128 * n : 128 * (n + 1)] = y1[:, aligned(row * 128, 128)]

    rows = contract(left[0], du_a[0], 0, 0) + contract(left[1], du_b[0], 0, 0)
    for n in range(4):
        out[n] = rows[128 * n : 128 * (n + 1)].astype(BF)


def out_grad_other_kernel(scal, heads, dao, small, out):
    parts = [contract(heads[0], dao[...], 0, 0), small[0]]
    out[0] = jnp.concatenate(parts, 1).astype(BF)


def up_grad_own_kernel(scal, y1_a, y1_b, du_a, du_b, heads, dao, small, came, came_out, *rest):
    outs, block = rest[:4], rest[4]
    core = scal[CORE]
    own = jnp.concatenate(up_parts(y1_a, y1_b, du_a, du_b), 1).astype(BF)
    block[:, aligned(core * 2048, 2048)] = own
    block[:, aligned((1 - core) * 2048, 2048)] = came[0]
    out_rows = contract(heads[0], dao[...], 0, 0) + came_out[0, :, :1024].astype(F32)
    block[:, 4096:5120] = out_rows.astype(BF)
    block[:, 5120:] = (small[0] + came_out[0, :, 1024:].astype(F32)).astype(BF)
    split_write(pl.program_id(0), block, *outs)


def of_row(index, flip):
    return lambda n, s: index(s[CHIP] ^ n, s[CORE] ^ flip, s)


def up_specs(flip):
    y1_spec = pl.BlockSpec((ROWS, 128), of_row(lambda q, c, s: (0, 2 * q + c), flip))
    du_spec = pl.BlockSpec((4, ROWS, 512), lambda n, s: (0, 0, 0))
    return [y1_spec, y1_spec, du_spec, du_spec]


def out_specs(flip):
    return [
        pl.BlockSpec((1, ROWS, 128), of_row(lambda q, c, s: (q ^ s[LOW], 0, c), flip)),
        pl.BlockSpec((ROWS, D), lambda n, s: (0, 0)),
        pl.BlockSpec((1, 128, 128), of_row(lambda q, c, s: (2 * q + c, 0, 0), flip)),
    ]


UP_SENT = pl.BlockSpec((1, 128, 2048), lambda n, s: (n, 0, 0))
OUT_SENT = pl.BlockSpec((1, 128, OUT_WIDTH), lambda n, s: (n, 0, 0))


def up_grad_other(scal, y1s, dus):
    y1_spec = pl.BlockSpec((ROWS, D), lambda q, s: (0, 0))
    du_spec = pl.BlockSpec((1, ROWS, 512), lambda q, s: (q, 0, 0))
    return pl.pallas_call(
        up_grad_other_kernel,
        out_shape=struct((4, 128, 2048), BF),
        grid_spec=pltpu.PrefetchScalarGridSpec(
            num_scalar_prefetch=1,
            grid=(4,),
            in_specs=[y1_spec, y1_spec, du_spec, du_spec],
            out_specs=pl.BlockSpec((4, 128, 512), lambda q, s: (0, 0, q)),
            scratch_shapes=[pltpu.VMEM((2, ROWS, 512), BF)],
        ),
        compiler_params=params(60),
        cost_estimate=takes(6),
        name="up_grad_other",
    )(scal, *y1s, *dus)


def out_grad_other(scal, heads, dao, small):
    return pl.pallas_call(
        out_grad_other_kernel,
        out_shape=struct((4, 128, OUT_WIDTH), BF),
        grid_spec=pltpu.PrefetchScalarGridSpec(
            num_scalar_prefetch=1, grid=(4,), in_specs=out_specs(1), out_specs=OUT_SENT
        ),
        compiler_params=params(60),
        cost_estimate=takes(3),
        name="out_grad_other",
    )(scal, heads, dao, small)


def up_grad_own(scal, y1s, dus, heads, dao, small, came, came_out):
    return pl.pallas_call(
        up_grad_own_kernel,
        out_shape=split_shapes(128, UP_WIDTH),
        grid_spec=pltpu.PrefetchScalarGridSpec(
            num_scalar_prefetch=1,
            grid=(4,),
            in_specs=up_specs(0) + out_specs(0) + [UP_SENT, OUT_SENT],
            out_specs=split_specs(128, UP_WIDTH),
            scratch_shapes=[pltpu.VMEM((128, UP_WIDTH), BF)],
        ),
        compiler_params=params(60),
        cost_estimate=takes(10),
        name="up_grad_own",
    )(scal, *y1s, *dus, heads, dao, small, came, came_out)


def qkv_grad_kernel(scal, x, dqkv, send, keep):
    ones = jnp.ones((dqkv.shape[0], 128), BF)
    lane = lax.broadcasted_iota(jnp.int32, (256, 128), 1)
    q_sum = contract(dqkv[:, 0:256], ones, 0, 0)
    v_sum = contract(dqkv[:, 512:768], ones, 0, 0)
    extra = jnp.where(lane == 0, q_sum, jnp.where(lane == 1, v_sum, 0.0))
    for y, out in ((1 - scal[TOP], send), (scal[TOP], keep)):
        for r in range(2):
            group = 2 * y + r
            rows = contract(x[:, aligned(256 * group, 256)], dqkv[...], 0, 0)
            here = jnp.where(scal[LOW] == group, 1.0, 0.0)
            block = jnp.concatenate([rows, extra * here], 1).astype(BF)
            for e in range(2):
                for f in range(4):
                    at = 128 * e + 32 * f
                    out[f, 2 * r + e] = block[at : at + 32, :]


def qkv_grad(scal, x_all, dqkv):
    return pl.pallas_call(
        qkv_grad_kernel,
        out_shape=(struct((4, 4, 32, 896), BF),) * 2,
        in_specs=[SMEM, VMEM, VMEM],
        out_specs=(VMEM, VMEM),
        compiler_params=params(60),
        cost_estimate=takes(8),
        name="qkv_grad",
    )(scal, x_all, dqkv)


def input_grad_kernel(scal, dqkv, weight, dao, out, *, first):
    held = pl.program_id(0) + first
    total = contract(dqkv[...], weight[...], 1, 1)
    turn = (held // 4) + 2 * ((held // 2) % 2) + 4 * (held % 2)
    for e in range(2):
        place = scal[INVERSE + 2 * (scal[ME] ^ turn) + e]
        other = (place // 2) ^ scal[ME]
        mine = jnp.where((other == 0) | (other == 4), 1.0, 0.0)
        source = aligned(((other // 4) % 2) * 256 + (place % 2) * BLK, BLK)
        rows = total[BLK * e : BLK * (e + 1)]
        out[0, BLK * e : BLK * (e + 1), :] = (rows + dao[source, :].astype(F32) * mine).astype(BF)


def input_grad(scal, dqkv, weight, dao, first):
    rows = pl.BlockSpec((256, 768), lambda n, s: (n + first, 0))
    return pl.pallas_call(
        partial(input_grad_kernel, first=first),
        out_shape=struct((4, 256, D), BF),
        grid_spec=pltpu.PrefetchScalarGridSpec(
            num_scalar_prefetch=1,
            grid=(4,),
            in_specs=[
                rows,
                pl.BlockSpec((D, 768), lambda n, s: (0, 0)),
                pl.BlockSpec((ROWS, D), lambda n, s: (0, 0)),
            ],
            out_specs=pl.BlockSpec((1, 256, D), lambda n, s: (n, 0, 0)),
        ),
        compiler_params=params(60),
        cost_estimate=takes(5),
        name="input_grad",
    )(scal, dqkv, weight, dao)


def after(value, *others):
    return lax.optimization_barrier((value,) + others)[0]


def tied(*values):
    return lax.optimization_barrier(values)


def add_low(a, b):
    return (a.astype(F32) + b.astype(F32)).astype(BF)


def add_far(a_keep, b_keep, a_came, b_came):
    return hop(add_low(a_keep[1], a_came[1]), 4), hop(add_low(b_keep[1], b_came[1]), 2)


def sum_chips(a_keep, b_keep, a_came, b_came, a_next, b_next):
    a_all = a_keep[0].astype(F32) + a_came[0].astype(F32) + a_next.astype(F32)
    b_all = b_keep[0].astype(F32) + b_came[0].astype(F32) + b_next.astype(F32)
    return jnp.concatenate([a_all, b_all], 0).astype(BF)


def sum_shards(rows):
    return lax.psum_scatter(rows, "fsdp", scatter_dimension=0, tiled=True)


def tiled_device(
    tokens, cotangent, lengths, order, w_qkv, w_out, w_up, w_down, q_bias, v_bias, out_bias,
    norm1_gain, norm1_bias, up_bias, down_bias, norm2_gain, norm2_bias,
):
    me = lax.axis_index("ctx")
    core, low, top = me % 2, me % 4, me // 4
    chunk = tokens.shape[2]
    half_groups = [[0, 1, 2, 3], [4, 5, 6, 7]]
    scal = scalars(order, lengths)
    small = jnp.zeros((16, 256), BF)
    row = lax.broadcasted_iota(jnp.int32, (16, 256), 0)
    rows_of_small = [
        q_bias, v_bias, out_bias, norm1_gain, norm1_bias, down_bias, norm2_gain, norm2_bias,
    ] + [up_bias[256 * k : 256 * (k + 1)] for k in range(4)]
    for k, vector in enumerate(rows_of_small):
        small = jnp.where(row == k, vector[None, :], small)
    own_rows, other_rows, cot_own, cot_other, pack, pack_sent, up_slice, down_slice = carve(
        tokens, cotangent, w_qkv, w_out, w_up, w_down, small
    )

    def around(value):
        return [
            lax.ppermute(value, "fsdp", [(i, (i + k) % 4) for i in range(4)]) for k in (1, 2, 3)
        ]

    *pack_near, from_y = tied(*around(pack_sent), hop(other_rows, 4))
    pack_near = jnp.stack(pack_near)
    from_x, pack_away = tied(hop(jnp.stack([own_rows, from_y]), 2), hop(pack_near, 4))
    up_own = lax.all_gather(after(up_slice, from_y), "fsdp", axis=0)
    core_own = hop(own_rows, 1)
    core_rest = hop(jnp.concatenate([from_y[None], from_x], 0), 1)
    down_own = lax.all_gather(after(down_slice, from_x), "fsdp", axis=0)
    qkv, x_all, qkv_weight, vecs, up_b = project(
        scal, pack, small, pack_near, pack_away,
        (own_rows, from_y, from_x, core_own, core_rest),
    )
    up_own, qkv = tied(up_own, qkv)
    foreign = jnp.stack(
        [lax.dynamic_index_in_dim(up_own, scal[SHARD + k], 0, False) for k in (1, 2, 3)]
    )
    up_x, up_y = hop(foreign, 2), hop(foreign, 4)
    out_far = hop(foreign[:, :, 512:], 6)
    *sent, turned, lse = attention_forward(scal, after(qkv, foreign), chunk)
    up_x, up_y, out_far, *sent = tied(up_x, up_y, out_far, *sent)
    near = jnp.stack([piece[:, :, 512:] for piece in (foreign, up_x, up_y)] + [out_far])
    away, *came_heads = tied(hop(near, 1), *[hop(sent[k], k) for k in (1, 2, 3)])
    heads = [sent[0], *came_heads]
    far_a, far_b = hop(after(up_y, away)[:, :128], 2), hop(after(up_x, away)[:, 128:], 4)
    ups = (foreign, up_x, up_y, far_a, far_b)
    y1, y1_low, n1, r1 = attention_out(scal, heads, vecs, x_all, w_out, near, away)
    y1, y1_low, n1, r1, far_a, far_b = tied(y1, y1_low, n1, r1, far_a, far_b)
    ups = (foreign, up_x, up_y, far_a, far_b)

    down_own = after(down_own, far_a, far_b)
    down_y, down_x = hop(down_own[:, 0], 4), hop(down_own[:, 1], 2)
    y1_away = hop(y1_low, 1)
    act, slope = feed_up(scal, y1_low, up_b, w_up, ups)
    act, slope, y1_away = tied(act, slope, y1_away)
    act_away, slope_away = feed_up(scal, y1_away, up_b, w_up, ups)
    act_away, slope_away, down_x, down_y = tied(act_away, slope_away, down_x, down_y)
    downs = (down_own, down_y, down_x)
    part_away = hop(feed_down(scal, act_away, downs, BF), 1)
    cot_came = hop(after(cot_other, act_away), 4)
    part = feed_down(scal, act, downs, F32)
    part, part_away, cot_came = tied(part, part_away, cot_came)
    out_own, out_away, dh2, dz2, sums2 = second_norm(y1, part, part_away, cot_own, cot_came, vecs)
    dz2_away = hop(dz2, 1)
    dak, das, dbk, dbs = down_grad(scal, (act, act_away), (dz2, dz2_away))
    dak, das, dbk, dbs, mixed_came = tied(dak, das, dbk, dbs, hop(out_away, 4))
    mixed = jnp.where(
        top == 0, jnp.stack([out_own, mixed_came]), jnp.stack([mixed_came, out_own])
    )[:, None]
    da_came, db_came = hop(das, 2), hop(dbs, 4)
    du, du_away, part, part_away, up_sums = feed_back(
        scal, (dz2, after(dz2_away, dak)), (slope, slope_away), w_up, ups, downs
    )
    part, du, du_away, up_sums, part_away, da_came, db_came = tied(
        part, du, du_away, up_sums, part_away, da_came, db_came
    )
    part_away = hop(part_away, 1)
    y1s, dus = (y1_low, y1_away), (du, du_away)
    up_other = up_grad_other(scal, y1s, dus)
    up_other, part_away = tied(up_other, part_away)
    dao, *dattn, sums1 = first_norm(
        scal, dh2, part, part_away, n1, r1, vecs, w_out, near, away
    )
    dattn = [dattn[0]] + [hop(dattn[k], k) for k in (1, 2, 3)]
    up_came = hop(up_other, 1)

    def per_owner(vector):
        return vector.reshape(8, 4, 32)

    unit_sums = up_sums[:4].reshape(4, 4, 128).transpose(1, 0, 2)
    mine = (jnp.arange(2) == core)[None, :, None, None]
    up_owner = jnp.where(mine, unit_sums[:, None], 0.0).reshape(8, 4, 128)
    vec_block = jnp.concatenate(
        [per_owner(sums1[2]), per_owner(sums1[0]), per_owner(sums1[1]), per_owner(sums2[2]),
         per_owner(sums2[0]), per_owner(sums2[1]), up_owner, jnp.zeros((8, 4, 64), F32)], 2
    ).reshape(8, 4, 3, 128)
    vec_block = jnp.concatenate([vec_block, jnp.zeros((8, 4, 29, 128), F32)], 2).reshape(
        8, 128, 128
    )
    all_heads = jnp.stack(heads)
    out_other = out_grad_other(scal, all_heads, dao, vec_block)
    uak, uas, ubk, ubs = up_grad_own(
        scal, y1s, dus, all_heads, dao, vec_block, up_came, hop(out_other, 1)
    )
    uak, uas, ubk, ubs, *dattn = tied(uak, uas, ubk, ubs, *dattn)
    da_next, db_next = add_far(dak, dbk, da_came, db_came)
    ua_came, ub_came = hop(uas, 2), hop(ubs, 4)
    dqkv = attention_backward(scal, after(qkv, uak), dattn, turned, lse, chunk, 0, 4)
    da_next, db_next, ua_came, ub_came, dqkv = tied(da_next, db_next, ua_came, ub_came, dqkv)

    ua_sent, ub_sent = add_low(uak[1], ua_came[1]), add_low(ubk[1], ub_came[1])
    ua_next, ub_next = hop(ua_sent, 4), hop(ub_sent, 2)
    down_sum = sum_chips(dak, dbk, da_came, db_came, after(da_next, ua_sent, ub_sent), db_next)
    down_rows = sum_shards(down_sum)
    grad_send, grad_keep = qkv_grad(scal, x_all, dqkv)
    grad_send, grad_keep, ua_next, ub_next = tied(grad_send, grad_keep, ua_next, ub_next)
    grad_came = hop(grad_send, 4)
    up_sum = sum_chips(uak, ubk, ua_came, ub_came, ua_next, ub_next)
    up_rows = sum_shards(up_sum).astype(F32)
    dx_away = input_grad(scal, after(dqkv, grad_keep, up_sum), qkv_weight, dao, 4)
    dx = input_grad(scal, dqkv, qkv_weight, after(dao, dx_away), 0)
    dx_came, dx, grad_came = tied(hop(dx_away, 1), dx, grad_came)
    grad_parts = lax.all_to_all(
        add_low(grad_keep, grad_came), "fsdp", 0, 0, tiled=True
    )
    sent_rows = add_low(dx[2:], dx_came[2:])
    far_rows = hop(sent_rows[1], 2)
    kept_rows = add_low(dx[:2], after(dx_came, sent_rows)[:2])
    far_rows, kept_rows = tied(far_rows, kept_rows)
    own_rows = hop(after(sent_rows[0], far_rows), 2)
    home_rows = hop(add_low(kept_rows[1], far_rows), 4)
    grad_parts, own_rows, home_rows = tied(grad_parts, own_rows, home_rows)
    grad_own = add_low(kept_rows[0], own_rows)
    tokens_grad = jnp.where(
        top == 0, jnp.stack([grad_own, home_rows]), jnp.stack([home_rows, grad_own])
    )[:, None]
    mine = lax.all_to_all(
        jnp.sum(grad_parts.astype(F32), 0).astype(BF), "ctx", 0, 0, tiled=True,
        axis_index_groups=half_groups,
    ).astype(F32)
    w_qkv_grad = mine[:, :, :768].reshape(4, 32, 3, 256).transpose(1, 2, 0, 3).reshape(32, 3072)
    q_bias_grad = jnp.sum(mine[:, :, 768], 0)
    v_bias_grad = jnp.sum(mine[:, :, 769], 0)

    w_up_grad = (
        up_rows[:, :4096].reshape(32, 8, 4, 128).transpose(0, 2, 1, 3).reshape(32, 4096)
    )
    w_out_grad = up_rows[:, 4096:5120]
    sums = up_rows[:3, 5120:].reshape(384)
    return (
        mixed, tokens_grad, w_qkv_grad, w_out_grad, w_up_grad, down_rows.astype(F32), q_bias_grad, v_bias_grad,
        sums[0:32], sums[32:64], sums[64:96], sums[192:320], sums[96:128], sums[128:160],
        sums[160:192],
    )


def pick_blocks(wanted, rows):
    shaped = rows.reshape(-1, BLK, rows.shape[-1])
    picked = [
        lax.dynamic_index_in_dim(shaped, wanted[e], 0, False) for e in range(wanted.shape[0])
    ]
    return jnp.concatenate(picked, 0)


def plain_device(
    tokens, cotangent, lengths, order, w_qkv, w_out, w_up, w_down, q_bias, v_bias, out_bias,
    norm1_gain, norm1_bias, up_bias, down_bias, norm2_gain, norm2_bias,
):
    shards = (
        w_qkv, w_out, w_up, w_down, q_bias, v_bias, out_bias, norm1_gain, norm1_bias, up_bias,
        down_bias, norm2_gain, norm2_bias,
    )
    me = lax.axis_index("ctx")
    count = lax.axis_size("ctx")
    rows = tokens.shape[2]
    per_device = rows // BLK
    whole_rows = rows * count
    scaling = 1.0 / math.sqrt(HD)
    (
        qkv_full, out_full, up_full, down_full, qbias_full, vbias_full, obias_full, gain_one,
        shift_one, ubias_full, dbias_full, gain_two, shift_two,
    ) = tuple(lax.all_gather(shard, "fsdp", axis=0, tiled=True) for shard in shards)
    full_bias = jnp.concatenate([qbias_full, jnp.zeros_like(qbias_full), vbias_full]).astype(F32)
    gain_one, shift_one, gain_two, shift_two = (
        vector.astype(F32) for vector in (gain_one, shift_one, gain_two, shift_two)
    )
    positions = jnp.arange(whole_rows, dtype=jnp.int32)
    mixed_list, grad_list, totals = [], [], None
    for micro in range(tokens.shape[0]):
        order_row = order[micro, 0]
        bound = lengths[micro, 0, 0]
        segment_all = (positions >= bound).astype(jnp.int32)
        segment_query = (me * rows + jnp.arange(rows, dtype=jnp.int32) >= bound).astype(jnp.int32)
        dealt = me * per_device + jnp.arange(per_device, dtype=jnp.int32)
        blocks = jnp.arange(order_row.shape[0], dtype=jnp.int32)
        inverse = jnp.sum(jnp.where(order_row[None, :] == dealt[:, None], blocks[None, :], 0), 1)
        forward = jnp.sum(jnp.where(blocks[None, :] == dealt[:, None], order_row[None, :], 0), 1)
        token_rows = tokens[micro, 0]
        cot_rows = pick_blocks(
            inverse, lax.all_gather(cotangent[micro, 0], "ctx", axis=0, tiled=True)
        ).astype(F32)
        qkv_rows = (jnp.dot(token_rows, qkv_full, preferred_element_type=F32) + full_bias).astype(BF)
        queries = qkv_rows[:, :D].reshape(rows, H, HD)
        keys_values = lax.all_gather(qkv_rows[:, D:], "ctx", axis=0, tiled=True)
        keys = keys_values[:, :D].reshape(whole_rows, H, HD)
        values = keys_values[:, D:].reshape(whole_rows, H, HD)
        allowed = (segment_query[:, None] == segment_all[None, :])[None]
        scores = jnp.einsum("rhd,khd->hrk", queries, keys, preferred_element_type=F32) * scaling
        scores = jnp.where(allowed, scores, NEGATIVE)
        expos = jnp.where(allowed, jnp.exp(scores - jnp.max(scores, -1, keepdims=True)), 0.0)
        probs = expos / jnp.sum(expos, -1, keepdims=True)
        probs_low = probs.astype(BF)
        attn_float = jnp.einsum("hrk,khd->rhd", probs_low, values, preferred_element_type=F32)
        attn_low = attn_float.reshape(rows, D).astype(BF)
        first_in = (
            token_rows.astype(F32)
            + jnp.dot(attn_low, out_full, preferred_element_type=F32)
            + obias_full.astype(F32)
        )
        first_out, normed_one, inverse_one = norm_forward(first_in, gain_one, shift_one)
        first_low = first_out.astype(BF)
        hidden_in = jnp.dot(first_low, up_full, preferred_element_type=F32) + ubias_full.astype(F32)
        activated, gelu_back = jax.vjp(partial(jax.nn.gelu, approximate=False), hidden_in)
        act_low = activated.astype(BF)
        second_in = (
            first_out
            + jnp.dot(act_low, down_full, preferred_element_type=F32)
            + dbias_full.astype(F32)
        )
        second_out, normed_two, inverse_two = norm_forward(second_in, gain_two, shift_two)
        out_all = lax.all_gather(second_out.astype(BF), "ctx", axis=0, tiled=True)
        mixed_list.append(pick_blocks(forward, out_all))

        grad_second = norm_backward(cot_rows, normed_two, inverse_two, gain_two)
        grad_down_low = grad_second.astype(BF)
        (grad_hidden,) = gelu_back(contract(grad_down_low, down_full, 1, 1))
        grad_hidden_low = grad_hidden.astype(BF)
        grad_first = grad_second + contract(grad_hidden_low, up_full, 1, 1)
        grad_first_in = norm_backward(grad_first, normed_one, inverse_one, gain_one)
        grad_branch = grad_first_in.astype(BF)
        grad_attn = contract(grad_branch, out_full, 1, 1).astype(BF).reshape(rows, H, HD)
        grad_probs = jnp.einsum("rhd,khd->hrk", grad_attn, values, preferred_element_type=F32)
        delta = jnp.sum(probs * grad_probs, -1, keepdims=True)
        grad_scores = (probs * (grad_probs - delta) * scaling).astype(BF)
        grad_query = jnp.einsum("hrk,khd->rhd", grad_scores, keys, preferred_element_type=F32)
        grad_keys = jnp.einsum("hrk,rhd->khd", grad_scores, queries, preferred_element_type=F32)
        grad_values = jnp.einsum("hrk,rhd->khd", probs_low, grad_attn, preferred_element_type=F32)
        both = jnp.concatenate(
            [grad_keys.reshape(whole_rows, D), grad_values.reshape(whole_rows, D)], 1
        )
        both = lax.psum_scatter(both, "ctx", scatter_dimension=0, tiled=True)
        grad_qkv = jnp.concatenate([grad_query.reshape(rows, D), both], 1).astype(BF)
        column_sums = jnp.sum(grad_qkv.astype(F32), 0)
        grad_list.append((grad_first_in + contract(grad_qkv, qkv_full, 1, 1)).astype(BF))
        parts = (
            contract(token_rows, grad_qkv, 0, 0),
            contract(attn_low, grad_branch, 0, 0),
            contract(first_low, grad_hidden_low, 0, 0),
            contract(act_low, grad_down_low, 0, 0),
            column_sums[:D],
            column_sums[2 * D :],
            jnp.sum(grad_branch.astype(F32), 0),
            jnp.sum(grad_first * normed_one, 0),
            jnp.sum(grad_first, 0),
            jnp.sum(grad_hidden_low.astype(F32), 0),
            jnp.sum(grad_down_low.astype(F32), 0),
            jnp.sum(cot_rows * normed_two, 0),
            jnp.sum(cot_rows, 0),
        )
        totals = parts if totals is None else tuple(a + b for a, b in zip(totals, parts))
    shares = tuple(
        lax.psum_scatter(part, ("ctx", "fsdp"), scatter_dimension=0, tiled=True) for part in totals
    )
    return (jnp.stack(mixed_list)[:, None], jnp.stack(grad_list)[:, None]) + shares


def solution(mesh):
    fits = mesh.shape["ctx"] == 8 and mesh.shape["fsdp"] == 4
    weights = (P("fsdp", None),) * 4 + (P("fsdp"),) * 9
    owners = (P(("ctx", "fsdp"), None),) * 4 + (P(("ctx", "fsdp")),) * 9
    rows = P(None, "fsdp", "ctx", None)
    return jax.shard_map(
        tiled_device if fits else plain_device,
        mesh=mesh,
        in_specs=(rows, rows, P(None, "fsdp", None), P(None, "fsdp", None)) + weights,
        out_specs=(rows, rows) + owners,
        check_vma=False,
    )
```

```python
from functools import partial
import math

import jax
import jax.numpy as jnp
from jax import lax
from jax.experimental import pallas as pl
from jax.experimental.pallas import tpu as pltpu
from jax.sharding import PartitionSpec as P

D = 1024
H = 16
HD = 64
BLK = 128
MB = 2

NEGATIVE = -1e30
EPSILON = 1e-05
BF = jnp.bfloat16
F32 = jnp.float32


def contract(a, b, ca, cb):
    return lax.dot_general(a, b, (((ca,), (cb,)), ((), ())), preferred_element_type=F32)


def norm_forward(values_in, gain_vec, shift_vec):
    center = values_in - jnp.mean(values_in, -1, keepdims=True)
    inverse = lax.rsqrt(jnp.mean(center * center, -1, keepdims=True) + EPSILON)
    normed = center * inverse
    return (normed * gain_vec + shift_vec, normed, inverse)


def norm_backward(grad_out, normed, inverse, gain_vec):
    grad_norm = grad_out * gain_vec
    return inverse * (
        grad_norm
        - jnp.mean(grad_norm, -1, keepdims=True)
        - normed * jnp.mean(grad_norm * normed, -1, keepdims=True)
    )


def hop(value, mask):
    count = lax.axis_size("ctx")
    return lax.ppermute(value, "ctx", [(i, i ^ mask) for i in range(count)])


VMEM = pl.BlockSpec(memory_space=pltpu.VMEM)
SMEM = pl.BlockSpec(memory_space=pltpu.SMEM)
HBM = pl.BlockSpec(memory_space=pltpu.HBM)


def takes(microseconds):
    return pl.CostEstimate(
        flops=int(microseconds * 1.15e9), bytes_accessed=1 << 20, transcendentals=0
    )


def params(mib):
    return pltpu.CompilerParams(vmem_limit_bytes=mib << 20)


def struct(shape, dtype):
    return jax.ShapeDtypeStruct(shape, dtype)


ME, LOW, TOP, SHARD, CORE, CHIP, SPLIT, ORDER, INVERSE = 0, 1, 2, 3, 7, 8, 9, 10, 26
CHUNKS = (0, 4, 2, 6, 1, 5, 3, 7)
ROWS = 512


def scalars(order, lengths):
    me = lax.axis_index("ctx")
    shard = lax.axis_index("fsdp")
    core, low, top = me % 2, me % 4, me // 4
    order_row = jnp.where(top == 0, order[0, 0], order[1, 0])
    first = jnp.where(top == 0, lengths[0, 0, 0], lengths[1, 0, 0])
    blocks = jnp.arange(16, dtype=jnp.int32)
    inverse = jnp.sum(jnp.where(order_row[None, :] == blocks[:, None], blocks[None, :], 0), 1)
    others = [(shard + 4 - k) % 4 for k in (1, 2, 3)]
    return jnp.concatenate(
        [jnp.stack([me, low, top, shard, *others, core, me // 2, first]), order_row, inverse]
    ).astype(jnp.int32)


def start_all(copies):
    for copy in copies:
        copy.start()


def wait_all(copies):
    for copy in copies:
        copy.wait()


def copies_of(pairs, sems, base=0):
    return [
        pltpu.make_async_copy(a, b, sems.at[base + i]) for i, (a, b) in enumerate(pairs)
    ]


def aligned(start, size):
    return pl.ds(pl.multiple_of(start, size), size)


def segment_lanes(first, rows, split, is_query):
    position = first + lax.broadcasted_iota(jnp.int32, (rows, HD), 0)
    lane = lax.broadcasted_iota(jnp.int32, (rows, HD), 1)
    second = (position >= split).astype(jnp.int32)
    if is_query:
        return jnp.where(lane == 1 - second, NEGATIVE, 0.0).astype(BF)
    return jnp.where(lane == second, 1.0, 0.0).astype(BF)


def key_range(q0, bq, split, bk, total):
    begin = jnp.where(q0 >= split, split // bk, 0)
    end = jnp.where(q0 + bq <= split, (split + bk - 1) // bk, total // bk)
    return begin, end


def widen(scal, qkv, qa, ka, begin, heads, chunk):
    total = qkv.shape[0]
    width = qkv.shape[1] // 3
    split = scal[SPLIT]
    for m in range(total // chunk):
        pos = pl.multiple_of((scal[ME] ^ CHUNKS[m]) * chunk, chunk)
        rows = slice(m * chunk, (m + 1) * chunk)
        qtail = segment_lanes(pos, chunk, split, True)
        ktail = segment_lanes(pos, chunk, split, False)
        for h in range(heads):
            at = begin + h * HD
            q = qkv[rows, at : at + HD]
            k = qkv[rows, width + at : width + at + HD]
            q = (q.astype(F32) * 0.125).astype(BF)
            qa[h, pl.ds(pos, chunk), :] = jnp.concatenate([q, qtail], 1)
            ka[h, pl.ds(pos, chunk), :] = jnp.concatenate([k, ktail], 1)


def attention_forward_kernel(
    scal, qkv, out0, out1, out2, out3, out_t, lse, qa, ka, vt, sc, out, *, heads, chunk, bq, bk
):
    total = qkv.shape[0]
    width = qkv.shape[1] // 3
    split = scal[SPLIT]
    widen(scal, qkv, qa, ka, 0, heads, chunk)
    for m in range(total // chunk):
        pos = pl.multiple_of((scal[ME] ^ CHUNKS[m]) * chunk, chunk)
        rows = slice(m * chunk, (m + 1) * chunk)
        vt[:, pl.ds(pos, chunk)] = qkv[rows, 2 * width :].T

    def q_step(qi, _):
        q0 = pl.multiple_of(qi * bq, bq)
        begin_k, end_k = key_range(q0, bq, split, bk, total)

        def max_step(ki, carry):
            k0 = pl.multiple_of(ki * bk, bk)
            result = []
            for h in range(heads):
                st = contract(ka[h, pl.ds(k0, bk), :], qa[h, pl.ds(q0, bq), :], 1, 1)
                sc[h, pl.ds(k0, bk), :] = st
                result.append(jnp.maximum(carry[h], jnp.max(st.reshape(bk // 8, 8, bq), 0)))
            return tuple(result)

        start = tuple(jnp.full((8, bq), NEGATIVE, F32) for _ in range(heads))
        peaks = lax.fori_loop(begin_k, end_k, max_step, start)
        peaks = [jnp.max(m, 0, keepdims=True) for m in peaks]

        def k_step(ki, carry):
            k0 = pl.multiple_of(ki * bk, bk)
            result = []
            for h in range(heads):
                total_p, acc = carry[2 * h : 2 * h + 2]
                p = jnp.exp(sc[h, pl.ds(k0, bk), :] - peaks[h])
                total_p = total_p + jnp.sum(p.reshape(bk // 8, 8, bq), 0)
                acc = acc + contract(
                    vt[h * HD : (h + 1) * HD, pl.ds(k0, bk)], p.astype(BF), 1, 0
                )
                result += [total_p, acc]
            return tuple(result)

        start = []
        for h in range(heads):
            start += [jnp.zeros((8, bq), F32), jnp.zeros((HD, bq), F32)]
        done = lax.fori_loop(begin_k, end_k, k_step, tuple(start))
        pieces = []
        for h in range(heads):
            denom = jnp.sum(done[2 * h], 0, keepdims=True)
            pieces.append(done[2 * h + 1] / denom)
            lse[h : h + 1, pl.ds(q0, bq)] = peaks[h] + jnp.log(denom)
        turned = jnp.concatenate(pieces, 0)
        out_t[:, pl.ds(q0, bq)] = turned
        low_rows = turned.T.astype(BF)
        for i in range(bq // BLK):
            place = scal[INVERSE + q0 // BLK + i]
            device = place // 2
            row = ((device // 4) ^ scal[TOP]) * 256 + (place % 2) * BLK
            out[(device % 4) ^ scal[LOW], aligned(row, BLK), :] = low_rows[
                i * BLK : (i + 1) * BLK
            ]
        return 0

    lax.fori_loop(0, total // bq, q_step, 0)
    for k, sent in enumerate((out0, out1, out2, out3)):
        sent[...] = out[k]


def attention_forward(scal, qkv, chunk, bq=512, bk=512):
    total = qkv.shape[0]
    width = qkv.shape[1] // 3
    heads = width // HD
    return pl.pallas_call(
        partial(attention_forward_kernel, heads=heads, chunk=chunk, bq=bq, bk=bk),
        out_shape=(struct((ROWS, width), BF),) * 4
        + (struct((width, total), F32), struct((heads, total), F32)),
        in_specs=[SMEM, VMEM],
        out_specs=(VMEM,) * 6,
        scratch_shapes=[
            pltpu.VMEM((heads, total, 128), BF),
            pltpu.VMEM((heads, total, 128), BF),
            pltpu.VMEM((width, total), BF),
            pltpu.VMEM((heads, total, bq), F32),
            pltpu.VMEM((4, ROWS, width), BF),
        ],
        compiler_params=params(60),
        cost_estimate=takes(23),
        name="attention_forward",
    )(scal, qkv)


def attention_backward_kernel(
    scal, qkv, grad0, grad1, grad2, grad3, out_t, lse, dqkv, qa, ka, kt, va, ga, gt, dkv, dq,
    *, first, heads, chunk, bq, bk
):
    total = qkv.shape[0]
    width = qkv.shape[1] // 3
    begin = first * HD
    end = begin + heads * HD
    split = scal[SPLIT]
    blank = jnp.zeros((chunk, HD), BF)
    short = jnp.zeros((BLK, HD), BF)
    widen(scal, qkv, qa, ka, begin, heads, chunk)
    for m in range(total // chunk):
        pos = pl.multiple_of((scal[ME] ^ CHUNKS[m]) * chunk, chunk)
        rows = slice(m * chunk, (m + 1) * chunk)
        for h in range(heads):
            at = 2 * width + begin + h * HD
            va[h, pl.ds(pos, chunk), :] = jnp.concatenate([qkv[rows, at : at + HD], blank], 1)
        kt[:, pl.ds(pos, chunk)] = qkv[rows, width + begin : width + end].T
    for k, grad in enumerate((grad0, grad1, grad2, grad3)):
        for e in range(4):
            device = (scal[LOW] ^ k) + 4 * ((e // 2) ^ scal[TOP])
            pos = pl.multiple_of(scal[ORDER + 2 * device + e % 2] * BLK, BLK)
            rows = slice(e * BLK, (e + 1) * BLK)
            for h in range(heads):
                g = grad[rows, begin + h * HD : begin + (h + 1) * HD]
                ga[h, pl.ds(pos, BLK), :] = jnp.concatenate([g, short], 1)
            gt[:, pl.ds(pos, BLK)] = grad[rows, begin:end].T
    dkv[...] = jnp.zeros_like(dkv)

    def q_step(qi, _):
        q0 = pl.multiple_of(qi * bq, bq)
        begin_k, end_k = key_range(q0, bq, split, bk, total)
        product = gt[:, pl.ds(q0, bq)].astype(F32) * out_t[begin:end, pl.ds(q0, bq)]
        delta = [jnp.sum(product[h * HD : (h + 1) * HD], 0, keepdims=True) for h in range(heads)]
        held_lse = lse[:, pl.ds(q0, bq)]
        totals = [held_lse[first + h : first + h + 1] for h in range(heads)]

        def k_step(ki, carry):
            k0 = pl.multiple_of(ki * bk, bk)
            result = []
            for h in range(heads):
                q = qa[h, pl.ds(q0, bq), :]
                g = ga[h, pl.ds(q0, bq), :]
                st = contract(ka[h, pl.ds(k0, bk), :], q, 1, 1)
                p = jnp.exp(st - totals[h])
                dp = contract(va[h, pl.ds(k0, bk), :], g, 1, 1)
                ds = (p * (dp - delta[h]) * 0.125).astype(BF)
                dkv[0, h, pl.ds(k0, bk), :] += contract(ds, q, 1, 0)
                dkv[1, h, pl.ds(k0, bk), :] += contract(p.astype(BF), g, 1, 0)
                result.append(
                    carry[h] + contract(kt[h * HD : (h + 1) * HD, pl.ds(k0, bk)], ds, 1, 0)
                )
            return tuple(result)

        start = tuple(jnp.zeros((HD, bq), F32) for _ in range(heads))
        turned = lax.fori_loop(begin_k, end_k, k_step, start)
        dq[pl.ds(q0, bq), :] = jnp.concatenate(turned, 0).T.astype(BF)
        return 0

    lax.fori_loop(0, total // bq, q_step, 0)
    for m in range(total // chunk):
        pos = pl.multiple_of((scal[ME] ^ CHUNKS[m]) * chunk, chunk)
        rows = slice(m * chunk, (m + 1) * chunk)
        dqkv[rows, 0 : heads * HD] = dq[pl.ds(pos, chunk), :]
        for h in range(0, heads, 2):
            for part, gain in ((0, 8.0), (1, 1.0)):
                pair = [dkv[part, h + e, pl.ds(pos, chunk), :][:, :HD] for e in range(2)]
                base = ((1 + part) * heads + h) * HD
                dqkv[rows, base : base + 2 * HD] = (jnp.concatenate(pair, 1) * gain).astype(BF)


def attention_backward(scal, qkv, grads, out_t, lse, chunk, first, heads, bq=512, bk=512):
    total = qkv.shape[0]
    width = heads * HD
    wide = pltpu.VMEM((heads, total, 128), BF)
    return pl.pallas_call(
        partial(
            attention_backward_kernel, first=first, heads=heads, chunk=chunk, bq=bq, bk=bk
        ),
        out_shape=struct((total, 3 * width), BF),
        in_specs=[SMEM] + [VMEM] * 7,
        out_specs=VMEM,
        scratch_shapes=[
            wide,
            wide,
            pltpu.VMEM((width, total), BF),
            wide,
            wide,
            pltpu.VMEM((width, total), BF),
            pltpu.VMEM((2, heads, total, 128), F32),
            pltpu.VMEM((total, width), BF),
        ],
        compiler_params=params(60),
        cost_estimate=takes(40),
        name="attention_backward",
    )(scal, qkv, *grads, out_t, lse)


def carve_kernel(
    tokens, cot, w_qkv, w_out, w_up, w_down, small,
    own, other, cot_own, cot_other, pack, pack_sent, up_slice, down_slice, sems,
):
    me = lax.axis_index("ctx")
    core, low, top, chip = me % 2, me % 4, me // 4, me // 2
    block = core * 4 + chip
    pairs = [(tokens.at[top, 0], own), (tokens.at[1 - top, 0], other)]
    half = aligned(top * 128, 128)
    for k in range(3):
        columns = aligned(k * D + low * 256, 256)
        target = slice(256 * k, 256 * (k + 1))
        pairs.append((w_qkv.at[:, columns], pack.at[:, target]))
        pairs.append((w_qkv.at[half, columns], pack_sent.at[0:128, target]))
    for k in range(4):
        columns = aligned(k * D + block * 128, 128)
        pairs.append((w_up.at[:, columns], up_slice.at[:, 128 * k : 128 * (k + 1)]))
    pairs.append((w_out.at[:, aligned(block * 128, 128)], up_slice.at[:, 512:640]))
    pairs.append((w_down.at[aligned(core * 512 + top * 128, 128), :], down_slice.at[0]))
    side = core * 512 + 256 + (chip % 2) * 128
    pairs.append((w_down.at[aligned(side, 128), :], down_slice.at[1]))
    pairs += [(cot.at[top, 0], cot_own), (cot.at[1 - top, 0], cot_other)]
    copies = copies_of(pairs, sems)
    start_all(copies)
    pack_sent[128:144, 0:256] = small[...]
    wait_all(copies)


def carve(tokens, cot, w_qkv, w_out, w_up, w_down, small):
    rows = tokens.shape[2]
    return pl.pallas_call(
        carve_kernel,
        out_shape=tuple(struct((rows, D), BF) for _ in range(4))
        + (
            struct((256, 768), BF),
            struct((144, 768), BF),
            struct((256, 640), BF),
            struct((2, 128, D), BF),
        ),
        in_specs=[HBM] * 6 + [VMEM],
        out_specs=(VMEM,) * 8,
        scratch_shapes=[pltpu.SemaphoreType.DMA((17,))],
        compiler_params=params(60),
        cost_estimate=takes(4),
        name="carve",
    )(tokens, cot, w_qkv, w_out, w_up, w_down, small)


def project_kernel(
    scal, pack, small, near, away, own, y, x, core_own, core_rest,
    qkv, x_all, weight, vecs, up_bias, qkv_held, x_held, rows_held, sems, out_sems,
):
    chunk = own.shape[0]
    own_f = scal[SHARD]
    pairs = [(pack, weight.at[aligned(own_f * 256, 256)]), (small, rows_held.at[own_f])]
    for k in range(3):
        f = scal[SHARD + 1 + k]
        mine = aligned(f * 256 + scal[TOP] * 128, 128)
        rest = aligned(f * 256 + (1 - scal[TOP]) * 128, 128)
        pairs.append((near.at[k, 0:128], weight.at[mine]))
        pairs.append((away.at[k, 0:128], weight.at[rest]))
        pairs.append((near.at[k, 128:144, 0:256], rows_held.at[f]))
    loads = len(pairs)
    sources = [own, y, x.at[0], x.at[1], core_own] + [core_rest.at[k] for k in range(3)]
    pairs += [
        (piece, x_held.at[m * chunk : (m + 1) * chunk]) for m, piece in enumerate(sources)
    ]
    copies = copies_of(pairs, sems)
    start_all(copies)
    wait_all(copies[:loads])
    for f in range(4):
        held = rows_held[f].astype(F32)
        vecs[:, 256 * f : 256 * (f + 1)] = held[0:8]
        for j in range(4):
            for e in range(2):
                up_bias[2 * j + e : 2 * j + e + 1, 128 * f : 128 * (f + 1)] = held[
                    8 + j : 9 + j, 128 * e : 128 * (e + 1)
                ]
    here = aligned(scal[LOW] * 256, 256)
    bias = jnp.concatenate([vecs[0:1, here], jnp.zeros((1, 256), F32), vecs[1:2, here]], 1)
    outs = []
    for m in range(8):
        copies[loads + m].wait()
        rows = slice(m * chunk, (m + 1) * chunk)
        qkv_held[rows, :] = (contract(x_held[rows, :], weight[...], 1, 0) + bias).astype(BF)
        sent = copies_of(
            [(x_held.at[rows], x_all.at[rows]), (qkv_held.at[rows], qkv.at[rows])], out_sems, 2 * m
        )
        start_all(sent)
        outs += sent
    wait_all(outs)


def project(scal, pack, small, near, away, pieces):
    chunk = pieces[0].shape[0]
    return pl.pallas_call(
        project_kernel,
        out_shape=(
            struct((8 * chunk, 768), BF),
            struct((8 * chunk, D), BF),
            struct((D, 768), BF),
            struct((8, D), F32),
            struct((8, 512), F32),
        ),
        in_specs=[SMEM] + [HBM] * 9,
        out_specs=(HBM, HBM, VMEM, VMEM, VMEM),
        scratch_shapes=[
            pltpu.VMEM((8 * chunk, 768), BF),
            pltpu.VMEM((8 * chunk, D), BF),
            pltpu.VMEM((4, 16, 256), BF),
            pltpu.SemaphoreType.DMA((19,)),
            pltpu.SemaphoreType.DMA((16,)),
        ],
        compiler_params=params(60),
        cost_estimate=takes(8),
        name="project",
    )(scal, pack, small, near, away, *pieces)


def out_pairs(scal, near, away, w_out, held):
    pairs = []
    for side, pieces in enumerate((near, away)):
        for m in range(4):
            block = 4 * (scal[CORE] ^ side) + (scal[CHIP] ^ m)
            for k in range(3):
                rows = aligned(scal[SHARD + 1 + k] * 256, 256)
                pairs.append((pieces.at[m, k], held.at[block, rows]))
            columns = aligned(block * 128, 128)
            rows = aligned(scal[SHARD] * 256, 256)
            pairs.append((w_out.at[:, columns], held.at[block, rows]))
    return pairs


def attention_out_kernel(
    scal, h0, h1, h2, h3, vecs, x_all, w_out, near, away, y1, y1_low, n1, r1, held, x, sems
):
    pairs = out_pairs(scal, near, away, w_out, held)
    for e in range(4):
        device = scal[ME] ^ (4 * (e // 2))
        given = scal[ORDER + 2 * device + e % 2]
        turn = scal[ME] ^ (given // 2)
        chunk = (turn % 2) * 4 + ((turn // 2) % 2) * 2 + turn // 4
        rows = aligned(chunk * 256 + (given % 2) * BLK, BLK)
        pairs.append((x_all.at[rows, :], x.at[e * BLK : (e + 1) * BLK]))
    copies = copies_of(pairs, sems)
    start_all(copies)
    wait_all(copies)
    columns = []
    for b in range(8):
        part = 0.0
        for k, heads in enumerate((h0, h1, h2, h3)):
            rows = aligned((scal[LOW] ^ k) * 256, 256)
            part = part + contract(heads[...], held[b, rows, :], 1, 0)
        columns.append(part)
    into = x[...].astype(F32) + jnp.concatenate(columns, 1) + vecs[2:3]
    out, normed, inverse = norm_forward(into, vecs[3:4], vecs[4:5])
    y1[...] = out
    y1_low[...] = out.astype(BF)
    n1[...] = normed
    r1[...] = jnp.broadcast_to(inverse, r1.shape)


def attention_out(scal, heads, vecs, x_all, w_out, near, away):
    return pl.pallas_call(
        attention_out_kernel,
        out_shape=(
            struct((ROWS, D), F32),
            struct((ROWS, D), BF),
            struct((ROWS, D), F32),
            struct((ROWS, 128), F32),
        ),
        in_specs=[SMEM] + [VMEM] * 5 + [HBM] * 4,
        out_specs=(VMEM,) * 4,
        scratch_shapes=[
            pltpu.VMEM((8, D, 128), BF),
            pltpu.VMEM((ROWS, D), BF),
            pltpu.SemaphoreType.DMA((36,)),
        ],
        compiler_params=params(60),
        cost_estimate=takes(9),
        name="attention_out",
    )(scal, *heads, vecs, x_all, w_out, near, away)


def up_pairs(scal, pieces, w_up, held):
    own, from_x, from_y, far_a, far_b = pieces
    groups = [[] for _ in range(4)]
    for k in range(3):
        base = scal[SHARD + 1 + k] * 256
        for m, piece in enumerate((own, from_x, from_y)):
            target = held.at[scal[CHIP] ^ m, aligned(base, 256)]
            groups[m].append((piece.at[k, :, 0:512], target))
        for half, piece in enumerate((far_a, far_b)):
            target = held.at[scal[CHIP] ^ 3, aligned(base + 128 * half, 128)]
            groups[3].append((piece.at[k, :, 0:512], target))
    rows = aligned(scal[SHARD] * 256, 256)
    for m in range(4):
        chip = scal[CHIP] ^ m
        for k in range(4):
            columns = aligned(k * D + (scal[CORE] * 4 + chip) * 128, 128)
            target = held.at[chip, rows, 128 * k : 128 * (k + 1)]
            groups[m].append((w_up.at[:, columns], target))
    return groups


UP_COPIES = 3 * 7 + 10


def grouped_copies(groups, sems, base=0):
    result = []
    for group in groups:
        result.append(copies_of(group, sems, base))
        base += len(group)
    return result


def down_pairs(scal, own, from_y, from_x, held):
    side = scal[CHIP] % 2
    pairs = []
    for f in range(4):
        rows = slice(128 * f, 128 * (f + 1))
        pairs.append((own.at[f, 0], held.at[scal[TOP], rows]))
        pairs.append((own.at[f, 1], held.at[2 + side, rows]))
        pairs.append((from_y.at[f], held.at[1 - scal[TOP], rows]))
        pairs.append((from_x.at[f], held.at[3 - side, rows]))
    return pairs


DOWN_COPIES = 16


def up_kernel(scal, y1_low, up_bias, w_up, *rest):
    pieces, (act, slope, held, act_held, slope_held, sems, out_sems) = rest[:5], rest[5:]
    groups = grouped_copies(up_pairs(scal, pieces, w_up, held), sems)
    for group in groups:
        start_all(group)
    outs = []
    for m, group in enumerate(groups):
        wait_all(group)
        q = scal[CHIP] ^ m
        bias = up_bias[pl.ds(scal[CORE] * 4 + q, 1), :]
        for r in (slice(0, 256), slice(256, 512)):
            u = contract(y1_low[r, :], held[q], 1, 0) + bias
            cdf = 0.5 * (1.0 + lax.erf(u * (1.0 / math.sqrt(2.0))))
            density = jnp.exp(-0.5 * u * u) * (1.0 / math.sqrt(2.0 * math.pi))
            slope_held[q, r, :] = (cdf + u * density).astype(BF)
            act_held[q, r, :] = (u * cdf).astype(BF)
        copies = copies_of(
            [(act_held.at[q], act.at[q]), (slope_held.at[q], slope.at[q])], out_sems, 2 * m
        )
        start_all(copies)
        outs += copies
    wait_all(outs)


def feed_up(scal, y1_low, up_bias, w_up, pieces):
    block = pltpu.VMEM((4, ROWS, 512), BF)
    return pl.pallas_call(
        up_kernel,
        out_shape=(struct((4, ROWS, 512), BF), struct((4, ROWS, 512), BF)),
        in_specs=[SMEM, VMEM, VMEM] + [HBM] * 6,
        out_specs=(HBM, HBM),
        scratch_shapes=[
            pltpu.VMEM((4, D, 512), BF),
            block,
            block,
            pltpu.SemaphoreType.DMA((UP_COPIES,)),
            pltpu.SemaphoreType.DMA((8,)),
        ],
        compiler_params=params(60),
        cost_estimate=takes(7),
        name="feed_up",
    )(scal, y1_low, up_bias, w_up, *pieces)


def down_kernel(scal, act, own, from_y, from_x, part, held, act_held, total, sems):
    pairs = down_pairs(scal, own, from_y, from_x, held)
    copies = copies_of(pairs, sems)
    acts = copies_of([(act.at[q], act_held.at[q]) for q in range(4)], sems, DOWN_COPIES)
    start_all(copies)
    start_all(acts)
    wait_all(copies)
    for q in range(4):
        acts[q].wait()
        moved = contract(act_held[q], held[q], 1, 0)
        if q == 0:
            total[...] = moved
        elif q < 3:
            total[...] += moved
        else:
            part[...] = (total[...] + moved).astype(part.dtype)


def feed_down(scal, act, pieces, dtype):
    return pl.pallas_call(
        down_kernel,
        out_shape=struct((ROWS, D), dtype),
        in_specs=[SMEM] + [HBM] * 4,
        out_specs=VMEM,
        scratch_shapes=[
            pltpu.VMEM((4, 512, D), BF),
            pltpu.VMEM((4, ROWS, 512), BF),
            pltpu.VMEM((ROWS, D), F32),
            pltpu.SemaphoreType.DMA((DOWN_COPIES + 4,)),
        ],
        compiler_params=params(60),
        cost_estimate=takes(5),
        name="feed_down",
    )(scal, act, *pieces)


def second_norm_kernel(y1, part, came, cot_own, cot_came, vecs, out_own, out_away, dh2, dz2, sums):
    n = pl.program_id(0)
    h2 = y1[...] + part[...] + came[...].astype(F32) + vecs[5:6]
    out, normed, inverse = norm_forward(h2, vecs[6:7], vecs[7:8])
    out = out.astype(BF)
    c = jnp.where(n < 2, cot_own[...], cot_came[...]).astype(F32)
    grad = norm_backward(c, normed, inverse, vecs[6:7])
    dh2[...] = grad
    low = grad.astype(BF)
    dz2[...] = low

    @pl.when(n == 0)
    def _():
        sums[...] = jnp.zeros_like(sums)

    for i, value in enumerate((c * normed, c, low.astype(F32))):
        sums[i : i + 1, :] += jnp.sum(value, 0, keepdims=True)

    @pl.when(n < 2)
    def _():
        out_own[...] = out

    @pl.when(n >= 2)
    def _():
        out_away[...] = out


def second_norm(y1, part, came, cot_own, cot_came, vecs):
    half = struct((ROWS // 2, D), BF)
    rows = pl.BlockSpec((128, D), lambda n: (n, 0))
    first = pl.BlockSpec((128, D), lambda n: (jnp.minimum(n, 1), 0))
    last = pl.BlockSpec((128, D), lambda n: (jnp.maximum(n - 2, 0), 0))
    whole = pl.BlockSpec((8, D), lambda n: (0, 0))
    return pl.pallas_call(
        second_norm_kernel,
        grid=(4,),
        out_shape=(half, half, struct((ROWS, D), F32), struct((ROWS, D), BF), struct((8, D), F32)),
        in_specs=[rows, rows, rows, first, last, whole],
        out_specs=(first, last, rows, rows, whole),
        compiler_params=params(60),
        cost_estimate=takes(4),
        name="second_norm",
    )(y1, part, came, cot_own, cot_came, vecs)


def back_kernel(scal, dz2_a, dz2_b, slope_a, slope_b, w_up, *rest):
    ups, downs, outs, scratch = rest[:5], rest[5:8], rest[8:13], rest[13:]
    du_a, du_b, part_a, part_b, up_sums = outs
    up_held, down_held, slopes, dus, acc_a, acc_b, sems, out_sems = scratch
    down_copies = copies_of(down_pairs(scal, *downs, down_held), sems)
    groups = grouped_copies(up_pairs(scal, ups, w_up, up_held), sems, DOWN_COPIES)
    loads = []
    for m in range(4):
        q = scal[CHIP] ^ m
        pairs = [(slope_b.at[q], slopes.at[1, q]), (slope_a.at[q], slopes.at[0, q])]
        loads.append(copies_of(pairs, sems, DOWN_COPIES + UP_COPIES + 2 * m))
    start_all(down_copies)
    for group, load in zip(groups, loads):
        start_all(load)
        start_all(group)
    wait_all(down_copies)
    sent = []
    for m in range(4):
        wait_all(loads[m])
        wait_all(groups[m])
        q = scal[CHIP] ^ m
        total = jnp.zeros((1, 512), F32)
        for side, (dz2, du, acc) in enumerate(((dz2_a, du_a, acc_a), (dz2_b, du_b, acc_b))):
            for r in (slice(0, 256), slice(256, 512)):
                low = contract(dz2[r, :], down_held[q], 1, 1) * slopes[side, q, r, :].astype(F32)
                low = low.astype(BF)
                dus[side, q, r, :] = low
                total = total + jnp.sum(low.astype(F32), 0, keepdims=True)
                moved = contract(low, up_held[q], 1, 1)
                if m == 0:
                    acc[r, :] = moved
                else:
                    acc[r, :] += moved
            copies = copies_of([(dus.at[side, q], du.at[q])], out_sems, 2 * m + side)
            start_all(copies)
            sent += copies
        up_sums[pl.ds(q, 1), :] = total
    part_a[...] = acc_a[...]
    part_b[...] = acc_b[...].astype(BF)
    wait_all(sent)


def feed_back(scal, dz2s, slopes, w_up, ups, downs):
    du = struct((4, ROWS, 512), BF)
    return pl.pallas_call(
        back_kernel,
        out_shape=(
            du, du, struct((ROWS, D), F32), struct((ROWS, D), BF), struct((8, 512), F32)
        ),
        in_specs=[SMEM, VMEM, VMEM] + [HBM] * 11,
        out_specs=(HBM, HBM, VMEM, VMEM, VMEM),
        scratch_shapes=[
            pltpu.VMEM((4, D, 512), BF),
            pltpu.VMEM((4, 512, D), BF),
            pltpu.VMEM((2, 4, ROWS, 512), BF),
            pltpu.VMEM((2, 4, ROWS, 512), BF),
            pltpu.VMEM((ROWS, D), F32),
            pltpu.VMEM((ROWS, D), F32),
            pltpu.SemaphoreType.DMA((DOWN_COPIES + UP_COPIES + 8,)),
            pltpu.SemaphoreType.DMA((8,)),
        ],
        compiler_params=params(60),
        cost_estimate=takes(22),
        name="feed_back",
    )(scal, *dz2s, *slopes, w_up, *ups, *downs)


def first_norm_kernel(
    scal, dh2, part, came, n1, r1, vecs, w_out, near, away, dao, g0, g1, g2, g3, sums, held, sems
):
    copies = copies_of(out_pairs(scal, near, away, w_out, held), sems)
    start_all(copies)
    dy1 = dh2[...] + part[...] + came[...].astype(F32)
    normed = n1[...]
    low = norm_backward(dy1, normed, r1[:, 0:1], vecs[3:4]).astype(BF)
    dao[...] = low
    sums[0:1, :] = jnp.sum(dy1 * normed, 0, keepdims=True)
    sums[1:2, :] = jnp.sum(dy1, 0, keepdims=True)
    sums[2:3, :] = jnp.sum(low.astype(F32), 0, keepdims=True)
    wait_all(copies)
    for k, out in enumerate((g0, g1, g2, g3)):
        rows = aligned((scal[LOW] ^ k) * 256, 256)
        total = 0.0
        for b in range(0, 8, 2):
            weight = jnp.concatenate([held[b, rows, :], held[b + 1, rows, :]], 1)
            total = total + contract(dao[:, b * 128 : (b + 2) * 128], weight, 1, 1)
        out[...] = total.astype(BF)


def first_norm(scal, dh2, part, came, n1, r1, vecs, w_out, near, away):
    return pl.pallas_call(
        first_norm_kernel,
        out_shape=(struct((ROWS, D), BF),) + (struct((ROWS, 256), BF),) * 4 + (struct((8, D), F32),),
        in_specs=[SMEM] + [VMEM] * 6 + [HBM] * 3,
        out_specs=(VMEM,) * 6,
        scratch_shapes=[pltpu.VMEM((8, D, 128), BF), pltpu.SemaphoreType.DMA((32,))],
        compiler_params=params(60),
        cost_estimate=takes(7),
        name="first_norm",
    )(scal, dh2, part, came, n1, r1, vecs, w_out, near, away)


def split_write(n, block, a_keep, a_send, b_keep, b_send):
    half = a_keep.shape[1]
    top_rows, low_rows = block[:half], block[half:]
    for step in range(4):

        @pl.when(n == step)
        def _():
            (a_send if step in (1, 3) else a_keep)[0] = top_rows
            (b_send if step in (2, 3) else b_keep)[0] = low_rows


def split_specs(rows, columns):
    half = (1, rows // 2, columns)
    return (
        pl.BlockSpec(half, lambda n, s: (n // 2, 0, 0)),
        pl.BlockSpec(half, lambda n, s: (n // 2, 0, 0)),
        pl.BlockSpec(half, lambda n, s: (jnp.minimum(n, 1), 0, 0)),
        pl.BlockSpec(half, lambda n, s: (jnp.maximum(n - 2, 0), 0, 0)),
    )


def split_shapes(rows, columns):
    return (struct((2, rows // 2, columns), BF),) * 4


def down_grad_kernel(scal, act_a, act_b, dz2_a, dz2_b, *outs):
    left = [jnp.concatenate([act[f] for f in range(4)], 1) for act in (act_a, act_b)]
    rows = contract(left[0], dz2_a[...], 0, 0) + contract(left[1], dz2_b[...], 0, 0)
    split_write(pl.program_id(0), rows.astype(BF), *outs)


def down_grad(scal, acts, dz2s):
    act_spec = pl.BlockSpec((4, ROWS, 128), lambda n, s: (0, 0, s[CHIP] ^ n))
    dz2_spec = pl.BlockSpec((ROWS, D), lambda n, s: (0, 0))
    return pl.pallas_call(
        down_grad_kernel,
        out_shape=split_shapes(512, D),
        grid_spec=pltpu.PrefetchScalarGridSpec(
            num_scalar_prefetch=1,
            grid=(4,),
            in_specs=[act_spec, act_spec, dz2_spec, dz2_spec],
            out_specs=split_specs(512, D),
        ),
        compiler_params=params(60),
        cost_estimate=takes(11),
        name="down_grad",
    )(scal, *acts, *dz2s)


OUT_WIDTH = 1024 + 128
UP_WIDTH = 4096 + 1024 + 128


def up_parts(y1_a, y1_b, du_a, du_b):
    return [
        contract(y1_a[...], du_a[q], 0, 0) + contract(y1_b[...], du_b[q], 0, 0) for q in range(4)
    ]


def up_grad_other_kernel(scal, y1_a, y1_b, du_a, du_b, out, left):
    @pl.when(pl.program_id(0) == 0)
    def _():
        for side, y1 in enumerate((y1_a, y1_b)):
            for n in range(4):
                row = 2 * (scal[CHIP] ^ n) + 1 - scal[CORE]
                left[side, :, 128 * n : 128 * (n + 1)] = y1[:, aligned(row * 128, 128)]

    rows = contract(left[0], du_a[0], 0, 0) + contract(left[1], du_b[0], 0, 0)
    for n in range(4):
        out[n] = rows[128 * n : 128 * (n + 1)].astype(BF)


def out_grad_other_kernel(scal, heads, dao, small, out):
    parts = [contract(heads[0], dao[...], 0, 0), small[0]]
    out[0] = jnp.concatenate(parts, 1).astype(BF)


def up_grad_own_kernel(scal, y1_a, y1_b, du_a, du_b, heads, dao, small, came, came_out, *rest):
    outs, block = rest[:4], rest[4]
    core = scal[CORE]
    own = jnp.concatenate(up_parts(y1_a, y1_b, du_a, du_b), 1).astype(BF)
    block[:, aligned(core * 2048, 2048)] = own
    block[:, aligned((1 - core) * 2048, 2048)] = came[0]
    out_rows = contract(heads[0], dao[...], 0, 0) + came_out[0, :, :1024].astype(F32)
    block[:, 4096:5120] = out_rows.astype(BF)
    block[:, 5120:] = (small[0] + came_out[0, :, 1024:].astype(F32)).astype(BF)
    split_write(pl.program_id(0), block, *outs)


def of_row(index, flip):
    return lambda n, s: index(s[CHIP] ^ n, s[CORE] ^ flip, s)


def up_specs(flip):
    y1_spec = pl.BlockSpec((ROWS, 128), of_row(lambda q, c, s: (0, 2 * q + c), flip))
    du_spec = pl.BlockSpec((4, ROWS, 512), lambda n, s: (0, 0, 0))
    return [y1_spec, y1_spec, du_spec, du_spec]


def out_specs(flip):
    return [
        pl.BlockSpec((1, ROWS, 128), of_row(lambda q, c, s: (q ^ s[LOW], 0, c), flip)),
        pl.BlockSpec((ROWS, D), lambda n, s: (0, 0)),
        pl.BlockSpec((1, 128, 128), of_row(lambda q, c, s: (2 * q + c, 0, 0), flip)),
    ]


UP_SENT = pl.BlockSpec((1, 128, 2048), lambda n, s: (n, 0, 0))
OUT_SENT = pl.BlockSpec((1, 128, OUT_WIDTH), lambda n, s: (n, 0, 0))


def up_grad_other(scal, y1s, dus):
    y1_spec = pl.BlockSpec((ROWS, D), lambda q, s: (0, 0))
    du_spec = pl.BlockSpec((1, ROWS, 512), lambda q, s: (q, 0, 0))
    return pl.pallas_call(
        up_grad_other_kernel,
        out_shape=struct((4, 128, 2048), BF),
        grid_spec=pltpu.PrefetchScalarGridSpec(
            num_scalar_prefetch=1,
            grid=(4,),
            in_specs=[y1_spec, y1_spec, du_spec, du_spec],
            out_specs=pl.BlockSpec((4, 128, 512), lambda q, s: (0, 0, q)),
            scratch_shapes=[pltpu.VMEM((2, ROWS, 512), BF)],
        ),
        compiler_params=params(60),
        cost_estimate=takes(6),
        name="up_grad_other",
    )(scal, *y1s, *dus)


def out_grad_other(scal, heads, dao, small):
    return pl.pallas_call(
        out_grad_other_kernel,
        out_shape=struct((4, 128, OUT_WIDTH), BF),
        grid_spec=pltpu.PrefetchScalarGridSpec(
            num_scalar_prefetch=1, grid=(4,), in_specs=out_specs(1), out_specs=OUT_SENT
        ),
        compiler_params=params(60),
        cost_estimate=takes(3),
        name="out_grad_other",
    )(scal, heads, dao, small)


def up_grad_own(scal, y1s, dus, heads, dao, small, came, came_out):
    return pl.pallas_call(
        up_grad_own_kernel,
        out_shape=split_shapes(128, UP_WIDTH),
        grid_spec=pltpu.PrefetchScalarGridSpec(
            num_scalar_prefetch=1,
            grid=(4,),
            in_specs=up_specs(0) + out_specs(0) + [UP_SENT, OUT_SENT],
            out_specs=split_specs(128, UP_WIDTH),
            scratch_shapes=[pltpu.VMEM((128, UP_WIDTH), BF)],
        ),
        compiler_params=params(60),
        cost_estimate=takes(10),
        name="up_grad_own",
    )(scal, *y1s, *dus, heads, dao, small, came, came_out)


def qkv_grad_kernel(scal, x, dqkv, send, keep):
    ones = jnp.ones((dqkv.shape[0], 128), BF)
    lane = lax.broadcasted_iota(jnp.int32, (256, 128), 1)
    q_sum = contract(dqkv[:, 0:256], ones, 0, 0)
    v_sum = contract(dqkv[:, 512:768], ones, 0, 0)
    extra = jnp.where(lane == 0, q_sum, jnp.where(lane == 1, v_sum, 0.0))
    for y, out in ((1 - scal[TOP], send), (scal[TOP], keep)):
        for r in range(2):
            group = 2 * y + r
            rows = contract(x[:, aligned(256 * group, 256)], dqkv[...], 0, 0)
            here = jnp.where(scal[LOW] == group, 1.0, 0.0)
            block = jnp.concatenate([rows, extra * here], 1).astype(BF)
            for e in range(2):
                for f in range(4):
                    at = 128 * e + 32 * f
                    out[f, 2 * r + e] = block[at : at + 32, :]


def qkv_grad(scal, x_all, dqkv):
    return pl.pallas_call(
        qkv_grad_kernel,
        out_shape=(struct((4, 4, 32, 896), BF),) * 2,
        in_specs=[SMEM, VMEM, VMEM],
        out_specs=(VMEM, VMEM),
        compiler_params=params(60),
        cost_estimate=takes(8),
        name="qkv_grad",
    )(scal, x_all, dqkv)


def input_grad_kernel(scal, dqkv, weight, dao, out, *, first):
    held = pl.program_id(0) + first
    total = contract(dqkv[...], weight[...], 1, 1)
    turn = (held // 4) + 2 * ((held // 2) % 2) + 4 * (held % 2)
    for e in range(2):
        place = scal[INVERSE + 2 * (scal[ME] ^ turn) + e]
        other = (place // 2) ^ scal[ME]
        mine = jnp.where((other == 0) | (other == 4), 1.0, 0.0)
        source = aligned(((other // 4) % 2) * 256 + (place % 2) * BLK, BLK)
        rows = total[BLK * e : BLK * (e + 1)]
        out[0, BLK * e : BLK * (e + 1), :] = (rows + dao[source, :].astype(F32) * mine).astype(BF)


def input_grad(scal, dqkv, weight, dao, first):
    rows = pl.BlockSpec((256, 768), lambda n, s: (n + first, 0))
    return pl.pallas_call(
        partial(input_grad_kernel, first=first),
        out_shape=struct((4, 256, D), BF),
        grid_spec=pltpu.PrefetchScalarGridSpec(
            num_scalar_prefetch=1,
            grid=(4,),
            in_specs=[
                rows,
                pl.BlockSpec((D, 768), lambda n, s: (0, 0)),
                pl.BlockSpec((ROWS, D), lambda n, s: (0, 0)),
            ],
            out_specs=pl.BlockSpec((1, 256, D), lambda n, s: (n, 0, 0)),
        ),
        compiler_params=params(60),
        cost_estimate=takes(5),
        name="input_grad",
    )(scal, dqkv, weight, dao)


def after(value, *others):
    return lax.optimization_barrier((value,) + others)[0]


def tied(*values):
    return lax.optimization_barrier(values)


def add_low(a, b):
    return (a.astype(F32) + b.astype(F32)).astype(BF)


def add_far(a_keep, b_keep, a_came, b_came):
    return hop(add_low(a_keep[1], a_came[1]), 4), hop(add_low(b_keep[1], b_came[1]), 2)


def sum_chips(a_keep, b_keep, a_came, b_came, a_next, b_next):
    a_all = a_keep[0].astype(F32) + a_came[0].astype(F32) + a_next.astype(F32)
    b_all = b_keep[0].astype(F32) + b_came[0].astype(F32) + b_next.astype(F32)
    return jnp.concatenate([a_all, b_all], 0).astype(BF)


def sum_shards(rows):
    return lax.psum_scatter(rows, "fsdp", scatter_dimension=0, tiled=True)


def tiled_device(
    tokens, cotangent, lengths, order, w_qkv, w_out, w_up, w_down, q_bias, v_bias, out_bias,
    norm1_gain, norm1_bias, up_bias, down_bias, norm2_gain, norm2_bias,
):
    me = lax.axis_index("ctx")
    core, low, top = me % 2, me % 4, me // 4
    chunk = tokens.shape[2]
    half_groups = [[0, 1, 2, 3], [4, 5, 6, 7]]
    scal = scalars(order, lengths)
    small = jnp.zeros((16, 256), BF)
    row = lax.broadcasted_iota(jnp.int32, (16, 256), 0)
    rows_of_small = [
        q_bias, v_bias, out_bias, norm1_gain, norm1_bias, down_bias, norm2_gain, norm2_bias,
    ] + [up_bias[256 * k : 256 * (k + 1)] for k in range(4)]
    for k, vector in enumerate(rows_of_small):
        small = jnp.where(row == k, vector[None, :], small)
    own_rows, other_rows, cot_own, cot_other, pack, pack_sent, up_slice, down_slice = carve(
        tokens, cotangent, w_qkv, w_out, w_up, w_down, small
    )

    def around(value):
        return [
            lax.ppermute(value, "fsdp", [(i, (i + k) % 4) for i in range(4)]) for k in (1, 2, 3)
        ]

    *pack_near, from_y = tied(*around(pack_sent), hop(other_rows, 4))
    pack_near = jnp.stack(pack_near)
    from_x, pack_away = tied(hop(jnp.stack([own_rows, from_y]), 2), hop(pack_near, 4))
    up_own = lax.all_gather(after(up_slice, from_y), "fsdp", axis=0)
    core_own = hop(own_rows, 1)
    core_rest = hop(jnp.concatenate([from_y[None], from_x], 0), 1)
    down_own = lax.all_gather(after(down_slice, from_x), "fsdp", axis=0)
    qkv, x_all, qkv_weight, vecs, up_b = project(
        scal, pack, small, pack_near, pack_away,
        (own_rows, from_y, from_x, core_own, core_rest),
    )
    up_own, qkv = tied(up_own, qkv)
    foreign = jnp.stack(
        [lax.dynamic_index_in_dim(up_own, scal[SHARD + k], 0, False) for k in (1, 2, 3)]
    )
    up_x, up_y = hop(foreign, 2), hop(foreign, 4)
    out_far = hop(foreign[:, :, 512:], 6)
    *sent, turned, lse = attention_forward(scal, after(qkv, foreign), chunk)
    up_x, up_y, out_far, *sent = tied(up_x, up_y, out_far, *sent)
    near = jnp.stack([piece[:, :, 512:] for piece in (foreign, up_x, up_y)] + [out_far])
    away, cot_came, *came_heads = tied(
        hop(near, 1), hop(after(cot_other, sent[0]), 4), *[hop(sent[k], k) for k in (1, 2, 3)]
    )
    heads = [sent[0], *came_heads]
    far_a, far_b = hop(after(up_y, away)[:, :128], 2), hop(after(up_x, away)[:, 128:], 4)
    ups = (foreign, up_x, up_y, far_a, far_b)
    y1, y1_low, n1, r1 = attention_out(scal, heads, vecs, x_all, w_out, near, away)
    y1, y1_low, n1, r1, far_a, far_b = tied(y1, y1_low, n1, r1, far_a, far_b)
    ups = (foreign, up_x, up_y, far_a, far_b)

    down_own = after(down_own, far_a, far_b)
    down_y, down_x = hop(down_own[:, 0], 4), hop(down_own[:, 1], 2)
    y1_away = hop(y1_low, 1)
    act, slope = feed_up(scal, y1_low, up_b, w_up, ups)
    act, slope, y1_away = tied(act, slope, y1_away)
    act_away, slope_away = feed_up(scal, y1_away, up_b, w_up, ups)
    act_away, slope_away, down_x, down_y = tied(act_away, slope_away, down_x, down_y)
    downs = (down_own, down_y, down_x)
    part_away = hop(feed_down(scal, act_away, downs, BF), 1)
    part = feed_down(scal, act, downs, F32)
    part, part_away = tied(part, part_away)
    out_own, out_away, dh2, dz2, sums2 = second_norm(y1, part, part_away, cot_own, cot_came, vecs)
    dz2_away = hop(dz2, 1)
    dak, das, dbk, dbs = down_grad(scal, (act, act_away), (dz2, dz2_away))
    dak, das, dbk, dbs, mixed_came = tied(dak, das, dbk, dbs, hop(out_away, 4))
    mixed = jnp.where(
        top == 0, jnp.stack([out_own, mixed_came]), jnp.stack([mixed_came, out_own])
    )[:, None]
    da_came, db_came = hop(das, 2), hop(dbs, 4)
    du, du_away, part, part_away, up_sums = feed_back(
        scal, (dz2, after(dz2_away, dak)), (slope, slope_away), w_up, ups, downs
    )
    part, du, du_away, up_sums, part_away, da_came, db_came = tied(
        part, du, du_away, up_sums, part_away, da_came, db_came
    )
    part_away = hop(part_away, 1)
    y1s, dus = (y1_low, y1_away), (du, du_away)
    up_other = up_grad_other(scal, y1s, dus)
    up_other, part_away = tied(up_other, part_away)
    dao, *dattn, sums1 = first_norm(
        scal, dh2, part, part_away, n1, r1, vecs, w_out, near, away
    )
    dattn = [dattn[0]] + [hop(dattn[k], k) for k in (1, 2, 3)]
    up_came = hop(up_other, 1)

    def per_owner(vector):
        return vector.reshape(8, 4, 32)

    unit_sums = up_sums[:4].reshape(4, 4, 128).transpose(1, 0, 2)
    mine = (jnp.arange(2) == core)[None, :, None, None]
    up_owner = jnp.where(mine, unit_sums[:, None], 0.0).reshape(8, 4, 128)
    vec_block = jnp.concatenate(
        [per_owner(sums1[2]), per_owner(sums1[0]), per_owner(sums1[1]), per_owner(sums2[2]),
         per_owner(sums2[0]), per_owner(sums2[1]), up_owner, jnp.zeros((8, 4, 64), F32)], 2
    ).reshape(8, 4, 3, 128)
    vec_block = jnp.concatenate([vec_block, jnp.zeros((8, 4, 29, 128), F32)], 2).reshape(
        8, 128, 128
    )
    all_heads = jnp.stack(heads)
    out_other = out_grad_other(scal, all_heads, dao, vec_block)
    uak, uas, ubk, ubs = up_grad_own(
        scal, y1s, dus, all_heads, dao, vec_block, up_came, hop(out_other, 1)
    )
    uak, uas, ubk, ubs, *dattn = tied(uak, uas, ubk, ubs, *dattn)
    ua_came, ub_came = hop(uas, 2), hop(ubs, 4)
    da_came, db_came = tied(da_came, db_came, uak)[:2]
    da_next, db_next = add_far(dak, dbk, da_came, db_came)
    dqkv = attention_backward(scal, after(qkv, uak), dattn, turned, lse, chunk, 0, 4)
    da_next, db_next, ua_came, ub_came, dqkv = tied(da_next, db_next, ua_came, ub_came, dqkv)

    ua_sent, ub_sent = add_low(uak[1], ua_came[1]), add_low(ubk[1], ub_came[1])
    ua_next, ub_next = hop(ua_sent, 4), hop(ub_sent, 2)
    down_sum = sum_chips(dak, dbk, da_came, db_came, after(da_next, ua_sent, ub_sent), db_next)
    down_rows = sum_shards(down_sum)
    grad_send, grad_keep = qkv_grad(scal, x_all, dqkv)
    grad_send, grad_keep, ua_next, ub_next = tied(grad_send, grad_keep, ua_next, ub_next)
    grad_came = hop(grad_send, 4)
    up_sum = sum_chips(uak, ubk, ua_came, ub_came, ua_next, ub_next)
    up_rows = sum_shards(up_sum).astype(F32)
    dx_away = input_grad(scal, after(dqkv, grad_keep, up_sum), qkv_weight, dao, 4)
    dx = input_grad(scal, dqkv, qkv_weight, after(dao, dx_away), 0)
    dx_came, dx, grad_came = tied(hop(dx_away, 1), dx, grad_came)
    grad_parts = lax.all_to_all(
        add_low(grad_keep, grad_came), "fsdp", 0, 0, tiled=True
    )
    sent_rows = add_low(dx[2:], dx_came[2:])
    far_rows = hop(sent_rows[1], 2)
    kept_rows = add_low(dx[:2], after(dx_came, sent_rows)[:2])
    far_rows, kept_rows = tied(far_rows, kept_rows)
    own_rows = hop(after(sent_rows[0], far_rows), 2)
    home_rows = hop(add_low(kept_rows[1], far_rows), 4)
    grad_parts, own_rows, home_rows = tied(grad_parts, own_rows, home_rows)
    grad_own = add_low(kept_rows[0], own_rows)
    tokens_grad = jnp.where(
        top == 0, jnp.stack([grad_own, home_rows]), jnp.stack([home_rows, grad_own])
    )[:, None]
    mine = lax.all_to_all(
        jnp.sum(grad_parts.astype(F32), 0).astype(BF), "ctx", 0, 0, tiled=True,
        axis_index_groups=half_groups,
    ).astype(F32)
    w_qkv_grad = mine[:, :, :768].reshape(4, 32, 3, 256).transpose(1, 2, 0, 3).reshape(32, 3072)
    q_bias_grad = jnp.sum(mine[:, :, 768], 0)
    v_bias_grad = jnp.sum(mine[:, :, 769], 0)

    w_up_grad = (
        up_rows[:, :4096].reshape(32, 8, 4, 128).transpose(0, 2, 1, 3).reshape(32, 4096)
    )
    w_out_grad = up_rows[:, 4096:5120]
    sums = up_rows[:3, 5120:].reshape(384)
    return (
        mixed, tokens_grad, w_qkv_grad, w_out_grad, w_up_grad, down_rows.astype(F32), q_bias_grad, v_bias_grad,
        sums[0:32], sums[32:64], sums[64:96], sums[192:320], sums[96:128], sums[128:160],
        sums[160:192],
    )


def pick_blocks(wanted, rows):
    shaped = rows.reshape(-1, BLK, rows.shape[-1])
    picked = [
        lax.dynamic_index_in_dim(shaped, wanted[e], 0, False) for e in range(wanted.shape[0])
    ]
    return jnp.concatenate(picked, 0)


def plain_device(
    tokens, cotangent, lengths, order, w_qkv, w_out, w_up, w_down, q_bias, v_bias, out_bias,
    norm1_gain, norm1_bias, up_bias, down_bias, norm2_gain, norm2_bias,
):
    shards = (
        w_qkv, w_out, w_up, w_down, q_bias, v_bias, out_bias, norm1_gain, norm1_bias, up_bias,
        down_bias, norm2_gain, norm2_bias,
    )
    me = lax.axis_index("ctx")
    count = lax.axis_size("ctx")
    rows = tokens.shape[2]
    per_device = rows // BLK
    whole_rows = rows * count
    scaling = 1.0 / math.sqrt(HD)
    (
        qkv_full, out_full, up_full, down_full, qbias_full, vbias_full, obias_full, gain_one,
        shift_one, ubias_full, dbias_full, gain_two, shift_two,
    ) = tuple(lax.all_gather(shard, "fsdp", axis=0, tiled=True) for shard in shards)
    full_bias = jnp.concatenate([qbias_full, jnp.zeros_like(qbias_full), vbias_full]).astype(F32)
    gain_one, shift_one, gain_two, shift_two = (
        vector.astype(F32) for vector in (gain_one, shift_one, gain_two, shift_two)
    )
    positions = jnp.arange(whole_rows, dtype=jnp.int32)
    mixed_list, grad_list, totals = [], [], None
    for micro in range(tokens.shape[0]):
        order_row = order[micro, 0]
        bound = lengths[micro, 0, 0]
        segment_all = (positions >= bound).astype(jnp.int32)
        segment_query = (me * rows + jnp.arange(rows, dtype=jnp.int32) >= bound).astype(jnp.int32)
        dealt = me * per_device + jnp.arange(per_device, dtype=jnp.int32)
        blocks = jnp.arange(order_row.shape[0], dtype=jnp.int32)
        inverse = jnp.sum(jnp.where(order_row[None, :] == dealt[:, None], blocks[None, :], 0), 1)
        forward = jnp.sum(jnp.where(blocks[None, :] == dealt[:, None], order_row[None, :], 0), 1)
        token_rows = tokens[micro, 0]
        cot_rows = pick_blocks(
            inverse, lax.all_gather(cotangent[micro, 0], "ctx", axis=0, tiled=True)
        ).astype(F32)
        qkv_rows = (jnp.dot(token_rows, qkv_full, preferred_element_type=F32) + full_bias).astype(BF)
        queries = qkv_rows[:, :D].reshape(rows, H, HD)
        keys_values = lax.all_gather(qkv_rows[:, D:], "ctx", axis=0, tiled=True)
        keys = keys_values[:, :D].reshape(whole_rows, H, HD)
        values = keys_values[:, D:].reshape(whole_rows, H, HD)
        allowed = (segment_query[:, None] == segment_all[None, :])[None]
        scores = jnp.einsum("rhd,khd->hrk", queries, keys, preferred_element_type=F32) * scaling
        scores = jnp.where(allowed, scores, NEGATIVE)
        expos = jnp.where(allowed, jnp.exp(scores - jnp.max(scores, -1, keepdims=True)), 0.0)
        probs = expos / jnp.sum(expos, -1, keepdims=True)
        probs_low = probs.astype(BF)
        attn_float = jnp.einsum("hrk,khd->rhd", probs_low, values, preferred_element_type=F32)
        attn_low = attn_float.reshape(rows, D).astype(BF)
        first_in = (
            token_rows.astype(F32)
            + jnp.dot(attn_low, out_full, preferred_element_type=F32)
            + obias_full.astype(F32)
        )
        first_out, normed_one, inverse_one = norm_forward(first_in, gain_one, shift_one)
        first_low = first_out.astype(BF)
        hidden_in = jnp.dot(first_low, up_full, preferred_element_type=F32) + ubias_full.astype(F32)
        activated, gelu_back = jax.vjp(partial(jax.nn.gelu, approximate=False), hidden_in)
        act_low = activated.astype(BF)
        second_in = (
            first_out
            + jnp.dot(act_low, down_full, preferred_element_type=F32)
            + dbias_full.astype(F32)
        )
        second_out, normed_two, inverse_two = norm_forward(second_in, gain_two, shift_two)
        out_all = lax.all_gather(second_out.astype(BF), "ctx", axis=0, tiled=True)
        mixed_list.append(pick_blocks(forward, out_all))

        grad_second = norm_backward(cot_rows, normed_two, inverse_two, gain_two)
        grad_down_low = grad_second.astype(BF)
        (grad_hidden,) = gelu_back(contract(grad_down_low, down_full, 1, 1))
        grad_hidden_low = grad_hidden.astype(BF)
        grad_first = grad_second + contract(grad_hidden_low, up_full, 1, 1)
        grad_first_in = norm_backward(grad_first, normed_one, inverse_one, gain_one)
        grad_branch = grad_first_in.astype(BF)
        grad_attn = contract(grad_branch, out_full, 1, 1).astype(BF).reshape(rows, H, HD)
        grad_probs = jnp.einsum("rhd,khd->hrk", grad_attn, values, preferred_element_type=F32)
        delta = jnp.sum(probs * grad_probs, -1, keepdims=True)
        grad_scores = (probs * (grad_probs - delta) * scaling).astype(BF)
        grad_query = jnp.einsum("hrk,khd->rhd", grad_scores, keys, preferred_element_type=F32)
        grad_keys = jnp.einsum("hrk,rhd->khd", grad_scores, queries, preferred_element_type=F32)
        grad_values = jnp.einsum("hrk,rhd->khd", probs_low, grad_attn, preferred_element_type=F32)
        both = jnp.concatenate(
            [grad_keys.reshape(whole_rows, D), grad_values.reshape(whole_rows, D)], 1
        )
        both = lax.psum_scatter(both, "ctx", scatter_dimension=0, tiled=True)
        grad_qkv = jnp.concatenate([grad_query.reshape(rows, D), both], 1).astype(BF)
        column_sums = jnp.sum(grad_qkv.astype(F32), 0)
        grad_list.append((grad_first_in + contract(grad_qkv, qkv_full, 1, 1)).astype(BF))
        parts = (
            contract(token_rows, grad_qkv, 0, 0),
            contract(attn_low, grad_branch, 0, 0),
            contract(first_low, grad_hidden_low, 0, 0),
            contract(act_low, grad_down_low, 0, 0),
            column_sums[:D],
            column_sums[2 * D :],
            jnp.sum(grad_branch.astype(F32), 0),
            jnp.sum(grad_first * normed_one, 0),
            jnp.sum(grad_first, 0),
            jnp.sum(grad_hidden_low.astype(F32), 0),
            jnp.sum(grad_down_low.astype(F32), 0),
            jnp.sum(cot_rows * normed_two, 0),
            jnp.sum(cot_rows, 0),
        )
        totals = parts if totals is None else tuple(a + b for a, b in zip(totals, parts))
    shares = tuple(
        lax.psum_scatter(part, ("ctx", "fsdp"), scatter_dimension=0, tiled=True) for part in totals
    )
    return (jnp.stack(mixed_list)[:, None], jnp.stack(grad_list)[:, None]) + shares


def solution(mesh):
    fits = mesh.shape["ctx"] == 8 and mesh.shape["fsdp"] == 4
    weights = (P("fsdp", None),) * 4 + (P("fsdp"),) * 9
    owners = (P(("ctx", "fsdp"), None),) * 4 + (P(("ctx", "fsdp")),) * 9
    rows = P(None, "fsdp", "ctx", None)
    return jax.shard_map(
        tiled_device if fits else plain_device,
        mesh=mesh,
        in_specs=(rows, rows, P(None, "fsdp", None), P(None, "fsdp", None)) + weights,
        out_specs=(rows, rows) + owners,
        check_vma=False,
    )
```
